32 devices in a mesh: group: 4 (over y, core), member: 8 (over z, x).
Axes of the slice: x: 2, y: 2, z: 4, core: 2. Of those that a mesh axis runs over, the one named last changes fastest.
Arguments:
- tokens: bfloat16 [128, 196, 768], P(('group', 'member')), may hold values from -6 to 6
- w_query: bfloat16 [768, 768], replicated, may hold values from -8 to 8
- w_key: bfloat16 [768, 768], replicated, may hold values from -1 to 1
- w_value: bfloat16 [768, 768], replicated, may hold values from -0.21875 to 0.21875
- w_out: bfloat16 [768, 768], replicated, may hold values from -0.21875 to 0.21875
- partners: int32 [128, 4], P(('group', 'member')), may hold values from 0 to 127, as said below
- counts: int32 [128], P(('group', 'member')), may hold values from 1 to 4
- key_slot: int32 [32], P(('group', 'member')), may hold values from 0 to 3
Outputs:
- refined: bfloat16 [128, 196, 768], P(('group', 'member'))
The draws below stay inside these ranges and needn't reach their ends.
Inputs may be any that keep to these rules, and one draw needn't show every extreme that they name: `partners`: every entry names a view held by another device of the same group; the entries of all views of one device name views of one other device at most 3 times, and those of some other device exactly 3 times.
All inputs are finite; a program needn't handle non-finite values.
Results may differ from the reference program's by a relative error of at most 0.011.
Values may be sent and summed in bfloat16 or wider, within the bound.
A program may use at most 128 MiB of HBM per device.

```python
import jax
import jax.numpy as jnp
from jax import lax

D = 768
HEADS = 12
SEQ = 196
DEG = 4
VIEWS_DEV = 4
VIEWS = 128
N_GROUP = 4
N_MEMBER = 8


def draw_tokens(key, part):
    normal_draw = jax.random.normal(key, (VIEWS, SEQ, D), jnp.float32)
    return jnp.clip(normal_draw, -6.0, 6.0).astype(jnp.bfloat16)


def weight_pair(key):
    pair_key = jax.random.fold_in(key, 101)
    key_matrix = jax.random.normal(jax.random.fold_in(pair_key, 1), (D, D), jnp.float32) / jnp.sqrt(jnp.float32(D))
    query_matrix = jax.random.normal(jax.random.fold_in(pair_key, 2), (D, D), jnp.float32) / jnp.sqrt(jnp.float32(D))
    return (jnp.clip(query_matrix, -8.0, 8.0), jnp.clip(key_matrix, -1.0, 1.0))


def draw_w_query(key, part):
    return weight_pair(key)[0].astype(jnp.bfloat16)


def draw_w_key(key, part):
    return weight_pair(key)[1].astype(jnp.bfloat16)


def draw_partners(key, part):
    devices_all = N_GROUP * N_MEMBER
    entry_count = VIEWS_DEV * DEG
    rotation = jax.random.randint(jax.random.fold_in(key, 11), (devices_all, 1), 0, N_MEMBER - 1)
    slots = jax.random.randint(jax.random.fold_in(key, 12), (devices_all, entry_count), 0, VIEWS_DEV)
    device_ids = jnp.arange(devices_all, dtype=jnp.int32)[:, None]
    entry_ids = jnp.arange(entry_count, dtype=jnp.int32)[None, :]
    group_index = device_ids // N_MEMBER
    member_index = device_ids % N_MEMBER
    peers = (member_index + 1 + (entry_ids + rotation) % (N_MEMBER - 1)) % N_MEMBER
    views = (group_index * N_MEMBER + peers) * VIEWS_DEV + slots
    return views.reshape(VIEWS, DEG).astype(jnp.int32)


def with_ends(values, key, low, top_value):
    dims = values.shape
    place = [jax.random.randint(jax.random.fold_in(key, axis), (), 0, dims[axis]) for axis in range(len(dims))]
    values = values.at[tuple(place)].set(low)
    longest = dims.index(max(dims))
    place[longest] = (place[longest] + 1) % dims[longest]
    return values.at[tuple(place)].set(top_value)


def centred(own_key, extent, width, bound, kind=jnp.bfloat16):
    values = width * jax.random.normal(own_key, extent, jnp.float32)
    return jnp.clip(values, min=-bound, max=bound).astype(kind)


def setup_inputs(seed: int = 0) -> dict:
    seeds = jax.random.split(jax.random.key(seed), 9)
    tokens = draw_tokens(jax.random.fold_in(seeds[8], 71), 0)
    w_query = draw_w_query(jax.random.fold_in(seeds[8], 71), 0)
    w_key = draw_w_key(jax.random.fold_in(seeds[8], 71), 0)
    w_value = centred(seeds[3], (D, D), D ** -0.5, 0.21875)
    w_out = centred(seeds[4], (D, D), D ** -0.5, 0.21875)
    partners = draw_partners(jax.random.fold_in(seeds[8], 71), 0)
    counts = with_ends(jax.random.randint(seeds[6], (VIEWS,), 1, DEG + 1), jax.random.fold_in(seeds[6], 1), 1, DEG).astype(jnp.int32)
    key_slot = with_ends(jax.random.randint(seeds[7], (N_GROUP * N_MEMBER,), 0, VIEWS_DEV), jax.random.fold_in(seeds[7], 1), 0, VIEWS_DEV - 1).astype(jnp.int32)
    return {"tokens": tokens, "w_query": w_query, "w_key": w_key, "w_value": w_value, "w_out": w_out, "partners": partners, "counts": counts, "key_slot": key_slot}


def layer_norm(values_in):
    values_in = values_in.astype(jnp.float32)
    centre = lax.optimization_barrier(jnp.mean(values_in, axis=-1, keepdims=True))
    spread = lax.optimization_barrier(jnp.mean((values_in - centre) ** 2, axis=-1, keepdims=True))
    return (values_in - centre) * lax.rsqrt(spread + 1e-05)

def attend(view_query, key_block, value_block, head_count):
    length, features = view_query.shape
    head_size = features // head_count
    entries = key_block.shape[0]
    query_heads = view_query.astype(jnp.float32).reshape(length, head_count, head_size)
    key_heads = key_block.astype(jnp.float32).reshape(entries, length, head_count, head_size)
    value_heads = value_block.astype(jnp.float32).reshape(entries, length, head_count, head_size)
    scores = jnp.einsum('qhd,ekhd->ehqk', query_heads, key_heads) / jnp.sqrt(jnp.float32(head_size))
    probabilities = jax.nn.softmax(scores, axis=-1).astype(jnp.bfloat16)
    outputs = jnp.einsum('ehqk,ekhd->eqhd', probabilities.astype(jnp.float32), value_heads)
    return outputs.reshape(entries, length, features)

def reference(tokens, w_query, w_key, w_value, w_out, partners, counts, key_slot):
    views, length, features = tokens.shape
    normed = layer_norm(tokens).astype(jnp.bfloat16)
    flat_rows = normed.reshape(views * length, features)
    queries = jnp.dot(flat_rows, w_query, preferred_element_type=jnp.float32).astype(jnp.bfloat16).reshape(views, length, features)
    keys_all = jnp.dot(flat_rows, w_key, preferred_element_type=jnp.float32).astype(jnp.bfloat16).reshape(views, length, features)
    values_all = jnp.dot(flat_rows, w_value, preferred_element_type=jnp.float32).astype(jnp.bfloat16).reshape(views, length, features)

    def one_view(view_id):
        device = view_id // VIEWS_DEV
        group_index = device // N_MEMBER
        member_index = device % N_MEMBER
        keyframe = (view_id % VIEWS_DEV == key_slot[device]).astype(jnp.int32)
        below_dev = (group_index - 1) % N_GROUP * N_MEMBER + member_index
        above_dev = (group_index + 1) % N_GROUP * N_MEMBER + member_index
        below_key = below_dev * VIEWS_DEV + key_slot[below_dev]
        above_key = above_dev * VIEWS_DEV + key_slot[above_dev]
        partner_ids = jnp.concatenate([partners[view_id], jnp.stack([below_key, above_key]).astype(jnp.int32)]).astype(jnp.int32)
        outputs = attend(queries[view_id], keys_all[partner_ids], values_all[partner_ids], HEADS)
        divisor = (counts[view_id] + 2 * keyframe).astype(jnp.float32)
        live_weight = (jnp.arange(DEG, dtype=jnp.int32) < counts[view_id]).astype(jnp.float32)
        key_weight = jnp.full((2,), keyframe, jnp.int32).astype(jnp.float32)
        pair_weights = jnp.concatenate([live_weight, key_weight]) / divisor
        return lax.optimization_barrier(jnp.sum(pair_weights[:, None, None] * outputs, axis=0)).astype(jnp.bfloat16)
    mixed = lax.map(one_view, jnp.arange(views, dtype=jnp.int32))
    projected = jnp.dot(mixed.reshape(views * length, features), w_out, preferred_element_type=jnp.float32)
    refined = tokens.astype(jnp.float32) + projected.reshape(views, length, features)
    return refined.astype(jnp.bfloat16)
```

```python
import functools

import jax
import jax.numpy as jnp
from jax import lax
from jax.experimental import pallas as pl
from jax.experimental.pallas import tpu as pltpu
from jax.sharding import PartitionSpec as P

HEADS = 12
ROW = 2
LAYERS = 4
MESH = pl.DeviceIdType.MESH


def layer_norm(values_in):
    values_in = values_in.astype(jnp.float32)
    centre = jnp.mean(values_in, axis=-1, keepdims=True)
    spread = jnp.mean((values_in - centre) ** 2, axis=-1, keepdims=True)
    return (values_in - centre) * lax.rsqrt(spread + 1e-05)


def project(rows, weights):
    return jnp.dot(rows, weights, preferred_element_type=jnp.float32)


def attend(query, normed, w_key, w_value, pair, store):
    features = normed.shape[1]
    size = features // HEADS
    lower = lax.broadcasted_iota(jnp.int32, (1, 2 * size), 1) < size
    pair[:, :features] = project(normed, w_key[...]).astype(jnp.bfloat16)
    pair[:, features:] = project(normed, w_value[...]).astype(jnp.bfloat16)
    for h in range(HEADS // 2):
        cols = pl.ds(2 * h * size, 2 * size)
        rows = query(cols)
        key = pair[:, cols]
        value = pair[:, pl.ds(features + 2 * h * size, 2 * size)]
        halves = []
        for keep in (lower, jnp.logical_not(lower)):
            part = jnp.where(keep, rows, jnp.zeros_like(rows))
            scores = lax.dot_general(
                part, key, (((1,), (1,)), ((), ())), preferred_element_type=jnp.float32
            )
            top = jnp.max(scores, axis=-1, keepdims=True)
            weights = jnp.exp(scores - top)
            mass = jnp.sum(weights, axis=-1, keepdims=True)
            halves.append(project(weights.astype(jnp.bfloat16), value) / mass)
        store(cols, jnp.where(lower, halves[0], halves[1]))


def sublayer_kernel(degree, capacity, *refs):
    table, ask, weight, key_weight, tokens_in, wq_in, wk_in, wv_in, wo_in, out_ref = refs[:10]
    tokens, w_query, w_key, w_value, w_out = refs[10:15]
    own, queries, near, b0, b1, b2, s0, s1, s2, keys, staged, key_out = refs[15:27]
    asked, cur, pair, results, load_sem, send_sem, recv_sem = refs[27:]
    views, length, features = tokens.shape
    members, groups = lax.axis_size("member"), lax.axis_size("group")
    entries = views * degree
    peers = members - 1
    size = features // HEADS
    me, group = lax.axis_index("member"), lax.axis_index("group")
    layer, side = me // ROW, me % ROW
    low = layer < LAYERS // 2
    toward = jnp.where(low, ROW, -ROW)
    is_end = jnp.logical_or(layer == 0, layer == LAYERS - 1)
    is_mid = jnp.logical_not(is_end)
    beside = {"member": layer * ROW + 1 - side}
    inner = {"member": me + toward}
    outer = {"member": jnp.clip(me - toward, 0, members - 1)}
    above = {"group": lax.rem(group + 1, groups)}
    below = {"group": lax.rem(group + groups - 1, groups)}

    blocks = (near, b0, s0, b1, s1, b2, s2)
    base, total = {}, 0
    for name, ref in (("near", near), ("b0", b0), ("b1", b1), ("b2", b2), ("s0", s0),
                      ("s1", s1), ("s2", s2), ("keys", keys)):
        base[name] = total
        total += ref.shape[0]

    def remote(source, target, send, recv, device):
        return pltpu.make_async_remote_copy(
            src_ref=source, dst_ref=target, send_sem=send_sem.at[send],
            recv_sem=recv_sem.at[recv], device_id=device, device_id_type=MESH,
        )

    sends = {}

    def slot(name, index):
        return sends.setdefault((name, index), len(sends))

    def hop(name, source, v, target, target_name, device):
        return remote(source.at[v], target.at[v], slot(name, v), base[target_name] + v, device)

    def to_near(v):
        return hop("near", own, v, near, "near", beside)

    def own_to_b1(v):
        return hop("in", own, v, b1, "b1", inner)

    def own_to_b0(v):
        return hop("in", own, v, b0, "b0", inner)

    def own_out(v):
        return hop("out", own, v, b0, "b0", outer)

    def b1_in(v):
        return hop("in2", b1, v, b2, "b2", inner)

    def b0_out(v):
        return hop("out1", b0, v, b1, "b1", outer)

    def b2_out(v):
        return hop("out2", b2, v, b2, "b2", outer)

    swaps = (s0, s1, s2)

    def swap(j, k):
        return remote(
            staged.at[j * capacity + k], swaps[j].at[k], slot("swap", j * capacity + k),
            base[f"s{j}"] + k, beside,
        )

    def key_send(i):
        return remote(
            key_out, keys.at[i], slot("key", i), base["keys"] + i, above if i == 0 else below
        )

    def ask_send():
        return remote(ask, asked, slot("ask", 0), total, beside)

    loads = [
        pltpu.make_async_copy(source, target, load_sem.at[i])
        for i, (source, target) in enumerate(
            ((tokens_in, tokens), (wq_in, w_query), (wk_in, w_key), (wv_in, w_value), (wo_in, w_out))
        )
    ]
    for load in loads:
        load.start()

    barrier = pltpu.get_barrier_semaphore()
    for device in (beside, inner, above, below):
        pl.semaphore_signal(barrier, inc=1, device_id=device, device_id_type=MESH)

    @pl.when(is_mid)
    def _():
        pl.semaphore_signal(barrier, inc=1, device_id=outer, device_id_type=MESH)

    loads[0].wait()
    own[0] = layer_norm(tokens[0]).astype(jnp.bfloat16)

    @pl.when(is_mid)
    def _():
        pl.semaphore_wait(barrier, 5)

    @pl.when(is_end)
    def _():
        pl.semaphore_wait(barrier, 4)

    for v in range(views):
        if v:
            own[v] = layer_norm(tokens[v]).astype(jnp.bfloat16)
        to_near(v).start()

        @pl.when(is_end)
        def _():
            own_to_b1(v).start()

        @pl.when(is_mid)
        def _():
            own_to_b0(v).start()
            own_out(v).start()

    ask_send().start()
    key_out[...] = own[table[3, 0]]
    loads[1].wait()
    for v in range(views):
        queries[v] = project(own[v], w_query[...]).astype(jnp.bfloat16) * jnp.bfloat16(size**-0.5)
    for i in range(2):
        key_send(i).start()
    loads[2].wait()
    loads[3].wait()
    for i in range(2):
        key_send(i).wait_recv()

    def stage(j, k, source):
        choice = asked[0, j * capacity + k]
        value = source[0]
        for v in range(1, k + views - capacity + 1):
            value = jnp.where(choice == v, source[v], value)
        staged[j * capacity + k] = value
        swap(j, k).start()

    def events(t):
        def far(v):
            @pl.when(is_end)
            def _():
                b0_out(v).wait_recv()

            @pl.when(is_mid)
            def _():
                b1_in(v).wait_recv()
                b2_out(v).start()

        def last(v):
            @pl.when(is_end)
            def _():
                b2_out(v).wait_recv()

        def arrive(j):
            for k in range(capacity):
                swap(j, k).wait_recv()

        extra = views - capacity

        def spread(wait, j, source, v):
            wait(v)
            if v >= extra:
                stage(j, v - extra, source)

        if t == first[0]:
            for v in range(views):
                own_to_b0(v).wait_recv()

                @pl.when(is_mid)
                def _():
                    b0_out(v).start()
                    own_to_b1(v).wait_recv()
                    b1_in(v).start()

                if v >= extra:
                    stage(0, v - extra, b0)
            for v in range(views):
                to_near(v).wait_recv()
        if t == first[2]:
            for v in range(views - 2):
                spread(far, 1, b1, v)
            arrive(0)
        if t == first[2] + 1:
            spread(far, 1, b1, views - 2)
        if t == first[3]:
            spread(far, 1, b1, views - 1)
        if t == first[4]:
            for v in range(views - 2):
                spread(last, 2, b2, v)
            arrive(1)
        if t == first[4] + 1:
            spread(last, 2, b2, views - 2)
        if t == first[5]:
            spread(last, 2, b2, views - 1)
        if t == first[6]:
            arrive(2)

    first = [2 + max(0, entries - capacity * (peers - j)) for j in range(peers)]

    def entry(t, carry):
        for when in sorted({first[0], first[2], first[2] + 1, first[3], first[4], first[4] + 1,
                            first[5], first[6]}):
            @pl.when(t == when)
            def _():
                events(when)

        @pl.when(t < 2)
        def _():
            cur[...] = keys[jnp.minimum(t, 1)]

        block, place, view = table[0, t], table[1, t], table[2, t]
        for j, ref in enumerate(blocks):
            @pl.when(t >= first[j])
            def _():
                value = ref[jnp.minimum(place, ref.shape[0] - 1)]
                cur[...] = jnp.where(block == j, value, cur[...])

        def store(cols, value):
            results[t, :, cols] = value

        attend(lambda cols: queries[view, :, cols], cur[...], w_key, w_value, pair, store)
        return carry

    ask_send().wait_recv()
    lax.fori_loop(0, entries + 2, entry, 0)
    loads[4].wait()
    for v in range(views):
        mixed = key_weight[v] * (results[0] + results[1])
        for e in range(degree):
            mixed += weight[v * degree + e] * results[table[4, v * degree + e]]
        out_ref[v] = (
            tokens[v].astype(jnp.float32) + project(mixed.astype(jnp.bfloat16), w_out[...])
        ).astype(out_ref.dtype)

    for v in range(views):
        to_near(v).wait_send()

        @pl.when(is_end)
        def _():
            own_to_b1(v).wait_send()

        @pl.when(is_mid)
        def _():
            own_to_b0(v).wait_send()
            own_out(v).wait_send()
            b1_in(v).wait_send()
            b0_out(v).wait_send()
            b2_out(v).wait_send()

    for j in range(3):
        for k in range(capacity):
            swap(j, k).wait_send()
    for i in range(2):
        key_send(i).wait_send()
    ask_send().wait_send()


def one_kernel(tokens, w_query, w_key, w_value, w_out, partners, counts, slot_key):
    views, length, features = tokens.shape
    members = lax.axis_size("member")
    me = lax.axis_index("member")
    degree = partners.shape[1]
    entry_list = partners.reshape(-1)
    entries = entry_list.shape[0]
    capacity = (entries + members - 2) // (members - 1)
    peers = entry_list // views % members
    places = entry_list % views
    layer, side = me // ROW, me % ROW
    ranking = jnp.array([[9, 0, 1, 2], [1, 9, 0, 2], [2, 0, 9, 1], [2, 1, 0, 9]], jnp.int32)[layer]
    layers = jnp.arange(LAYERS, dtype=jnp.int32)
    peer_layer = peers // ROW
    turn = jnp.sum(jnp.where(peer_layer[:, None] == layers[None, :], ranking[None, :], 0), axis=1)
    across = peers % ROW != side
    block = jnp.where(peer_layer == layer, 0, 1 + 2 * turn + across.astype(jnp.int32))
    order = jnp.arange(entries, dtype=jnp.int32)
    code = block * entries + order
    position = jnp.sum((code[None, :] < code[:, None]).astype(jnp.int32), axis=1)
    spots = jnp.arange(views, dtype=jnp.int32)
    turns = jnp.arange(LAYERS - 1, dtype=jnp.int32)
    wanted = jnp.any(
        (block[None, None, :] == 2 + 2 * turns[:, None, None])
        & (places[None, None, :] == spots[None, :, None]),
        axis=2,
    ).astype(jnp.int32)
    before = jnp.sum(
        jnp.where(spots[None, None, :] < spots[None, :, None], wanted[:, None, :], 0), axis=2
    )
    slots = capacity - jnp.sum(wanted, axis=1, keepdims=True) + before
    slot_ids = jnp.arange(capacity, dtype=jnp.int32)
    ask = jnp.sum(
        jnp.where(
            (wanted[:, None, :] == 1) & (slots[:, None, :] == slot_ids[None, :, None]),
            spots[None, None, :],
            0,
        ),
        axis=2,
    ).reshape(1, -1)
    picked = jnp.sum(
        jnp.where(
            (block[:, None, None] == 2 + 2 * turns[None, :, None])
            & (places[:, None, None] == spots[None, None, :]),
            slots[None, :, :],
            0,
        ),
        axis=(1, 2),
    )
    spot = jnp.where((block > 0) & across, picked, places)
    here = position[None, :] == order[:, None]
    data = jnp.stack((block, spot, order // degree))
    data = jnp.sum(jnp.where(here[None], data[:, None, :], 0), axis=2)
    lead = jnp.stack((jnp.full((2,), -1, jnp.int32), jnp.zeros((2,), jnp.int32), jnp.full((2,), slot_key)))
    data = jnp.concatenate((lead, data), axis=1)
    tail = jnp.stack(
        (jnp.full((entries + 2,), slot_key), jnp.concatenate((position + 2, jnp.zeros((2,), jnp.int32))))
    )
    table = jnp.concatenate((data, tail), axis=0)
    is_key = (spots == slot_key).astype(jnp.int32)
    inverse = 1.0 / (counts + 2 * is_key).astype(jnp.float32)
    live = (jnp.arange(degree, dtype=jnp.int32)[None, :] < counts[:, None]).astype(jnp.float32)
    weight = (live * inverse[:, None]).reshape(-1)
    key_weight = is_key.astype(jnp.float32) * inverse

    smem = pl.BlockSpec(memory_space=pltpu.SMEM)
    hbm = pl.BlockSpec(memory_space=pl.ANY)
    slab = (length, features)
    weights_shape = pltpu.VMEM((features, features), jnp.bfloat16)
    half = jnp.bfloat16
    blocks = [pltpu.VMEM((views, *slab), half)] * 6 + [pltpu.VMEM((capacity, *slab), half)] * 3
    sends = 6 * views + 3 * capacity + 3 + views
    receives = 4 * views + 3 * capacity + 3
    return pl.pallas_call(
        functools.partial(sublayer_kernel, degree, capacity),
        out_shape=jax.ShapeDtypeStruct(tokens.shape, tokens.dtype),
        in_specs=[smem] * 4 + [hbm] * 5,
        out_specs=pl.BlockSpec(memory_space=pltpu.VMEM),
        scratch_shapes=[
            pltpu.VMEM(tokens.shape, tokens.dtype),
            weights_shape,
            weights_shape,
            weights_shape,
            weights_shape,
            *blocks,
            pltpu.VMEM((2, *slab), half),
            pltpu.VMEM((3 * capacity, *slab), half),
            pltpu.VMEM(slab, half),
            pltpu.SMEM(ask.shape, jnp.int32),
            pltpu.VMEM(slab, half),
            pltpu.VMEM((length, 2 * features), half),
            pltpu.VMEM((entries + 2, *slab), jnp.float32),
            pltpu.SemaphoreType.DMA((5,)),
            pltpu.SemaphoreType.DMA((sends,)),
            pltpu.SemaphoreType.DMA((receives,)),
        ],
        compiler_params=pltpu.CompilerParams(
            collective_id=0, has_side_effects=True, vmem_limit_bytes=60 * 1024 * 1024
        ),
        name="sublayer",
    )(table, ask, weight, key_weight, tokens, w_query, w_key, w_value, w_out)


def local_kernel(table, queries, w_key, w_value, block, inverse, tokens, w_out, out_ref, *scratch):
    held, pair, total, sem = scratch
    copy = pltpu.make_async_copy(block, held, sem)
    copy.start()
    total[...] = jnp.zeros_like(total)
    copy.wait()
    views, length, _ = total.shape

    def entry(e, carry):
        @pl.when(table[0, e] == 1)
        def _():
            place, view = table[1, e], table[2, e]

            def store(cols, value):
                total[view, :, cols] += value

            normed = layer_norm(held[place]).astype(jnp.bfloat16)
            attend(lambda cols: queries[view, :, cols], normed, w_key, w_value, pair, store)

        return carry

    lax.fori_loop(0, table.shape[1], entry, 0)
    for v in range(views):
        mixed = (total[v] * inverse[v]).astype(jnp.bfloat16)
        out_ref[v] = (tokens[v].astype(jnp.float32) + project(mixed, w_out[...])).astype(out_ref.dtype)


def exchange(tokens, w_query, w_key, w_value, w_out, partners, counts, slot_key):
    views, length, features = tokens.shape
    members, groups = lax.axis_size("member"), lax.axis_size("group")
    degree = partners.shape[1]
    entry_list = partners.reshape(-1)
    entries = entry_list.shape[0]
    capacity = (entries + members - 2) // (members - 1)
    peers = entry_list // views % members
    places = entry_list % views
    order = jnp.arange(entries, dtype=jnp.int32)
    earlier = (peers[:, None] == peers[None, :]) & (order[None, :] < order[:, None])
    cells = peers * capacity + jnp.sum(earlier.astype(jnp.int32), axis=1)
    requests = jnp.zeros((members * capacity,), jnp.int32).at[cells].set(places)
    asked = lax.all_to_all(
        requests.reshape(members, capacity), "member", split_axis=0, concat_axis=0, tiled=True
    )
    outgoing = tokens[asked.reshape(-1)].reshape(members, capacity, length, features)
    arrived = lax.all_to_all(outgoing, "member", split_axis=0, concat_axis=0, tiled=True)
    own_key = lax.dynamic_slice_in_dim(tokens, slot_key, 1, 0)
    below = lax.ppermute(own_key, "group", [(g, (g + 1) % groups) for g in range(groups)])
    above = lax.ppermute(own_key, "group", [((g + 1) % groups, g) for g in range(groups)])
    block = jnp.concatenate((arrived.reshape(members * capacity, length, features), below, above))
    normed = layer_norm(tokens).astype(jnp.bfloat16)
    queries = project(normed.reshape(views * length, features), w_query).astype(jnp.bfloat16)
    queries = queries.reshape(tokens.shape) * jnp.bfloat16((features // HEADS) ** -0.5)
    is_key = (jnp.arange(views, dtype=jnp.int32) == slot_key).astype(jnp.int32)
    inverse = 1.0 / (counts + 2 * is_key).astype(jnp.float32)
    live = (jnp.arange(degree, dtype=jnp.int32)[None, :] < counts[:, None]).reshape(-1)
    two = jnp.arange(2, dtype=jnp.int32)
    table = jnp.stack(
        (
            jnp.concatenate((live.astype(jnp.int32), jnp.ones_like(two))),
            jnp.concatenate((cells, members * capacity + two)),
            jnp.concatenate((order // degree, jnp.full_like(two, slot_key))),
        )
    )
    vmem = pl.BlockSpec(memory_space=pltpu.VMEM)
    smem = pl.BlockSpec(memory_space=pltpu.SMEM)
    hbm = pl.BlockSpec(memory_space=pl.ANY)
    return pl.pallas_call(
        local_kernel,
        out_shape=jax.ShapeDtypeStruct(tokens.shape, tokens.dtype),
        in_specs=[smem, vmem, vmem, vmem, hbm, smem, vmem, vmem],
        out_specs=vmem,
        scratch_shapes=[
            pltpu.VMEM(block.shape, block.dtype),
            pltpu.VMEM((length, 2 * features), jnp.bfloat16),
            pltpu.VMEM(tokens.shape, jnp.float32),
            pltpu.SemaphoreType.DMA,
        ],
        compiler_params=pltpu.CompilerParams(vmem_limit_bytes=60 * 1024 * 1024),
        name="attend_all",
    )(table, queries, w_key, w_value, block, inverse, tokens, w_out)


def sublayer(tokens, w_query, w_key, w_value, w_out, partners, counts, key_slot):
    views = tokens.shape[0]
    members = lax.axis_size("member")
    entries = partners.shape[0] * partners.shape[1]
    capacity = (entries + members - 2) // (members - 1)
    grid = members == LAYERS * ROW and views == capacity + 1
    run = one_kernel if grid else exchange
    return run(tokens, w_query, w_key, w_value, w_out, partners, counts, key_slot[0])


def solution(mesh):
    return jax.shard_map(
        sublayer,
        mesh=mesh,
        in_specs=(
            P(("group", "member"), None, None),
            P(),
            P(),
            P(),
            P(),
            P(("group", "member"), None),
            P(("group", "member")),
            P(("group", "member")),
        ),
        out_specs=P(("group", "member"), None, None),
        check_vma=False,
    )
```

```python
import functools

import jax
import jax.numpy as jnp
from jax import lax
from jax.experimental import pallas as pl
from jax.experimental.pallas import tpu as pltpu
from jax.sharding import PartitionSpec as P

HEADS = 12
ROW = 2
LAYERS = 4
MESH = pl.DeviceIdType.MESH


def layer_norm(values_in):
    values_in = values_in.astype(jnp.float32)
    centre = jnp.mean(values_in, axis=-1, keepdims=True)
    spread = jnp.mean((values_in - centre) ** 2, axis=-1, keepdims=True)
    return (values_in - centre) * lax.rsqrt(spread + 1e-05)


def project(rows, weights):
    return jnp.dot(rows, weights, preferred_element_type=jnp.float32)


def attend(query, normed, w_key, w_value, pair, store):
    features = normed.shape[1]
    size = features // HEADS
    lower = lax.broadcasted_iota(jnp.int32, (1, 2 * size), 1) < size
    pair[:, :features] = project(normed, w_key[...]).astype(jnp.bfloat16)
    pair[:, features:] = project(normed, w_value[...]).astype(jnp.bfloat16)
    for h in range(HEADS // 2):
        cols = pl.ds(2 * h * size, 2 * size)
        rows = query(cols)
        key = pair[:, cols]
        value = pair[:, pl.ds(features + 2 * h * size, 2 * size)]
        halves = []
        for keep in (lower, jnp.logical_not(lower)):
            part = jnp.where(keep, rows, jnp.zeros_like(rows))
            scores = lax.dot_general(
                part, key, (((1,), (1,)), ((), ())), preferred_element_type=jnp.float32
            )
            top = jnp.max(scores, axis=-1, keepdims=True)
            weights = jnp.exp(scores - top)
            mass = jnp.sum(weights, axis=-1, keepdims=True)
            halves.append(project(weights.astype(jnp.bfloat16), value) / mass)
        store(cols, jnp.where(lower, halves[0], halves[1]))


RAW_BLOCK, RAW_PLACE, POSITION, BLOCK, PLACE, VIEW = range(6)


def build_tables(layer, side, degree, capacity, views, members, partners, key_view, ask, table):
    entries = views * degree
    low = layer < LAYERS // 2

    def mirror(value):
        return jnp.where(low, value, LAYERS - 1 - value)

    here = mirror(layer)

    def read(e, flags):
        partner = partners[lax.div(e, degree), lax.rem(e, degree)]
        peer = lax.rem(lax.div(partner, views), members)
        place = lax.rem(partner, views)
        there = mirror(lax.div(peer, ROW))
        inside = jnp.where(there == 0, 1, jnp.where(there == 2, 0, 2))
        turn = jnp.where(here == 0, there - 1, inside)
        across = (lax.rem(peer, ROW) != side).astype(jnp.int32)
        block = jnp.where(there == here, 0, 1 + 2 * turn + across)
        table[RAW_BLOCK, e] = block
        table[RAW_PLACE, e] = place
        return tuple(
            jnp.where((block == 2 + 2 * (i // views)) & (place == i % views), 1, flag)
            for i, flag in enumerate(flags)
        )

    flags = lax.fori_loop(0, entries, read, (jnp.int32(0),) * (3 * views))
    slots = []
    for j in range(3):
        wanted = flags[j * views : (j + 1) * views]
        slot = capacity - sum(wanted)
        for v in range(views):
            slots.append(slot)
            slot = slot + wanted[v]
        for k in range(capacity):
            ask[0, j * capacity + k] = sum(
                jnp.where((wanted[v] == 1) & (slots[j * views + v] == k), v, 0) for v in range(views)
            )

    def rank(e, carry):
        block, place = table[RAW_BLOCK, e], table[RAW_PLACE, e]
        position = jnp.int32(2)
        for other in range(entries):
            ahead = (table[RAW_BLOCK, other] * entries + other) < block * entries + e
            position = position + ahead.astype(jnp.int32)
        table[POSITION, e] = position
        spot = place
        for i, slot in enumerate(slots):
            spot = jnp.where((block == 2 + 2 * (i // views)) & (place == i % views), slot, spot)
        table[RAW_PLACE, e] = spot
        return carry

    lax.fori_loop(0, entries, rank, 0)

    def sort(r, carry):
        block, place, view = jnp.int32(-1), jnp.int32(0), key_view
        for e in range(entries):
            match = table[POSITION, e] == r
            block = jnp.where(match, table[RAW_BLOCK, e], block)
            place = jnp.where(match, table[RAW_PLACE, e], place)
            view = jnp.where(match, e // degree, view)
        table[BLOCK, r], table[PLACE, r], table[VIEW, r] = block, place, view
        return carry

    lax.fori_loop(0, entries + 2, sort, 0)


def sublayer_kernel(degree, capacity, *refs):
    partners, counts, key_slot, tokens, wq_in, wk_in, wv_in, wo_in, out_ref = refs[:9]
    w_query, w_key, w_value, w_out = refs[9:13]
    own, queries, near, b0, b1, b2, s0, s1, s2, keys, staged, key_out = refs[13:25]
    ask, asked, table, cur, pair, results, load_sem, send_sem, recv_sem = refs[25:]
    views, length, features = tokens.shape
    members, groups = lax.axis_size("member"), lax.axis_size("group")
    entries = views * degree
    peers = members - 1
    size = features // HEADS
    me, group = lax.axis_index("member"), lax.axis_index("group")
    layer, side = me // ROW, me % ROW
    low = layer < LAYERS // 2
    toward = jnp.where(low, ROW, -ROW)
    is_end = jnp.logical_or(layer == 0, layer == LAYERS - 1)
    is_mid = jnp.logical_not(is_end)
    beside = {"member": layer * ROW + 1 - side}
    inner = {"member": me + toward}
    outer = {"member": jnp.clip(me - toward, 0, members - 1)}
    above = {"group": lax.rem(group + 1, groups)}
    below = {"group": lax.rem(group + groups - 1, groups)}

    blocks = (near, b0, s0, b1, s1, b2, s2)
    base, total = {}, 0
    for name, ref in (("near", near), ("b0", b0), ("b1", b1), ("b2", b2), ("s0", s0),
                      ("s1", s1), ("s2", s2), ("keys", keys)):
        base[name] = total
        total += ref.shape[0]

    def remote(source, target, send, recv, device):
        return pltpu.make_async_remote_copy(
            src_ref=source, dst_ref=target, send_sem=send_sem.at[send],
            recv_sem=recv_sem.at[recv], device_id=device, device_id_type=MESH,
        )

    sends = {}

    def slot(name, index):
        return sends.setdefault((name, index), len(sends))

    def hop(name, source, v, target, target_name, device):
        return remote(source.at[v], target.at[v], slot(name, v), base[target_name] + v, device)

    def to_near(v):
        return hop("near", own, v, near, "near", beside)

    def own_to_b1(v):
        return hop("in", own, v, b1, "b1", inner)

    def own_to_b0(v):
        return hop("in", own, v, b0, "b0", inner)

    def own_out(v):
        return hop("out", own, v, b0, "b0", outer)

    def b1_in(v):
        return hop("in2", b1, v, b2, "b2", inner)

    def b0_out(v):
        return hop("out1", b0, v, b1, "b1", outer)

    def b2_out(v):
        return hop("out2", b2, v, b2, "b2", outer)

    swaps = (s0, s1, s2)

    def swap(j, k):
        return remote(
            staged.at[j * capacity + k], swaps[j].at[k], slot("swap", j * capacity + k),
            base[f"s{j}"] + k, beside,
        )

    def key_send(i):
        return remote(
            key_out, keys.at[i], slot("key", i), base["keys"] + i, above if i == 0 else below
        )

    def ask_send():
        return remote(ask, asked, slot("ask", 0), total, beside)

    loads = [
        pltpu.make_async_copy(source, target, load_sem.at[i])
        for i, (source, target) in enumerate(
            ((wq_in, w_query), (wk_in, w_key), (wv_in, w_value), (wo_in, w_out))
        )
    ]
    for load in loads:
        load.start()

    barrier = pltpu.get_barrier_semaphore()
    for device in (beside, inner, above, below):
        pl.semaphore_signal(barrier, inc=1, device_id=device, device_id_type=MESH)

    @pl.when(is_mid)
    def _():
        pl.semaphore_signal(barrier, inc=1, device_id=outer, device_id_type=MESH)

    own[0] = layer_norm(tokens[0]).astype(jnp.bfloat16)

    @pl.when(is_mid)
    def _():
        pl.semaphore_wait(barrier, 5)

    @pl.when(is_end)
    def _():
        pl.semaphore_wait(barrier, 4)

    for v in range(views):
        if v:
            own[v] = layer_norm(tokens[v]).astype(jnp.bfloat16)
        to_near(v).start()

        @pl.when(is_end)
        def _():
            own_to_b1(v).start()

        @pl.when(is_mid)
        def _():
            own_to_b0(v).start()
            own_out(v).start()

    key_view = key_slot[0]
    key_out[...] = own[key_view]
    loads[0].wait()
    for v in range(views):
        queries[v] = project(own[v], w_query[...]).astype(jnp.bfloat16) * jnp.bfloat16(size**-0.5)
    for i in range(2):
        key_send(i).start()
    build_tables(layer, side, degree, capacity, views, members, partners, key_view, ask, table)
    ask_send().start()
    loads[1].wait()
    loads[2].wait()
    for i in range(2):
        key_send(i).wait_recv()

    def stage(j, k, source):
        choice = asked[0, j * capacity + k]
        value = source[0]
        for v in range(1, k + views - capacity + 1):
            value = jnp.where(choice == v, source[v], value)
        staged[j * capacity + k] = value
        swap(j, k).start()

    def events(t):
        def far(v):
            @pl.when(is_end)
            def _():
                b0_out(v).wait_recv()

            @pl.when(is_mid)
            def _():
                b1_in(v).wait_recv()
                b2_out(v).start()

        def last(v):
            @pl.when(is_end)
            def _():
                b2_out(v).wait_recv()

        def arrive(j):
            for k in range(capacity):
                swap(j, k).wait_recv()

        extra = views - capacity

        def spread(wait, j, source, v):
            wait(v)
            if v >= extra:
                stage(j, v - extra, source)

        if t == first[0]:
            for v in range(views):
                own_to_b0(v).wait_recv()

                @pl.when(is_mid)
                def _():
                    b0_out(v).start()
                    own_to_b1(v).wait_recv()
                    b1_in(v).start()

                if v >= extra:
                    stage(0, v - extra, b0)
            for v in range(views):
                to_near(v).wait_recv()
        if t == first[2]:
            for v in range(views - 2):
                spread(far, 1, b1, v)
            arrive(0)
        if t == first[2] + 1:
            spread(far, 1, b1, views - 2)
        if t == first[3]:
            spread(far, 1, b1, views - 1)
        if t == first[4]:
            for v in range(views - 2):
                spread(last, 2, b2, v)
            arrive(1)
        if t == first[4] + 1:
            spread(last, 2, b2, views - 2)
        if t == first[5]:
            spread(last, 2, b2, views - 1)
        if t == first[6]:
            arrive(2)

    first = [2 + max(0, entries - capacity * (peers - j)) for j in range(peers)]

    def entry(t, carry):
        for when in sorted({first[0], first[2], first[2] + 1, first[3], first[4], first[4] + 1,
                            first[5], first[6]}):
            @pl.when(t == when)
            def _():
                events(when)

        @pl.when(t < 2)
        def _():
            cur[...] = keys[jnp.minimum(t, 1)]

        block, place, view = table[BLOCK, t], table[PLACE, t], table[VIEW, t]
        for j, ref in enumerate(blocks):
            @pl.when(t >= first[j])
            def _():
                value = ref[jnp.minimum(place, ref.shape[0] - 1)]
                cur[...] = jnp.where(block == j, value, cur[...])

        def store(cols, value):
            results[t, :, cols] = value

        attend(lambda cols: queries[view, :, cols], cur[...], w_key, w_value, pair, store)
        return carry

    ask_send().wait_recv()
    lax.fori_loop(0, entries + 2, entry, 0)
    loads[3].wait()
    for v in range(views):
        is_key = (key_view == v).astype(jnp.int32)
        count = counts[v]
        mixed = is_key.astype(jnp.float32) * (results[0] + results[1])
        for e in range(degree):
            live = (count > e).astype(jnp.int32).astype(jnp.float32)
            mixed += live * results[table[POSITION, v * degree + e]]
        divisor = jnp.full((1, features), count + 2 * is_key, jnp.int32).astype(jnp.float32)
        mixed = mixed * (1.0 / divisor)
        out_ref[v] = (
            tokens[v].astype(jnp.float32) + project(mixed.astype(jnp.bfloat16), w_out[...])
        ).astype(out_ref.dtype)

    for v in range(views):
        to_near(v).wait_send()

        @pl.when(is_end)
        def _():
            own_to_b1(v).wait_send()

        @pl.when(is_mid)
        def _():
            own_to_b0(v).wait_send()
            own_out(v).wait_send()
            b1_in(v).wait_send()
            b0_out(v).wait_send()
            b2_out(v).wait_send()

    for j in range(3):
        for k in range(capacity):
            swap(j, k).wait_send()
    for i in range(2):
        key_send(i).wait_send()
    ask_send().wait_send()


def one_kernel(tokens, w_query, w_key, w_value, w_out, partners, counts, key_slot):
    views, length, features = tokens.shape
    members = lax.axis_size("member")
    degree = partners.shape[1]
    entries = views * degree
    capacity = (entries + members - 2) // (members - 1)
    smem = pl.BlockSpec(memory_space=pltpu.SMEM)
    hbm = pl.BlockSpec(memory_space=pltpu.HBM)
    vmem = pl.BlockSpec(memory_space=pltpu.VMEM)
    slab = (length, features)
    weights_shape = pltpu.VMEM((features, features), jnp.bfloat16)
    half = jnp.bfloat16
    blocks = [pltpu.VMEM((views, *slab), half)] * 6 + [pltpu.VMEM((capacity, *slab), half)] * 3
    sends = 6 * views + 3 * capacity + 3 + views
    receives = 4 * views + 3 * capacity + 3
    return pl.pallas_call(
        functools.partial(sublayer_kernel, degree, capacity),
        out_shape=jax.ShapeDtypeStruct(tokens.shape, tokens.dtype),
        in_specs=[smem] * 3 + [vmem] + [hbm] * 4,
        out_specs=vmem,
        scratch_shapes=[
            weights_shape,
            weights_shape,
            weights_shape,
            weights_shape,
            *blocks,
            pltpu.VMEM((2, *slab), half),
            pltpu.VMEM((3 * capacity, *slab), half),
            pltpu.VMEM(slab, half),
            pltpu.SMEM((1, 3 * capacity), jnp.int32),
            pltpu.SMEM((1, 3 * capacity), jnp.int32),
            pltpu.SMEM((6, entries + 2), jnp.int32),
            pltpu.VMEM(slab, half),
            pltpu.VMEM((length, 2 * features), half),
            pltpu.VMEM((entries + 2, *slab), jnp.float32),
            pltpu.SemaphoreType.DMA((4,)),
            pltpu.SemaphoreType.DMA((sends,)),
            pltpu.SemaphoreType.DMA((receives,)),
        ],
        compiler_params=pltpu.CompilerParams(
            collective_id=0, has_side_effects=True, vmem_limit_bytes=44 * 1024 * 1024
        ),
        name="sublayer",
    )(partners, counts, key_slot, tokens, w_query, w_key, w_value, w_out)


def local_kernel(table, queries, w_key, w_value, block, inverse, tokens, w_out, out_ref, *scratch):
    held, pair, total, sem = scratch
    copy = pltpu.make_async_copy(block, held, sem)
    copy.start()
    total[...] = jnp.zeros_like(total)
    copy.wait()
    views, length, _ = total.shape

    def entry(e, carry):
        @pl.when(table[0, e] == 1)
        def _():
            place, view = table[1, e], table[2, e]

            def store(cols, value):
                total[view, :, cols] += value

            normed = layer_norm(held[place]).astype(jnp.bfloat16)
            attend(lambda cols: queries[view, :, cols], normed, w_key, w_value, pair, store)

        return carry

    lax.fori_loop(0, table.shape[1], entry, 0)
    for v in range(views):
        mixed = (total[v] * inverse[v]).astype(jnp.bfloat16)
        out_ref[v] = (tokens[v].astype(jnp.float32) + project(mixed, w_out[...])).astype(out_ref.dtype)


def exchange(tokens, w_query, w_key, w_value, w_out, partners, counts, key_slot):
    slot_key = key_slot[0]
    views, length, features = tokens.shape
    members, groups = lax.axis_size("member"), lax.axis_size("group")
    degree = partners.shape[1]
    entry_list = partners.reshape(-1)
    entries = entry_list.shape[0]
    capacity = (entries + members - 2) // (members - 1)
    peers = entry_list // views % members
    places = entry_list % views
    order = jnp.arange(entries, dtype=jnp.int32)
    earlier = (peers[:, None] == peers[None, :]) & (order[None, :] < order[:, None])
    cells = peers * capacity + jnp.sum(earlier.astype(jnp.int32), axis=1)
    requests = jnp.zeros((members * capacity,), jnp.int32).at[cells].set(places)
    asked = lax.all_to_all(
        requests.reshape(members, capacity), "member", split_axis=0, concat_axis=0, tiled=True
    )
    outgoing = tokens[asked.reshape(-1)].reshape(members, capacity, length, features)
    arrived = lax.all_to_all(outgoing, "member", split_axis=0, concat_axis=0, tiled=True)
    own_key = lax.dynamic_slice_in_dim(tokens, slot_key, 1, 0)
    below = lax.ppermute(own_key, "group", [(g, (g + 1) % groups) for g in range(groups)])
    above = lax.ppermute(own_key, "group", [((g + 1) % groups, g) for g in range(groups)])
    block = jnp.concatenate((arrived.reshape(members * capacity, length, features), below, above))
    normed = layer_norm(tokens).astype(jnp.bfloat16)
    queries = project(normed.reshape(views * length, features), w_query).astype(jnp.bfloat16)
    queries = queries.reshape(tokens.shape) * jnp.bfloat16((features // HEADS) ** -0.5)
    is_key = (jnp.arange(views, dtype=jnp.int32) == slot_key).astype(jnp.int32)
    inverse = 1.0 / (counts + 2 * is_key).astype(jnp.float32)
    live = (jnp.arange(degree, dtype=jnp.int32)[None, :] < counts[:, None]).reshape(-1)
    two = jnp.arange(2, dtype=jnp.int32)
    table = jnp.stack(
        (
            jnp.concatenate((live.astype(jnp.int32), jnp.ones_like(two))),
            jnp.concatenate((cells, members * capacity + two)),
            jnp.concatenate((order // degree, jnp.full_like(two, slot_key))),
        )
    )
    vmem = pl.BlockSpec(memory_space=pltpu.VMEM)
    smem = pl.BlockSpec(memory_space=pltpu.SMEM)
    hbm = pl.BlockSpec(memory_space=pl.ANY)
    return pl.pallas_call(
        local_kernel,
        out_shape=jax.ShapeDtypeStruct(tokens.shape, tokens.dtype),
        in_specs=[smem, vmem, vmem, vmem, hbm, smem, vmem, vmem],
        out_specs=vmem,
        scratch_shapes=[
            pltpu.VMEM(block.shape, block.dtype),
            pltpu.VMEM((length, 2 * features), jnp.bfloat16),
            pltpu.VMEM(tokens.shape, jnp.float32),
            pltpu.SemaphoreType.DMA,
        ],
        compiler_params=pltpu.CompilerParams(vmem_limit_bytes=60 * 1024 * 1024),
        name="attend_all",
    )(table, queries, w_key, w_value, block, inverse, tokens, w_out)


def sublayer(tokens, w_query, w_key, w_value, w_out, partners, counts, key_slot):
    views = tokens.shape[0]
    members = lax.axis_size("member")
    entries = partners.shape[0] * partners.shape[1]
    capacity = (entries + members - 2) // (members - 1)
    grid = members == LAYERS * ROW and views == capacity + 1
    run = one_kernel if grid else exchange
    return run(tokens, w_query, w_key, w_value, w_out, partners, counts, key_slot)


def solution(mesh):
    return jax.shard_map(
        sublayer,
        mesh=mesh,
        in_specs=(
            P(("group", "member"), None, None),
            P(),
            P(),
            P(),
            P(),
            P(("group", "member"), None),
            P(("group", "member")),
            P(("group", "member")),
        ),
        out_specs=P(("group", "member"), None, None),
        check_vma=False,
    )
```

```python
import functools

import jax
import jax.numpy as jnp
from jax import lax
from jax.experimental import pallas as pl
from jax.experimental.pallas import tpu as pltpu
from jax.sharding import PartitionSpec as P

HEADS = 12
ROW = 2
LAYERS = 4
MESH = pl.DeviceIdType.MESH


def layer_norm(values_in):
    values_in = values_in.astype(jnp.float32)
    centre = jnp.mean(values_in, axis=-1, keepdims=True)
    spread = jnp.mean((values_in - centre) ** 2, axis=-1, keepdims=True)
    return (values_in - centre) * lax.rsqrt(spread + 1e-05)


def project(rows, weights):
    return jnp.dot(rows, weights, preferred_element_type=jnp.float32)


def attend(query, normed, w_key, w_value, pair, store):
    features = normed.shape[1]
    size = features // HEADS
    lower = lax.broadcasted_iota(jnp.int32, (1, 2 * size), 1) < size
    pair[:, :features] = project(normed, w_key[...]).astype(jnp.bfloat16)
    pair[:, features:] = project(normed, w_value[...]).astype(jnp.bfloat16)
    for h in range(HEADS // 2):
        cols = pl.ds(2 * h * size, 2 * size)
        rows = query(cols)
        key = pair[:, cols]
        value = pair[:, pl.ds(features + 2 * h * size, 2 * size)]
        halves = []
        for keep in (lower, jnp.logical_not(lower)):
            part = jnp.where(keep, rows, jnp.zeros_like(rows))
            scores = lax.dot_general(
                part, key, (((1,), (1,)), ((), ())), preferred_element_type=jnp.float32
            )
            top = jnp.max(scores, axis=-1, keepdims=True)
            weights = jnp.exp(scores - top)
            mass = jnp.sum(weights, axis=-1, keepdims=True)
            halves.append(project(weights.astype(jnp.bfloat16), value) / mass)
        store(cols, jnp.where(lower, halves[0], halves[1]))


RAW_BLOCK, RAW_PLACE, POSITION, BLOCK, PLACE, VIEW = range(6)


def build_tables(layer, side, degree, capacity, views, members, partners, key_view, ask, table):
    entries = views * degree
    low = layer < LAYERS // 2

    def mirror(value):
        return jnp.where(low, value, LAYERS - 1 - value)

    here = mirror(layer)

    def read(e, flags):
        partner = partners[lax.div(e, degree), lax.rem(e, degree)]
        peer = lax.rem(lax.div(partner, views), members)
        place = lax.rem(partner, views)
        there = mirror(lax.div(peer, ROW))
        inside = jnp.where(there == 0, 1, jnp.where(there == 2, 0, 2))
        turn = jnp.where(here == 0, there - 1, inside)
        across = (lax.rem(peer, ROW) != side).astype(jnp.int32)
        block = jnp.where(there == here, 0, 1 + 2 * turn + across)
        table[RAW_BLOCK, e] = block
        table[RAW_PLACE, e] = place
        return tuple(
            jnp.where((block == 2 + 2 * (i // views)) & (place == i % views), 1, flag)
            for i, flag in enumerate(flags)
        )

    flags = lax.fori_loop(0, entries, read, (jnp.int32(0),) * (3 * views))
    slots = []
    for j in range(3):
        wanted = flags[j * views : (j + 1) * views]
        slot = capacity - sum(wanted)
        for v in range(views):
            slots.append(slot)
            slot = slot + wanted[v]
        for k in range(capacity):
            ask[0, j * capacity + k] = sum(
                jnp.where((wanted[v] == 1) & (slots[j * views + v] == k), v, 0) for v in range(views)
            )

    def rank(e, carry):
        block, place = table[RAW_BLOCK, e], table[RAW_PLACE, e]
        position = jnp.int32(2)
        for other in range(entries):
            ahead = (table[RAW_BLOCK, other] * entries + other) < block * entries + e
            position = position + ahead.astype(jnp.int32)
        table[POSITION, e] = position
        spot = place
        for i, slot in enumerate(slots):
            spot = jnp.where((block == 2 + 2 * (i // views)) & (place == i % views), slot, spot)
        table[RAW_PLACE, e] = spot
        return carry

    lax.fori_loop(0, entries, rank, 0)

    def sort(r, carry):
        block, place, view = jnp.int32(-1), jnp.int32(0), key_view
        for e in range(entries):
            match = table[POSITION, e] == r
            block = jnp.where(match, table[RAW_BLOCK, e], block)
            place = jnp.where(match, table[RAW_PLACE, e], place)
            view = jnp.where(match, e // degree, view)
        table[BLOCK, r], table[PLACE, r], table[VIEW, r] = block, place, view
        return carry

    lax.fori_loop(0, entries + 2, sort, 0)


def sublayer_kernel(degree, capacity, *refs):
    partners, counts, key_slot, tokens, wq_in, wk_in, wv_in, wo_in, out_ref = refs[:9]
    w_query, w_key, w_value, w_out = refs[9:13]
    own, queries, near, b0, b1, b2, s0, s1, s2, keys, staged, key_out = refs[13:25]
    ask, asked, table, cur, pair, results, load_sem, send_sem, recv_sem = refs[25:]
    views, length, features = tokens.shape
    members, groups = lax.axis_size("member"), lax.axis_size("group")
    entries = views * degree
    peers = members - 1
    size = features // HEADS
    me, group = lax.axis_index("member"), lax.axis_index("group")
    layer, side = me // ROW, me % ROW
    low = layer < LAYERS // 2
    toward = jnp.where(low, ROW, -ROW)
    is_end = jnp.logical_or(layer == 0, layer == LAYERS - 1)
    is_mid = jnp.logical_not(is_end)
    beside = {"member": layer * ROW + 1 - side}
    inner = {"member": me + toward}
    outer = {"member": jnp.clip(me - toward, 0, members - 1)}
    above = {"group": lax.rem(group + 1, groups)}
    below = {"group": lax.rem(group + groups - 1, groups)}

    blocks = (near, b0, s0, b1, s1, b2, s2)
    base, total = {}, 0
    for name, ref in (("near", near), ("b0", b0), ("b1", b1), ("b2", b2), ("s0", s0),
                      ("s1", s1), ("s2", s2), ("keys", keys)):
        base[name] = total
        total += ref.shape[0]

    def remote(source, target, send, recv, device):
        return pltpu.make_async_remote_copy(
            src_ref=source, dst_ref=target, send_sem=send_sem.at[send],
            recv_sem=recv_sem.at[recv], device_id=device, device_id_type=MESH,
        )

    sends = {}

    def slot(name, index):
        return sends.setdefault((name, index), len(sends))

    def hop(name, source, v, target, target_name, device):
        return remote(source.at[v], target.at[v], slot(name, v), base[target_name] + v, device)

    def to_near(v):
        return hop("near", own, v, near, "near", beside)

    def own_to_b1(v):
        return hop("in", own, v, b1, "b1", inner)

    def own_to_b0(v):
        return hop("in", own, v, b0, "b0", inner)

    def own_out(v):
        return hop("out", own, v, b0, "b0", outer)

    def b1_in(v):
        return hop("in2", b1, v, b2, "b2", inner)

    def b0_out(v):
        return hop("out1", b0, v, b1, "b1", outer)

    def b2_out(v):
        return hop("out2", b2, v, b2, "b2", outer)

    swaps = (s0, s1, s2)

    def swap(j, k):
        return remote(
            staged.at[j * capacity + k], swaps[j].at[k], slot("swap", j * capacity + k),
            base[f"s{j}"] + k, beside,
        )

    def key_send(i):
        return remote(
            key_out, keys.at[i], slot("key", i), base["keys"] + i, above if i == 0 else below
        )

    def ask_send():
        return remote(ask, asked, slot("ask", 0), total, beside)

    loads = [
        pltpu.make_async_copy(source, target, load_sem.at[i])
        for i, (source, target) in enumerate(
            ((wq_in, w_query), (wk_in, w_key), (wv_in, w_value), (wo_in, w_out))
        )
    ]
    for load in loads:
        load.start()

    barrier = pltpu.get_barrier_semaphore()
    for device in (beside, inner, above, below):
        pl.semaphore_signal(barrier, inc=1, device_id=device, device_id_type=MESH)

    @pl.when(is_mid)
    def _():
        pl.semaphore_signal(barrier, inc=1, device_id=outer, device_id_type=MESH)

    own[0] = layer_norm(tokens[0]).astype(jnp.bfloat16)

    @pl.when(is_mid)
    def _():
        pl.semaphore_wait(barrier, 5)

    @pl.when(is_end)
    def _():
        pl.semaphore_wait(barrier, 4)

    for v in range(views):
        if v:
            own[v] = layer_norm(tokens[v]).astype(jnp.bfloat16)
        to_near(v).start()

        @pl.when(is_end)
        def _():
            own_to_b1(v).start()

        @pl.when(is_mid)
        def _():
            own_to_b0(v).start()
            own_out(v).start()

    key_view = key_slot[0]
    key_out[...] = own[key_view]
    loads[0].wait()
    for v in range(views):
        queries[v] = project(own[v], w_query[...]).astype(jnp.bfloat16) * jnp.bfloat16(size**-0.5)
    for i in range(2):
        key_send(i).start()
    build_tables(layer, side, degree, capacity, views, members, partners, key_view, ask, table)
    ask_send().start()
    loads[1].wait()
    loads[2].wait()
    for i in range(2):
        key_send(i).wait_recv()

    def stage(j, k, source):
        choice = asked[0, j * capacity + k]
        value = source[0]
        for v in range(1, k + views - capacity + 1):
            value = jnp.where(choice == v, source[v], value)
        staged[j * capacity + k] = value
        swap(j, k).start()

    def events(t):
        def far(v):
            @pl.when(is_end)
            def _():
                b0_out(v).wait_recv()

            @pl.when(is_mid)
            def _():
                b1_in(v).wait_recv()
                b2_out(v).start()

        def last(v):
            @pl.when(is_end)
            def _():
                b2_out(v).wait_recv()

        def arrive(j):
            for k in range(capacity):
                swap(j, k).wait_recv()

        extra = views - capacity

        def spread(wait, j, source, v):
            wait(v)
            if v >= extra:
                stage(j, v - extra, source)

        if t == first[0]:
            for v in range(views):
                own_to_b0(v).wait_recv()

                @pl.when(is_mid)
                def _():
                    b0_out(v).start()
                    own_to_b1(v).wait_recv()
                    b1_in(v).start()

                if v >= extra:
                    stage(0, v - extra, b0)
            for v in range(views):
                to_near(v).wait_recv()
        if t == first[2]:
            for v in range(views - 2):
                spread(far, 1, b1, v)
            arrive(0)
        if t == first[2] + 1:
            spread(far, 1, b1, views - 2)
        if t == first[3]:
            spread(far, 1, b1, views - 1)
        if t == first[4]:
            for v in range(views - 2):
                spread(last, 2, b2, v)
            arrive(1)
        if t == first[4] + 1:
            spread(last, 2, b2, views - 2)
        if t == first[5]:
            spread(last, 2, b2, views - 1)
        if t == first[6]:
            arrive(2)

    first = [2 + max(0, entries - capacity * (peers - j)) for j in range(peers)]

    def entry(t, carry):
        for when in sorted({first[0], first[2], first[2] + 1, first[3], first[4], first[4] + 1,
                            first[5], first[6]}):
            @pl.when(t == when)
            def _():
                events(when)

        @pl.when(t < 2)
        def _():
            cur[...] = keys[jnp.minimum(t, 1)]

        block, place, view = table[BLOCK, t], table[PLACE, t], table[VIEW, t]
        for j, ref in enumerate(blocks):
            @pl.when(t >= first[j])
            def _():
                value = ref[jnp.minimum(place, ref.shape[0] - 1)]
                cur[...] = jnp.where(block == j, value, cur[...])

        def store(cols, value):
            results[t, :, cols] = value

        attend(lambda cols: queries[view, :, cols], cur[...], w_key, w_value, pair, store)
        return carry

    ask_send().wait_recv()
    lax.fori_loop(0, entries + 2, entry, 0)
    loads[3].wait()
    for v in range(views):
        is_key = (key_view == v).astype(jnp.int32)
        count = counts[v]
        mixed = is_key.astype(jnp.float32) * (results[0] + results[1])
        for e in range(degree):
            live = (count > e).astype(jnp.int32).astype(jnp.float32)
            mixed += live * results[table[POSITION, v * degree + e]]
        divisor = jnp.full((1, features), count + 2 * is_key, jnp.int32).astype(jnp.float32)
        mixed = mixed * (1.0 / divisor)
        out_ref[v] = (
            tokens[v].astype(jnp.float32) + project(mixed.astype(jnp.bfloat16), w_out[...])
        ).astype(out_ref.dtype)

    for v in range(views):
        to_near(v).wait_send()

        @pl.when(is_end)
        def _():
            own_to_b1(v).wait_send()

        @pl.when(is_mid)
        def _():
            own_to_b0(v).wait_send()
            own_out(v).wait_send()
            b1_in(v).wait_send()
            b0_out(v).wait_send()
            b2_out(v).wait_send()

    for j in range(3):
        for k in range(capacity):
            swap(j, k).wait_send()
    for i in range(2):
        key_send(i).wait_send()
    ask_send().wait_send()


def one_kernel(tokens, w_query, w_key, w_value, w_out, partners, counts, key_slot):
    views, length, features = tokens.shape
    members = lax.axis_size("member")
    degree = partners.shape[1]
    entries = views * degree
    capacity = (entries + members - 2) // (members - 1)
    smem = pl.BlockSpec(memory_space=pltpu.SMEM)
    hbm = pl.BlockSpec(memory_space=pltpu.HBM)
    vmem = pl.BlockSpec(memory_space=pltpu.VMEM)
    stay = [
        pltpu.with_memory_space_constraint(w, pltpu.HBM) for w in (w_query, w_key, w_value, w_out)
    ]
    slab = (length, features)
    weights_shape = pltpu.VMEM((features, features), jnp.bfloat16)
    half = jnp.bfloat16
    blocks = [pltpu.VMEM((views, *slab), half)] * 6 + [pltpu.VMEM((capacity, *slab), half)] * 3
    sends = 6 * views + 3 * capacity + 3 + views
    receives = 4 * views + 3 * capacity + 3
    return pl.pallas_call(
        functools.partial(sublayer_kernel, degree, capacity),
        out_shape=jax.ShapeDtypeStruct(tokens.shape, tokens.dtype),
        in_specs=[smem] * 3 + [vmem] + [hbm] * 4,
        out_specs=vmem,
        scratch_shapes=[
            weights_shape,
            weights_shape,
            weights_shape,
            weights_shape,
            *blocks,
            pltpu.VMEM((2, *slab), half),
            pltpu.VMEM((3 * capacity, *slab), half),
            pltpu.VMEM(slab, half),
            pltpu.SMEM((1, 3 * capacity), jnp.int32),
            pltpu.SMEM((1, 3 * capacity), jnp.int32),
            pltpu.SMEM((6, entries + 2), jnp.int32),
            pltpu.VMEM(slab, half),
            pltpu.VMEM((length, 2 * features), half),
            pltpu.VMEM((entries + 2, *slab), jnp.float32),
            pltpu.SemaphoreType.DMA((4,)),
            pltpu.SemaphoreType.DMA((sends,)),
            pltpu.SemaphoreType.DMA((receives,)),
        ],
        compiler_params=pltpu.CompilerParams(
            collective_id=0, has_side_effects=True, vmem_limit_bytes=44 * 1024 * 1024
        ),
        name="sublayer",
    )(partners, counts, key_slot, tokens, *stay)


def local_kernel(table, queries, w_key, w_value, block, inverse, tokens, w_out, out_ref, *scratch):
    held, pair, total, sem = scratch
    copy = pltpu.make_async_copy(block, held, sem)
    copy.start()
    total[...] = jnp.zeros_like(total)
    copy.wait()
    views, length, _ = total.shape

    def entry(e, carry):
        @pl.when(table[0, e] == 1)
        def _():
            place, view = table[1, e], table[2, e]

            def store(cols, value):
                total[view, :, cols] += value

            normed = layer_norm(held[place]).astype(jnp.bfloat16)
            attend(lambda cols: queries[view, :, cols], normed, w_key, w_value, pair, store)

        return carry

    lax.fori_loop(0, table.shape[1], entry, 0)
    for v in range(views):
        mixed = (total[v] * inverse[v]).astype(jnp.bfloat16)
        out_ref[v] = (tokens[v].astype(jnp.float32) + project(mixed, w_out[...])).astype(out_ref.dtype)


def exchange(tokens, w_query, w_key, w_value, w_out, partners, counts, key_slot):
    slot_key = key_slot[0]
    views, length, features = tokens.shape
    members, groups = lax.axis_size("member"), lax.axis_size("group")
    degree = partners.shape[1]
    entry_list = partners.reshape(-1)
    entries = entry_list.shape[0]
    capacity = (entries + members - 2) // (members - 1)
    peers = entry_list // views % members
    places = entry_list % views
    order = jnp.arange(entries, dtype=jnp.int32)
    earlier = (peers[:, None] == peers[None, :]) & (order[None, :] < order[:, None])
    cells = peers * capacity + jnp.sum(earlier.astype(jnp.int32), axis=1)
    requests = jnp.zeros((members * capacity,), jnp.int32).at[cells].set(places)
    asked = lax.all_to_all(
        requests.reshape(members, capacity), "member", split_axis=0, concat_axis=0, tiled=True
    )
    outgoing = tokens[asked.reshape(-1)].reshape(members, capacity, length, features)
    arrived = lax.all_to_all(outgoing, "member", split_axis=0, concat_axis=0, tiled=True)
    own_key = lax.dynamic_slice_in_dim(tokens, slot_key, 1, 0)
    below = lax.ppermute(own_key, "group", [(g, (g + 1) % groups) for g in range(groups)])
    above = lax.ppermute(own_key, "group", [((g + 1) % groups, g) for g in range(groups)])
    block = jnp.concatenate((arrived.reshape(members * capacity, length, features), below, above))
    normed = layer_norm(tokens).astype(jnp.bfloat16)
    queries = project(normed.reshape(views * length, features), w_query).astype(jnp.bfloat16)
    queries = queries.reshape(tokens.shape) * jnp.bfloat16((features // HEADS) ** -0.5)
    is_key = (jnp.arange(views, dtype=jnp.int32) == slot_key).astype(jnp.int32)
    inverse = 1.0 / (counts + 2 * is_key).astype(jnp.float32)
    live = (jnp.arange(degree, dtype=jnp.int32)[None, :] < counts[:, None]).reshape(-1)
    two = jnp.arange(2, dtype=jnp.int32)
    table = jnp.stack(
        (
            jnp.concatenate((live.astype(jnp.int32), jnp.ones_like(two))),
            jnp.concatenate((cells, members * capacity + two)),
            jnp.concatenate((order // degree, jnp.full_like(two, slot_key))),
        )
    )
    vmem = pl.BlockSpec(memory_space=pltpu.VMEM)
    smem = pl.BlockSpec(memory_space=pltpu.SMEM)
    hbm = pl.BlockSpec(memory_space=pl.ANY)
    return pl.pallas_call(
        local_kernel,
        out_shape=jax.ShapeDtypeStruct(tokens.shape, tokens.dtype),
        in_specs=[smem, vmem, vmem, vmem, hbm, smem, vmem, vmem],
        out_specs=vmem,
        scratch_shapes=[
            pltpu.VMEM(block.shape, block.dtype),
            pltpu.VMEM((length, 2 * features), jnp.bfloat16),
            pltpu.VMEM(tokens.shape, jnp.float32),
            pltpu.SemaphoreType.DMA,
        ],
        compiler_params=pltpu.CompilerParams(vmem_limit_bytes=60 * 1024 * 1024),
        name="attend_all",
    )(table, queries, w_key, w_value, block, inverse, tokens, w_out)


def sublayer(tokens, w_query, w_key, w_value, w_out, partners, counts, key_slot):
    views = tokens.shape[0]
    members = lax.axis_size("member")
    entries = partners.shape[0] * partners.shape[1]
    capacity = (entries + members - 2) // (members - 1)
    grid = members == LAYERS * ROW and views == capacity + 1
    run = one_kernel if grid else exchange
    return run(tokens, w_query, w_key, w_value, w_out, partners, counts, key_slot)


def solution(mesh):
    return jax.shard_map(
        sublayer,
        mesh=mesh,
        in_specs=(
            P(("group", "member"), None, None),
            P(),
            P(),
            P(),
            P(),
            P(("group", "member"), None),
            P(("group", "member")),
            P(("group", "member")),
        ),
        out_specs=P(("group", "member"), None, None),
        check_vma=False,
    )
```

```python
import functools

import jax
import jax.numpy as jnp
from jax import lax
from jax.experimental import pallas as pl
from jax.experimental.pallas import tpu as pltpu
from jax.sharding import PartitionSpec as P

HEADS = 12
ROW = 2
LAYERS = 4
MESH = pl.DeviceIdType.MESH


def layer_norm(values_in):
    values_in = values_in.astype(jnp.float32)
    centre = jnp.mean(values_in, axis=-1, keepdims=True)
    spread = jnp.mean((values_in - centre) ** 2, axis=-1, keepdims=True)
    return (values_in - centre) * lax.rsqrt(spread + 1e-05)


def project(rows, weights):
    return jnp.dot(rows, weights, preferred_element_type=jnp.float32)


def attend(query, normed, w_key, w_value, pair, store):
    features = normed.shape[1]
    size = features // HEADS
    lower = lax.broadcasted_iota(jnp.int32, (1, 2 * size), 1) < size
    pair[:, :features] = project(normed, w_key[...]).astype(jnp.bfloat16)
    pair[:, features:] = project(normed, w_value[...]).astype(jnp.bfloat16)
    for h in range(HEADS // 2):
        cols = pl.ds(2 * h * size, 2 * size)
        rows = query(cols)
        key = pair[:, cols]
        value = pair[:, pl.ds(features + 2 * h * size, 2 * size)]
        halves = []
        for keep in (lower, jnp.logical_not(lower)):
            part = jnp.where(keep, rows, jnp.zeros_like(rows))
            scores = lax.dot_general(
                part, key, (((1,), (1,)), ((), ())), preferred_element_type=jnp.float32
            )
            top = jnp.max(scores, axis=-1, keepdims=True)
            weights = jnp.exp(scores - top)
            mass = jnp.sum(weights, axis=-1, keepdims=True)
            halves.append(project(weights.astype(jnp.bfloat16), value) / mass)
        store(cols, jnp.where(lower, halves[0], halves[1]))


RAW_BLOCK, RAW_PLACE, POSITION, BLOCK, PLACE, VIEW = range(6)


def build_tables(layer, side, degree, capacity, views, members, partners, key_view, ask, table):
    entries = views * degree
    low = layer < LAYERS // 2

    def mirror(value):
        return jnp.where(low, value, LAYERS - 1 - value)

    here = mirror(layer)

    def read(e, flags):
        partner = partners[lax.div(e, degree), lax.rem(e, degree)]
        peer = lax.rem(lax.div(partner, views), members)
        place = lax.rem(partner, views)
        there = mirror(lax.div(peer, ROW))
        inside = jnp.where(there == 0, 1, jnp.where(there == 2, 0, 2))
        turn = jnp.where(here == 0, there - 1, inside)
        across = (lax.rem(peer, ROW) != side).astype(jnp.int32)
        block = jnp.where(there == here, 0, 1 + 2 * turn + across)
        table[RAW_BLOCK, e] = block
        table[RAW_PLACE, e] = place
        return tuple(
            jnp.where((block == 2 + 2 * (i // views)) & (place == i % views), 1, flag)
            for i, flag in enumerate(flags)
        )

    flags = lax.fori_loop(0, entries, read, (jnp.int32(0),) * (3 * views))
    slots = []
    for j in range(3):
        wanted = flags[j * views : (j + 1) * views]
        slot = capacity - sum(wanted)
        for v in range(views):
            slots.append(slot)
            slot = slot + wanted[v]
        for k in range(capacity):
            ask[0, j * capacity + k] = sum(
                jnp.where((wanted[v] == 1) & (slots[j * views + v] == k), v, 0) for v in range(views)
            )

    def rank(e, carry):
        block, place = table[RAW_BLOCK, e], table[RAW_PLACE, e]
        position = jnp.int32(2)
        for other in range(entries):
            ahead = (table[RAW_BLOCK, other] * entries + other) < block * entries + e
            position = position + ahead.astype(jnp.int32)
        table[POSITION, e] = position
        spot = place
        for i, slot in enumerate(slots):
            spot = jnp.where((block == 2 + 2 * (i // views)) & (place == i % views), slot, spot)
        table[RAW_PLACE, e] = spot
        return carry

    lax.fori_loop(0, entries, rank, 0)

    def sort(r, carry):
        block, place, view = jnp.int32(-1), jnp.int32(0), key_view
        for e in range(entries):
            match = table[POSITION, e] == r
            block = jnp.where(match, table[RAW_BLOCK, e], block)
            place = jnp.where(match, table[RAW_PLACE, e], place)
            view = jnp.where(match, e // degree, view)
        table[BLOCK, r], table[PLACE, r], table[VIEW, r] = block, place, view
        return carry

    lax.fori_loop(0, entries + 2, sort, 0)


def sublayer_kernel(degree, capacity, *refs):
    partners, counts, key_slot, tokens, wq_in, wk_in, wv_in, wo_in, out_ref = refs[:9]
    w_query, w_key, w_value, w_out = refs[9:13]
    own, queries, near, b0, b1, b2, s0, s1, s2, keys, staged, key_out = refs[13:25]
    ask, asked, table, cur, pair, results, load_sem, send_sem, recv_sem = refs[25:]
    views, length, features = tokens.shape
    members, groups = lax.axis_size("member"), lax.axis_size("group")
    entries = views * degree
    peers = members - 1
    size = features // HEADS
    me, group = lax.axis_index("member"), lax.axis_index("group")
    layer, side = me // ROW, me % ROW
    low = layer < LAYERS // 2
    toward = jnp.where(low, ROW, -ROW)
    is_end = jnp.logical_or(layer == 0, layer == LAYERS - 1)
    is_mid = jnp.logical_not(is_end)
    beside = {"member": layer * ROW + 1 - side}
    inner = {"member": me + toward}
    outer = {"member": jnp.clip(me - toward, 0, members - 1)}
    above = {"group": lax.rem(group + 1, groups)}
    below = {"group": lax.rem(group + groups - 1, groups)}

    blocks = (near, b0, s0, b1, s1, b2, s2)
    base, total = {}, 0
    for name, ref in (("near", near), ("b0", b0), ("b1", b1), ("b2", b2), ("s0", s0),
                      ("s1", s1), ("s2", s2), ("keys", keys)):
        base[name] = total
        total += ref.shape[0]

    def remote(source, target, send, recv, device):
        return pltpu.make_async_remote_copy(
            src_ref=source, dst_ref=target, send_sem=send_sem.at[send],
            recv_sem=recv_sem.at[recv], device_id=device, device_id_type=MESH,
        )

    sends = {}

    def slot(name, index):
        return sends.setdefault((name, index), len(sends))

    def hop(name, source, v, target, target_name, device):
        return remote(source.at[v], target.at[v], slot(name, v), base[target_name] + v, device)

    def to_near(v):
        return hop("near", own, v, near, "near", beside)

    def own_to_b1(v):
        return hop("in", own, v, b1, "b1", inner)

    def own_to_b0(v):
        return hop("in", own, v, b0, "b0", inner)

    def own_out(v):
        return hop("out", own, v, b0, "b0", outer)

    def b1_in(v):
        return hop("in2", b1, v, b2, "b2", inner)

    def b0_out(v):
        return hop("out1", b0, v, b1, "b1", outer)

    def b2_out(v):
        return hop("out2", b2, v, b2, "b2", outer)

    swaps = (s0, s1, s2)

    def swap(j, k):
        return remote(
            staged.at[j * capacity + k], swaps[j].at[k], slot("swap", j * capacity + k),
            base[f"s{j}"] + k, beside,
        )

    def key_send(i):
        return remote(
            key_out, keys.at[i], slot("key", i), base["keys"] + i, above if i == 0 else below
        )

    def ask_send():
        return remote(ask, asked, slot("ask", 0), total, beside)

    loads = [
        pltpu.make_async_copy(source, target, load_sem.at[i])
        for i, (source, target) in enumerate(
            ((wq_in, w_query), (wk_in, w_key), (wv_in, w_value), (wo_in, w_out))
        )
    ]
    for load in loads:
        load.start()

    barrier = pltpu.get_barrier_semaphore()
    for device in (beside, inner, above, below):
        pl.semaphore_signal(barrier, inc=1, device_id=device, device_id_type=MESH)

    @pl.when(is_mid)
    def _():
        pl.semaphore_signal(barrier, inc=1, device_id=outer, device_id_type=MESH)

    own[0] = layer_norm(tokens[0]).astype(jnp.bfloat16)

    @pl.when(is_mid)
    def _():
        pl.semaphore_wait(barrier, 5)

    @pl.when(is_end)
    def _():
        pl.semaphore_wait(barrier, 4)

    for v in range(views):
        if v:
            own[v] = layer_norm(tokens[v]).astype(jnp.bfloat16)
        to_near(v).start()

        @pl.when(is_end)
        def _():
            own_to_b1(v).start()

        @pl.when(is_mid)
        def _():
            own_to_b0(v).start()
            own_out(v).start()

    key_view = key_slot[0]
    key_out[...] = own[key_view]
    loads[0].wait()
    for v in range(views):
        queries[v] = project(own[v], w_query[...]).astype(jnp.bfloat16) * jnp.bfloat16(size**-0.5)
    for i in range(2):
        key_send(i).start()
    build_tables(layer, side, degree, capacity, views, members, partners, key_view, ask, table)
    ask_send().start()
    loads[1].wait()
    loads[2].wait()
    for i in range(2):
        key_send(i).wait_recv()

    def stage(j, k, source):
        choice = asked[0, j * capacity + k]
        value = source[0]
        for v in range(1, k + views - capacity + 1):
            value = jnp.where(choice == v, source[v], value)
        staged[j * capacity + k] = value
        swap(j, k).start()

    def events(t):
        def far(v):
            @pl.when(is_end)
            def _():
                b0_out(v).wait_recv()

            @pl.when(is_mid)
            def _():
                b1_in(v).wait_recv()
                b2_out(v).start()

        def last(v):
            @pl.when(is_end)
            def _():
                b2_out(v).wait_recv()

        def arrive(j):
            for k in range(capacity):
                swap(j, k).wait_recv()

        extra = views - capacity

        def spread(wait, j, source, v):
            wait(v)
            if v >= extra:
                stage(j, v - extra, source)

        if t == first[0]:
            for v in range(views):
                own_to_b0(v).wait_recv()

                @pl.when(is_mid)
                def _():
                    b0_out(v).start()
                    own_to_b1(v).wait_recv()
                    b1_in(v).start()

                if v >= extra:
                    stage(0, v - extra, b0)
            for v in range(views):
                to_near(v).wait_recv()
        if t == first[2]:
            for v in range(views - 2):
                spread(far, 1, b1, v)
            arrive(0)
        if t == first[2] + 1:
            spread(far, 1, b1, views - 2)
        if t == first[3]:
            spread(far, 1, b1, views - 1)
        if t == first[4]:
            for v in range(views - 2):
                spread(last, 2, b2, v)
            arrive(1)
        if t == first[4] + 1:
            spread(last, 2, b2, views - 2)
        if t == first[5]:
            spread(last, 2, b2, views - 1)
        if t == first[6]:
            arrive(2)

    first = [2 + max(0, entries - capacity * (peers - j)) for j in range(peers)]

    def entry(t, carry):
        for when in sorted({first[0], first[2], first[2] + 1, first[3], first[4], first[4] + 1,
                            first[5], first[6]}):
            @pl.when(t == when)
            def _():
                events(when)

        @pl.when(t < 2)
        def _():
            cur[...] = keys[jnp.minimum(t, 1)]

        block, place, view = table[BLOCK, t], table[PLACE, t], table[VIEW, t]
        for j, ref in enumerate(blocks):
            @pl.when(t >= first[j])
            def _():
                value = ref[jnp.minimum(place, ref.shape[0] - 1)]
                cur[...] = jnp.where(block == j, value, cur[...])

        def store(cols, value):
            results[t, :, cols] = value

        attend(lambda cols: queries[view, :, cols], cur[...], w_key, w_value, pair, store)
        return carry

    ask_send().wait_recv()
    lax.fori_loop(0, entries + 2, entry, 0)
    loads[3].wait()
    for v in range(views):
        is_key = (key_view == v).astype(jnp.int32)
        count = counts[v]
        mixed = is_key.astype(jnp.float32) * (results[0] + results[1])
        for e in range(degree):
            live = (count > e).astype(jnp.int32).astype(jnp.float32)
            mixed += live * results[table[POSITION, v * degree + e]]
        divisor = jnp.full((1, features), count + 2 * is_key, jnp.int32).astype(jnp.float32)
        mixed = mixed * (1.0 / divisor)
        out_ref[v] = (
            tokens[v].astype(jnp.float32) + project(mixed.astype(jnp.bfloat16), w_out[...])
        ).astype(out_ref.dtype)

    for v in range(views):
        to_near(v).wait_send()

        @pl.when(is_end)
        def _():
            own_to_b1(v).wait_send()

        @pl.when(is_mid)
        def _():
            own_to_b0(v).wait_send()
            own_out(v).wait_send()
            b1_in(v).wait_send()
            b0_out(v).wait_send()
            b2_out(v).wait_send()

    for j in range(3):
        for k in range(capacity):
            swap(j, k).wait_send()
    for i in range(2):
        key_send(i).wait_send()
    ask_send().wait_send()


def one_kernel(tokens, w_query, w_key, w_value, w_out, partners, counts, key_slot):
    views, length, features = tokens.shape
    members = lax.axis_size("member")
    degree = partners.shape[1]
    entries = views * degree
    capacity = (entries + members - 2) // (members - 1)
    smem = pl.BlockSpec(memory_space=pltpu.SMEM)
    hbm = pl.BlockSpec(memory_space=pltpu.HBM)
    vmem = pl.BlockSpec(memory_space=pltpu.VMEM)
    stay = [
        pltpu.with_memory_space_constraint(w, pltpu.HBM) for w in (w_query, w_key, w_value, w_out)
    ]
    slab = (length, features)
    weights_shape = pltpu.VMEM((features, features), jnp.bfloat16)
    half = jnp.bfloat16
    blocks = [pltpu.VMEM((views, *slab), half)] * 6 + [pltpu.VMEM((capacity, *slab), half)] * 3
    sends = 6 * views + 3 * capacity + 3 + views
    receives = 4 * views + 3 * capacity + 3
    return pl.pallas_call(
        functools.partial(sublayer_kernel, degree, capacity),
        out_shape=jax.ShapeDtypeStruct(tokens.shape, tokens.dtype),
        in_specs=[smem] * 3 + [vmem] + [hbm] * 4,
        out_specs=vmem,
        scratch_shapes=[
            weights_shape,
            weights_shape,
            weights_shape,
            weights_shape,
            *blocks,
            pltpu.VMEM((2, *slab), half),
            pltpu.VMEM((3 * capacity, *slab), half),
            pltpu.VMEM(slab, half),
            pltpu.SMEM((1, 3 * capacity), jnp.int32),
            pltpu.SMEM((1, 3 * capacity), jnp.int32),
            pltpu.SMEM((6, entries + 2), jnp.int32),
            pltpu.VMEM(slab, half),
            pltpu.VMEM((length, 2 * features), half),
            pltpu.VMEM((entries + 2, *slab), jnp.float32),
            pltpu.SemaphoreType.DMA((4,)),
            pltpu.SemaphoreType.DMA((sends,)),
            pltpu.SemaphoreType.DMA((receives,)),
        ],
        compiler_params=pltpu.CompilerParams(
            collective_id=0, has_side_effects=True, vmem_limit_bytes=44 * 1024 * 1024
        ),
        name="sublayer",
    )(partners, counts, key_slot, tokens, *stay)


FAR, WIDE = 9, 7
FREE, SLOTS, CROSS, PLAIN = 4, 5, 5 + FAR, 5 + FAR + WIDE


def quick_kernel(degree, *refs):
    partners, counts, key_slot, tokens, wq_in, wk_in, wv_in, wo_in, out_ref, flag_ref = refs[:10]
    w_query, w_key, w_value, w_out = refs[10:14]
    own, queries, near, b0, b1, b2, first_view, far, wide, keys, far_out, wide_out, key_out = refs[14:27]
    ask, asked, union, codes, sources, picks, table, cur, pair, results = refs[27:37]
    load_sem, send_sem, recv_sem = refs[37:40]
    notes = refs[40:]
    views, length, features = tokens.shape
    members, groups = lax.axis_size("member"), lax.axis_size("group")
    entries = views * degree
    size = features // HEADS
    me, group = lax.axis_index("member"), lax.axis_index("group")
    layer, side = me // ROW, me % ROW
    low = layer < LAYERS // 2
    toward = jnp.where(low, ROW, -ROW)
    is_end = jnp.logical_or(layer == 0, layer == LAYERS - 1)
    is_mid = jnp.logical_not(is_end)
    beside = {"member": layer * ROW + 1 - side}
    inner = {"member": me + toward}
    outer = {"member": jnp.clip(me - toward, 0, members - 1)}
    above = {"group": lax.rem(group + 1, groups)}
    below = {"group": lax.rem(group + groups - 1, groups)}
    key_view = key_slot[0]
    cells = 7 * views
    names = {}

    def number(kind, name):
        return names.setdefault((kind, name), sum(1 for k, _ in names if k == kind))

    def remote(name, source, target, landing, device):
        return pltpu.make_async_remote_copy(
            src_ref=source, dst_ref=target, send_sem=send_sem.at[number(0, name)],
            recv_sem=recv_sem.at[number(1, landing)], device_id=device, device_id_type=MESH,
        )

    def to_near(v):
        return remote(("near", v), own.at[v], near.at[v], ("near", v), beside)

    def own_to_b1(v):
        return remote(("in", v), own.at[v], b1.at[v], ("b1", v), inner)

    def own_to_b0(v):
        return remote(("in", v), own.at[v], b0.at[v], ("b0", v), inner)

    def b1_in(v):
        return remote(("in2", v), b1.at[v], b2.at[v], ("b2", v), inner)

    def own_out():
        return remote("free", own.at[0], first_view, "free", outer)

    def far_send(q):
        return remote(("far", q), far_out.at[q], far.at[q], ("far", q), outer)

    def wide_send(k):
        return remote(("wide", k), wide_out.at[k], wide.at[k], ("wide", k), beside)

    def key_send(i):
        return remote(("key", i), key_out, keys.at[i], ("key", i), below if i else above)

    def ask_send():
        return remote("ask", ask, asked, "ask", beside)

    def union_send():
        return remote("union", union, union, "union", inner)

    def note(i, device):
        return remote(("note", i), notes[2 * i], notes[2 * i + 1], ("note", i), device)

    loads = [
        pltpu.make_async_copy(source, target, load_sem.at[i])
        for i, (source, target) in enumerate(
            ((wq_in, w_query), (wk_in, w_key), (wv_in, w_value), (wo_in, w_out))
        )
    ]
    for load in loads:
        load.start()
    barrier = pltpu.get_barrier_semaphore()
    for device in (beside, inner, above, below):
        pl.semaphore_signal(barrier, inc=1, device_id=device, device_id_type=MESH)

    @pl.when(is_mid)
    def _():
        pl.semaphore_signal(barrier, inc=1, device_id=outer, device_id_type=MESH)

    def mirror(value):
        return jnp.where(low, value, LAYERS - 1 - value)

    here = mirror(layer)

    def read(e, carry):
        partner = partners[lax.div(e, degree), lax.rem(e, degree)]
        peer = lax.rem(lax.div(partner, views), members)
        there = mirror(lax.div(peer, ROW))
        inside = jnp.where(there == 0, 1, jnp.where(there == 2, 0, 2))
        turn = jnp.where(here == 0, there - 1, inside)
        across = (lax.rem(peer, ROW) != side).astype(jnp.int32)
        block = jnp.where(there == here, 0, 1 + 2 * turn + across)
        live = lax.rem(e, degree) < counts[lax.div(e, degree)]
        codes[0, e] = jnp.where(live, block * views + lax.rem(partner, views), 0)
        return carry

    lax.fori_loop(0, entries, read, 0)

    def mark(cell, carry):
        found = jnp.int32(0)
        for e in range(entries):
            found = jnp.where(codes[0, e] == cell, 1, found)
        ask[0, cell] = found
        return carry

    lax.fori_loop(0, cells, mark, 0)
    own[0] = layer_norm(tokens[0]).astype(jnp.bfloat16)

    @pl.when(is_mid)
    def _():
        pl.semaphore_wait(barrier, 5)

    @pl.when(is_end)
    def _():
        pl.semaphore_wait(barrier, 4)

    ask_send().start()
    for v in range(views):
        if v:
            own[v] = layer_norm(tokens[v]).astype(jnp.bfloat16)
        to_near(v).start()

        @pl.when(is_end)
        def _():
            own_to_b1(v).start()

        @pl.when(is_mid)
        def _():
            own_to_b0(v).start()
            if v == 0:
                own_out().start()

    key_out[...] = own[key_view]
    count = 3 * views

    def same(ref, c):
        return ref[0, (1 + 2 * (c // views)) * views + c % views]

    def cross(ref, c):
        return ref[0, (2 + 2 * (c // views)) * views + c % views]

    ask_send().wait_recv()

    @pl.when(is_end)
    def _():
        for c in range(count):
            union[0, c] = jnp.maximum(same(ask, c), cross(asked, c))
        union_send().start()

    loads[0].wait()
    for v in range(views):
        queries[v] = project(own[v], w_query[...]).astype(jnp.bfloat16) * jnp.bfloat16(size**-0.5)
    for i in range(2):
        key_send(i).start()

    @pl.when(is_mid)
    def _():
        union_send().wait_recv()

    def line_up(flags, ready):
        spots, last = [], jnp.int32(-1)
        for flag, at in zip(flags, ready):
            spot = jnp.maximum(last + 1, at)
            spots.append(spot)
            last = jnp.where(flag == 1, spot, last)
        return spots, last

    far_ready = [0] * views + [v + 1 for v in range(views)] + [v + 1 + views for v in range(views)]

    def far_slots(flags):
        spots, last = line_up(flags[1:], far_ready[1:])
        return [jnp.int32(-1)] + spots, last

    def wide_slots(flags, behind):
        ready = []
        for c in range(count):
            late = 0 if c < 2 * views else c - 2 * views + 1
            ready.append(jnp.where(is_end, jnp.maximum(behind[c] - 2, 0), late))
        return line_up(flags, ready)

    def found(c, spots):
        return jnp.where(is_end, FREE if c == 0 else SLOTS + spots[c], PLAIN + c)

    mine = [union[0, c] for c in range(count)]
    my_far, far_last = far_slots(mine)
    beside_far, _ = far_slots([jnp.maximum(same(asked, c), cross(ask, c)) for c in range(count)])
    out_flags = [cross(asked, c) for c in range(count)]
    my_wide, out_last = wide_slots(out_flags, my_far)
    beside_wide, in_last = wide_slots([cross(ask, c) for c in range(count)], beside_far)
    for q in range(FAR):
        pick = jnp.int32(0)
        for c in range(1, count):
            pick = jnp.where((mine[c] == 1) & (my_far[c] == q), c, pick)
        picks[0, q] = pick
    for k in range(WIDE):
        pick = jnp.where(is_end, FREE, PLAIN)
        for c in range(count):
            pick = jnp.where((out_flags[c] == 1) & (my_wide[c] == k), found(c, my_far), pick)
        picks[0, FAR + k] = pick
    for v in range(views):
        sources[0, v] = v
    for c in range(count):
        sources[0, (1 + 2 * (c // views)) * views + c % views] = found(c, my_far)
        sources[0, (2 + 2 * (c // views)) * views + c % views] = CROSS + beside_wide[c]
    full = (far_last >= FAR) | (out_last >= WIDE) | (in_last >= WIDE)
    notes[0][0, 0] = full.astype(jnp.int32)

    def choose(choice, options):
        value = None
        for key, load in options:
            value = load() if value is None else jnp.where(choice == key, load(), value)
        return value

    def far_stage(q):
        options = [(c, functools.partial(own.__getitem__, c)) for c in range(min(views, q + views))]
        options += [(views + v, functools.partial(b0.__getitem__, v)) for v in range(views) if v < q]
        options += [
            (2 * views + v, functools.partial(b2.__getitem__, v)) for v in range(views) if v + views < q
        ]
        far_out[q] = choose(picks[0, q], options)
        far_send(q).start()

    def far_turn(q):
        @pl.when(is_mid)
        def _():
            if 1 <= q <= views:
                own_to_b0(q - 1).wait_recv()
                own_to_b1(q - 1).wait_recv()
                b1_in(q - 1).start()
            if q > views:
                b1_in(q - 1 - views).wait_recv()
            far_stage(q)

    def wide_stage(k):
        choice = picks[0, FAR + k]

        @pl.when(is_end)
        def _():
            options = [(FREE, lambda: first_view[...])]
            options += [(SLOTS + q, functools.partial(far.__getitem__, q)) for q in range(k + 3)]
            wide_out[k] = choose(choice, options)

        @pl.when(is_mid)
        def _():
            options = [(PLAIN + v, functools.partial(b0.__getitem__, v)) for v in range(views)]
            options += [(PLAIN + views + v, functools.partial(b1.__getitem__, v)) for v in range(views)]
            options += [
                (PLAIN + 2 * views + v, functools.partial(b2.__getitem__, v))
                for v in range(views)
                if v < k
            ]
            wide_out[k] = choose(choice, options)

        wide_send(k).start()

    def far_arrive(q):
        @pl.when(is_end)
        def _():
            far_send(q).wait_recv()

    def wide_turn(k):
        far_arrive(k + 2)
        wide_stage(k)

    def note_value(i, value):
        notes[2 * i][0, 0] = value

    def seen(i):
        return notes[2 * i + 1][0, 0]

    rounds = groups // 2

    def note_step(i):
        if i == 0:
            note(0, beside).start()
        if i == 1:
            note(0, beside).wait_recv()
            note_value(1, jnp.maximum(notes[0][0, 0], seen(0)))

            @pl.when(is_end)
            def _():
                note(1, inner).start()
        if i == 2:
            @pl.when(is_mid)
            def _():
                note(1, inner).wait_recv()
                note_value(2, jnp.maximum(notes[2][0, 0], seen(1)))
                note(2, inner).start()
        if i == 3:
            @pl.when(is_mid)
            def _():
                note(2, inner).wait_recv()
                note_value(3, jnp.maximum(notes[4][0, 0], seen(2)))
                note(3, outer).start()
                note_value(4, notes[6][0, 0])
        if i == 4:
            @pl.when(is_end)
            def _():
                note(3, outer).wait_recv()
                note_value(4, seen(3))

            note_value(5, notes[8][0, 0])
            note(4, above).start()
            note(5, below).start()
        if i > 4:
            j = 2 * i - 6
            note(j, above).wait_recv()
            note(j + 1, below).wait_recv()
            value = jnp.maximum(notes[2 * j][0, 0], jnp.maximum(seen(j), seen(j + 1)))
            if i < 4 + rounds:
                note_value(j + 2, value)
                note_value(j + 3, value)
                note(j + 2, above).start()
                note(j + 3, below).start()
            else:
                flag_ref[0, 0] = value

    far_turn(0)
    note_step(0)

    def rank(e, carry):
        code = codes[0, e] * entries + e
        position = jnp.int32(2)
        for other in range(entries):
            position = position + (codes[0, other] * entries + other < code).astype(jnp.int32)
        table[0, e] = position
        return carry

    lax.fori_loop(0, entries, rank, 0)

    def sort(r, carry):
        cell, view = jnp.int32(0), key_view
        for e in range(entries):
            match = table[0, e] == r
            cell = jnp.where(match, codes[0, e], cell)
            view = jnp.where(match, e // degree, view)
        table[1, r], table[2, r] = sources[0, cell], view
        return carry

    lax.fori_loop(0, entries + 2, sort, 0)
    loads[1].wait()
    loads[2].wait()
    for i in range(2):
        key_send(i).wait_recv()

    late = [2 + max(0, entries - n) for n in (15, 12, 9, 7, 3)]
    turns = {
        1: [lambda: far_turn(1), lambda: note_step(1)],
        2: [lambda: far_turn(2), lambda: far_turn(3), lambda: far_turn(4)]
        + [functools.partial(far_arrive, q) for q in range(2)],
        late[0]: [lambda: far_turn(5), lambda: wide_turn(1), lambda: far_turn(6)]
        + [lambda: wide_turn(2), lambda: note_step(3)],
        late[1]: [lambda: far_turn(8), lambda: wide_turn(4), lambda: note_step(4)],
        late[2]: [lambda: wide_turn(5), lambda: note_step(5)],
        late[3]: [lambda: wide_turn(6), lambda: note_step(6)],
        late[4]: [],
    }

    def events(t):
        for turn in turns[t]:
            turn()
        if t == 2:
            @pl.when(is_end)
            def _():
                own_out().wait_recv()

            for v in range(views):
                to_near(v).wait_recv()
            wide_turn(0)
            note_step(2)
        if t == late[0]:
            for k in range(3):
                wide_send(k).wait_recv()
            far_turn(7)
            wide_turn(3)
        if t == late[2]:
            wide_send(3).wait_recv()
            wide_send(4).wait_recv()
        if t == late[3]:
            wide_send(5).wait_recv()
        if t == late[4]:
            wide_send(6).wait_recv()

    def entry(t, carry):
        for when in turns:
            @pl.when(t == when)
            def _():
                events(when)

        source, view = table[1, t], table[2, t]

        def take(condition, key, load):
            @pl.when(condition)
            def _():
                cur[...] = jnp.where(source == key, load(), cur[...])

        def take_any(condition, start, ref):
            spot = source - start
            held = ref.shape[0]

            @pl.when(condition)
            def _():
                value = ref[jnp.clip(spot, 0, held - 1)]
                cur[...] = jnp.where((spot >= 0) & (spot < held), value, cur[...])

        @pl.when(t < 2)
        def _():
            cur[...] = keys[jnp.minimum(t, 1)]

        take_any(t >= 2, 0, near)
        for j, ref in enumerate((b0, b1)):
            take_any((t >= 2) & is_mid, PLAIN + j * views, ref)
        take_any((t >= late[1]) & is_mid, PLAIN + 2 * views, b2)
        take((t >= 2) & is_end, FREE, lambda: first_view[...])
        for q in range(FAR - 2):
            since = 2 if q < 3 else late[1]
            take(
                (t >= since) & (t < late[3]) & is_end, SLOTS + q,
                functools.partial(far.__getitem__, q),
            )
        take_any((t >= late[3]) & is_end, SLOTS, far)
        for k in range(WIDE - 1):
            since = late[0] if k < 3 else (late[2] if k < 5 else late[3])
            take((t >= since) & (t < late[4]), CROSS + k, functools.partial(wide.__getitem__, k))
        take_any(t >= late[4], CROSS, wide)

        def store(cols, value):
            results[t, :, cols] = value

        attend(lambda cols: queries[view, :, cols], cur[...], w_key, w_value, pair, store)
        return carry

    lax.fori_loop(0, entries + 2, entry, 0)
    loads[3].wait()
    for v in range(views):
        is_key = (key_view == v).astype(jnp.int32)
        total = counts[v]
        mixed = is_key.astype(jnp.float32) * (results[0] + results[1])
        for e in range(degree):
            live = (total > e).astype(jnp.int32).astype(jnp.float32)
            mixed += live * results[table[0, v * degree + e]]
        divisor = jnp.full((1, features), total + 2 * is_key, jnp.int32).astype(jnp.float32)
        mixed = mixed * (1.0 / divisor)
        out_ref[v] = (
            tokens[v].astype(jnp.float32) + project(mixed.astype(jnp.bfloat16), w_out[...])
        ).astype(out_ref.dtype)

    for v in range(views):
        to_near(v).wait_send()

        @pl.when(is_end)
        def _():
            own_to_b1(v).wait_send()

        @pl.when(is_mid)
        def _():
            own_to_b0(v).wait_send()
            b1_in(v).wait_send()

    @pl.when(is_mid)
    def _():
        own_out().wait_send()
        for q in range(FAR):
            far_send(q).wait_send()
        note(2, inner).wait_send()
        note(3, outer).wait_send()

    @pl.when(is_end)
    def _():
        union_send().wait_send()
        note(1, inner).wait_send()

    for k in range(WIDE):
        wide_send(k).wait_send()
    for i in range(2):
        key_send(i).wait_send()
    ask_send().wait_send()
    note(0, beside).wait_send()
    for i in range(4, 4 + 2 * rounds):
        note(i, above if i % 2 == 0 else below).wait_send()


def quick(tokens, w_query, w_key, w_value, w_out, partners, counts, key_slot):
    views, length, features = tokens.shape
    degree = partners.shape[1]
    entries = views * degree
    rounds = lax.axis_size("group") // 2
    smem = pl.BlockSpec(memory_space=pltpu.SMEM)
    hbm = pl.BlockSpec(memory_space=pltpu.HBM)
    vmem = pl.BlockSpec(memory_space=pltpu.VMEM)
    stay = [
        pltpu.with_memory_space_constraint(w, pltpu.HBM) for w in (w_query, w_key, w_value, w_out)
    ]
    slab = (length, features)
    half = jnp.bfloat16

    def slabs(count):
        return pltpu.VMEM((count, *slab), half)

    def numbers(*shape):
        return pltpu.SMEM(shape, jnp.int32)

    return pl.pallas_call(
        functools.partial(quick_kernel, degree),
        out_shape=(
            jax.ShapeDtypeStruct(tokens.shape, tokens.dtype),
            jax.ShapeDtypeStruct((1, 1), jnp.int32),
        ),
        in_specs=[smem] * 3 + [vmem] + [hbm] * 4,
        out_specs=(vmem, smem),
        scratch_shapes=[
            *[pltpu.VMEM((features, features), half)] * 4,
            *[slabs(views)] * 6,
            pltpu.VMEM(slab, half),
            slabs(FAR),
            slabs(WIDE),
            slabs(2),
            slabs(FAR),
            slabs(WIDE),
            pltpu.VMEM(slab, half),
            numbers(1, 7 * views),
            numbers(1, 7 * views),
            numbers(1, 3 * views),
            numbers(1, entries),
            numbers(1, 7 * views),
            numbers(1, FAR + WIDE),
            numbers(3, entries + 2),
            pltpu.VMEM(slab, half),
            pltpu.VMEM((length, 2 * features), half),
            pltpu.VMEM((entries + 2, *slab), jnp.float32),
            pltpu.SemaphoreType.DMA((4,)),
            pltpu.SemaphoreType.DMA((5 * views + FAR + WIDE + 16,)),
            pltpu.SemaphoreType.DMA((5 * views + FAR + WIDE + 16,)),
            *[numbers(1, 1)] * (2 * (4 + 2 * rounds)),
        ],
        compiler_params=pltpu.CompilerParams(
            collective_id=1, has_side_effects=True, vmem_limit_bytes=48 * 1024 * 1024
        ),
        name="sublayer_quick",
    )(partners, counts, key_slot, tokens, *stay)


def select_kernel(*arguments):
    result, flag = quick(*arguments)
    return lax.cond(flag[0, 0] > 0, lambda: one_kernel(*arguments), lambda: result)


def local_kernel(table, queries, w_key, w_value, block, inverse, tokens, w_out, out_ref, *scratch):
    held, pair, total, sem = scratch
    copy = pltpu.make_async_copy(block, held, sem)
    copy.start()
    total[...] = jnp.zeros_like(total)
    copy.wait()
    views, length, _ = total.shape

    def entry(e, carry):
        @pl.when(table[0, e] == 1)
        def _():
            place, view = table[1, e], table[2, e]

            def store(cols, value):
                total[view, :, cols] += value

            normed = layer_norm(held[place]).astype(jnp.bfloat16)
            attend(lambda cols: queries[view, :, cols], normed, w_key, w_value, pair, store)

        return carry

    lax.fori_loop(0, table.shape[1], entry, 0)
    for v in range(views):
        mixed = (total[v] * inverse[v]).astype(jnp.bfloat16)
        out_ref[v] = (tokens[v].astype(jnp.float32) + project(mixed, w_out[...])).astype(out_ref.dtype)


def exchange(tokens, w_query, w_key, w_value, w_out, partners, counts, key_slot):
    slot_key = key_slot[0]
    views, length, features = tokens.shape
    members, groups = lax.axis_size("member"), lax.axis_size("group")
    degree = partners.shape[1]
    entry_list = partners.reshape(-1)
    entries = entry_list.shape[0]
    capacity = (entries + members - 2) // (members - 1)
    peers = entry_list // views % members
    places = entry_list % views
    order = jnp.arange(entries, dtype=jnp.int32)
    earlier = (peers[:, None] == peers[None, :]) & (order[None, :] < order[:, None])
    cells = peers * capacity + jnp.sum(earlier.astype(jnp.int32), axis=1)
    requests = jnp.zeros((members * capacity,), jnp.int32).at[cells].set(places)
    asked = lax.all_to_all(
        requests.reshape(members, capacity), "member", split_axis=0, concat_axis=0, tiled=True
    )
    outgoing = tokens[asked.reshape(-1)].reshape(members, capacity, length, features)
    arrived = lax.all_to_all(outgoing, "member", split_axis=0, concat_axis=0, tiled=True)
    own_key = lax.dynamic_slice_in_dim(tokens, slot_key, 1, 0)
    below = lax.ppermute(own_key, "group", [(g, (g + 1) % groups) for g in range(groups)])
    above = lax.ppermute(own_key, "group", [((g + 1) % groups, g) for g in range(groups)])
    block = jnp.concatenate((arrived.reshape(members * capacity, length, features), below, above))
    normed = layer_norm(tokens).astype(jnp.bfloat16)
    queries = project(normed.reshape(views * length, features), w_query).astype(jnp.bfloat16)
    queries = queries.reshape(tokens.shape) * jnp.bfloat16((features // HEADS) ** -0.5)
    is_key = (jnp.arange(views, dtype=jnp.int32) == slot_key).astype(jnp.int32)
    inverse = 1.0 / (counts + 2 * is_key).astype(jnp.float32)
    live = (jnp.arange(degree, dtype=jnp.int32)[None, :] < counts[:, None]).reshape(-1)
    two = jnp.arange(2, dtype=jnp.int32)
    table = jnp.stack(
        (
            jnp.concatenate((live.astype(jnp.int32), jnp.ones_like(two))),
            jnp.concatenate((cells, members * capacity + two)),
            jnp.concatenate((order // degree, jnp.full_like(two, slot_key))),
        )
    )
    vmem = pl.BlockSpec(memory_space=pltpu.VMEM)
    smem = pl.BlockSpec(memory_space=pltpu.SMEM)
    hbm = pl.BlockSpec(memory_space=pl.ANY)
    return pl.pallas_call(
        local_kernel,
        out_shape=jax.ShapeDtypeStruct(tokens.shape, tokens.dtype),
        in_specs=[smem, vmem, vmem, vmem, hbm, smem, vmem, vmem],
        out_specs=vmem,
        scratch_shapes=[
            pltpu.VMEM(block.shape, block.dtype),
            pltpu.VMEM((length, 2 * features), jnp.bfloat16),
            pltpu.VMEM(tokens.shape, jnp.float32),
            pltpu.SemaphoreType.DMA,
        ],
        compiler_params=pltpu.CompilerParams(vmem_limit_bytes=60 * 1024 * 1024),
        name="attend_all",
    )(table, queries, w_key, w_value, block, inverse, tokens, w_out)


def sublayer(tokens, w_query, w_key, w_value, w_out, partners, counts, key_slot):
    views = tokens.shape[0]
    members = lax.axis_size("member")
    entries = partners.shape[0] * partners.shape[1]
    capacity = (entries + members - 2) // (members - 1)
    grid = members == LAYERS * ROW and views == capacity + 1
    run = select_kernel if grid else exchange
    return run(tokens, w_query, w_key, w_value, w_out, partners, counts, key_slot)


def solution(mesh):
    return jax.shard_map(
        sublayer,
        mesh=mesh,
        in_specs=(
            P(("group", "member"), None, None),
            P(),
            P(),
            P(),
            P(),
            P(("group", "member"), None),
            P(("group", "member")),
            P(("group", "member")),
        ),
        out_specs=P(("group", "member"), None, None),
        check_vma=False,
    )
```

```python
import functools

import jax
import jax.numpy as jnp
from jax import lax
from jax.experimental import pallas as pl
from jax.experimental.pallas import tpu as pltpu
from jax.sharding import PartitionSpec as P

HEADS = 12
ROW = 2
LAYERS = 4
MESH = pl.DeviceIdType.MESH


def layer_norm(values_in):
    values_in = values_in.astype(jnp.float32)
    centre = jnp.mean(values_in, axis=-1, keepdims=True)
    spread = jnp.mean((values_in - centre) ** 2, axis=-1, keepdims=True)
    return (values_in - centre) * lax.rsqrt(spread + 1e-05)


def project(rows, weights):
    return jnp.dot(rows, weights, preferred_element_type=jnp.float32)


def attend(query, normed, w_key, w_value, pair, store):
    features = normed.shape[1]
    size = features // HEADS
    lower = lax.broadcasted_iota(jnp.int32, (1, 2 * size), 1) < size
    pair[:, :features] = project(normed, w_key[...]).astype(jnp.bfloat16)
    pair[:, features:] = project(normed, w_value[...]).astype(jnp.bfloat16)
    for h in range(HEADS // 2):
        cols = pl.ds(2 * h * size, 2 * size)
        rows = query(cols)
        key = pair[:, cols]
        value = pair[:, pl.ds(features + 2 * h * size, 2 * size)]
        halves = []
        for keep in (lower, jnp.logical_not(lower)):
            part = jnp.where(keep, rows, jnp.zeros_like(rows))
            scores = lax.dot_general(
                part, key, (((1,), (1,)), ((), ())), preferred_element_type=jnp.float32
            )
            top = jnp.max(scores, axis=-1, keepdims=True)
            weights = jnp.exp(scores - top)
            mass = jnp.sum(weights, axis=-1, keepdims=True)
            halves.append(project(weights.astype(jnp.bfloat16), value) / mass)
        store(cols, jnp.where(lower, halves[0], halves[1]))


RAW_BLOCK, RAW_PLACE, POSITION, BLOCK, PLACE, VIEW = range(6)


def build_tables(layer, side, degree, capacity, views, members, partners, key_view, ask, table):
    entries = views * degree
    low = layer < LAYERS // 2

    def mirror(value):
        return jnp.where(low, value, LAYERS - 1 - value)

    here = mirror(layer)

    def read(e, flags):
        partner = partners[lax.div(e, degree), lax.rem(e, degree)]
        peer = lax.rem(lax.div(partner, views), members)
        place = lax.rem(partner, views)
        there = mirror(lax.div(peer, ROW))
        inside = jnp.where(there == 0, 1, jnp.where(there == 2, 0, 2))
        turn = jnp.where(here == 0, there - 1, inside)
        across = (lax.rem(peer, ROW) != side).astype(jnp.int32)
        block = jnp.where(there == here, 0, 1 + 2 * turn + across)
        table[RAW_BLOCK, e] = block
        table[RAW_PLACE, e] = place
        return tuple(
            jnp.where((block == 2 + 2 * (i // views)) & (place == i % views), 1, flag)
            for i, flag in enumerate(flags)
        )

    flags = lax.fori_loop(0, entries, read, (jnp.int32(0),) * (3 * views))
    slots = []
    for j in range(3):
        wanted = flags[j * views : (j + 1) * views]
        slot = capacity - sum(wanted)
        for v in range(views):
            slots.append(slot)
            slot = slot + wanted[v]
        for k in range(capacity):
            ask[0, j * capacity + k] = sum(
                jnp.where((wanted[v] == 1) & (slots[j * views + v] == k), v, 0) for v in range(views)
            )

    def rank(e, carry):
        block, place = table[RAW_BLOCK, e], table[RAW_PLACE, e]
        position = jnp.int32(2)
        for other in range(entries):
            ahead = (table[RAW_BLOCK, other] * entries + other) < block * entries + e
            position = position + ahead.astype(jnp.int32)
        table[POSITION, e] = position
        spot = place
        for i, slot in enumerate(slots):
            spot = jnp.where((block == 2 + 2 * (i // views)) & (place == i % views), slot, spot)
        table[RAW_PLACE, e] = spot
        return carry

    lax.fori_loop(0, entries, rank, 0)

    def sort(r, carry):
        block, place, view = jnp.int32(-1), jnp.int32(0), key_view
        for e in range(entries):
            match = table[POSITION, e] == r
            block = jnp.where(match, table[RAW_BLOCK, e], block)
            place = jnp.where(match, table[RAW_PLACE, e], place)
            view = jnp.where(match, e // degree, view)
        table[BLOCK, r], table[PLACE, r], table[VIEW, r] = block, place, view
        return carry

    lax.fori_loop(0, entries + 2, sort, 0)


def sublayer_kernel(degree, capacity, *refs):
    partners, counts, key_slot, tokens, wq_in, wk_in, wv_in, wo_in, out_ref = refs[:9]
    w_query, w_key, w_value, w_out = refs[9:13]
    own, queries, near, b0, b1, b2, s0, s1, s2, keys, staged, key_out = refs[13:25]
    ask, asked, table, cur, pair, results, load_sem, send_sem, recv_sem = refs[25:]
    views, length, features = tokens.shape
    members, groups = lax.axis_size("member"), lax.axis_size("group")
    entries = views * degree
    peers = members - 1
    size = features // HEADS
    me, group = lax.axis_index("member"), lax.axis_index("group")
    layer, side = me // ROW, me % ROW
    low = layer < LAYERS // 2
    toward = jnp.where(low, ROW, -ROW)
    is_end = jnp.logical_or(layer == 0, layer == LAYERS - 1)
    is_mid = jnp.logical_not(is_end)
    beside = {"member": layer * ROW + 1 - side}
    inner = {"member": me + toward}
    outer = {"member": jnp.clip(me - toward, 0, members - 1)}
    above = {"group": lax.rem(group + 1, groups)}
    below = {"group": lax.rem(group + groups - 1, groups)}

    blocks = (near, b0, s0, b1, s1, b2, s2)
    base, total = {}, 0
    for name, ref in (("near", near), ("b0", b0), ("b1", b1), ("b2", b2), ("s0", s0),
                      ("s1", s1), ("s2", s2), ("keys", keys)):
        base[name] = total
        total += ref.shape[0]

    def remote(source, target, send, recv, device):
        return pltpu.make_async_remote_copy(
            src_ref=source, dst_ref=target, send_sem=send_sem.at[send],
            recv_sem=recv_sem.at[recv], device_id=device, device_id_type=MESH,
        )

    sends = {}

    def slot(name, index):
        return sends.setdefault((name, index), len(sends))

    def hop(name, source, v, target, target_name, device):
        return remote(source.at[v], target.at[v], slot(name, v), base[target_name] + v, device)

    def to_near(v):
        return hop("near", own, v, near, "near", beside)

    def own_to_b1(v):
        return hop("in", own, v, b1, "b1", inner)

    def own_to_b0(v):
        return hop("in", own, v, b0, "b0", inner)

    def own_out(v):
        return hop("out", own, v, b0, "b0", outer)

    def b1_in(v):
        return hop("in2", b1, v, b2, "b2", inner)

    def b0_out(v):
        return hop("out1", b0, v, b1, "b1", outer)

    def b2_out(v):
        return hop("out2", b2, v, b2, "b2", outer)

    swaps = (s0, s1, s2)

    def swap(j, k):
        return remote(
            staged.at[j * capacity + k], swaps[j].at[k], slot("swap", j * capacity + k),
            base[f"s{j}"] + k, beside,
        )

    def key_send(i):
        return remote(
            key_out, keys.at[i], slot("key", i), base["keys"] + i, above if i == 0 else below
        )

    def ask_send():
        return remote(ask, asked, slot("ask", 0), total, beside)

    loads = [
        pltpu.make_async_copy(source, target, load_sem.at[i])
        for i, (source, target) in enumerate(
            ((wq_in, w_query), (wk_in, w_key), (wv_in, w_value), (wo_in, w_out))
        )
    ]
    for load in loads:
        load.start()

    barrier = pltpu.get_barrier_semaphore()
    for device in (beside, inner, above, below):
        pl.semaphore_signal(barrier, inc=1, device_id=device, device_id_type=MESH)

    @pl.when(is_mid)
    def _():
        pl.semaphore_signal(barrier, inc=1, device_id=outer, device_id_type=MESH)

    own[0] = layer_norm(tokens[0]).astype(jnp.bfloat16)

    @pl.when(is_mid)
    def _():
        pl.semaphore_wait(barrier, 5)

    @pl.when(is_end)
    def _():
        pl.semaphore_wait(barrier, 4)

    for v in range(views):
        if v:
            own[v] = layer_norm(tokens[v]).astype(jnp.bfloat16)
        to_near(v).start()

        @pl.when(is_end)
        def _():
            own_to_b1(v).start()

        @pl.when(is_mid)
        def _():
            own_to_b0(v).start()
            own_out(v).start()

    key_view = key_slot[0]
    key_out[...] = own[key_view]
    loads[0].wait()
    for v in range(views):
        queries[v] = project(own[v], w_query[...]).astype(jnp.bfloat16) * jnp.bfloat16(size**-0.5)
    for i in range(2):
        key_send(i).start()
    build_tables(layer, side, degree, capacity, views, members, partners, key_view, ask, table)
    ask_send().start()
    loads[1].wait()
    loads[2].wait()
    for i in range(2):
        key_send(i).wait_recv()

    def stage(j, k, source):
        choice = asked[0, j * capacity + k]
        value = source[0]
        for v in range(1, k + views - capacity + 1):
            value = jnp.where(choice == v, source[v], value)
        staged[j * capacity + k] = value
        swap(j, k).start()

    def events(t):
        def far(v):
            @pl.when(is_end)
            def _():
                b0_out(v).wait_recv()

            @pl.when(is_mid)
            def _():
                b1_in(v).wait_recv()
                b2_out(v).start()

        def last(v):
            @pl.when(is_end)
            def _():
                b2_out(v).wait_recv()

        def arrive(j):
            for k in range(capacity):
                swap(j, k).wait_recv()

        extra = views - capacity

        def spread(wait, j, source, v):
            wait(v)
            if v >= extra:
                stage(j, v - extra, source)

        if t == first[0]:
            for v in range(views):
                own_to_b0(v).wait_recv()

                @pl.when(is_mid)
                def _():
                    b0_out(v).start()
                    own_to_b1(v).wait_recv()
                    b1_in(v).start()

                if v >= extra:
                    stage(0, v - extra, b0)
            for v in range(views):
                to_near(v).wait_recv()
        if t == first[2]:
            for v in range(views - 2):
                spread(far, 1, b1, v)
            arrive(0)
        if t == first[2] + 1:
            spread(far, 1, b1, views - 2)
        if t == first[3]:
            spread(far, 1, b1, views - 1)
        if t == first[4]:
            for v in range(views - 2):
                spread(last, 2, b2, v)
            arrive(1)
        if t == first[4] + 1:
            spread(last, 2, b2, views - 2)
        if t == first[5]:
            spread(last, 2, b2, views - 1)
        if t == first[6]:
            arrive(2)

    first = [2 + max(0, entries - capacity * (peers - j)) for j in range(peers)]

    def entry(t, carry):
        for when in sorted({first[0], first[2], first[2] + 1, first[3], first[4], first[4] + 1,
                            first[5], first[6]}):
            @pl.when(t == when)
            def _():
                events(when)

        @pl.when(t < 2)
        def _():
            cur[...] = keys[jnp.minimum(t, 1)]

        block, place, view = table[BLOCK, t], table[PLACE, t], table[VIEW, t]
        for j, ref in enumerate(blocks):
            @pl.when(t >= first[j])
            def _():
                value = ref[jnp.minimum(place, ref.shape[0] - 1)]
                cur[...] = jnp.where(block == j, value, cur[...])

        def store(cols, value):
            results[t, :, cols] = value

        attend(lambda cols: queries[view, :, cols], cur[...], w_key, w_value, pair, store)
        return carry

    ask_send().wait_recv()
    lax.fori_loop(0, entries + 2, entry, 0)
    loads[3].wait()
    for v in range(views):
        is_key = (key_view == v).astype(jnp.int32)
        count = counts[v]
        mixed = is_key.astype(jnp.float32) * (results[0] + results[1])
        for e in range(degree):
            live = (count > e).astype(jnp.int32).astype(jnp.float32)
            mixed += live * results[table[POSITION, v * degree + e]]
        divisor = jnp.full((1, features), count + 2 * is_key, jnp.int32).astype(jnp.float32)
        mixed = mixed * (1.0 / divisor)
        out_ref[v] = (
            tokens[v].astype(jnp.float32) + project(mixed.astype(jnp.bfloat16), w_out[...])
        ).astype(out_ref.dtype)

    for v in range(views):
        to_near(v).wait_send()

        @pl.when(is_end)
        def _():
            own_to_b1(v).wait_send()

        @pl.when(is_mid)
        def _():
            own_to_b0(v).wait_send()
            own_out(v).wait_send()
            b1_in(v).wait_send()
            b0_out(v).wait_send()
            b2_out(v).wait_send()

    for j in range(3):
        for k in range(capacity):
            swap(j, k).wait_send()
    for i in range(2):
        key_send(i).wait_send()
    ask_send().wait_send()


def one_kernel(tokens, w_query, w_key, w_value, w_out, partners, counts, key_slot):
    views, length, features = tokens.shape
    members = lax.axis_size("member")
    degree = partners.shape[1]
    entries = views * degree
    capacity = (entries + members - 2) // (members - 1)
    smem = pl.BlockSpec(memory_space=pltpu.SMEM)
    hbm = pl.BlockSpec(memory_space=pltpu.HBM)
    vmem = pl.BlockSpec(memory_space=pltpu.VMEM)
    stay = [
        pltpu.with_memory_space_constraint(w, pltpu.HBM) for w in (w_query, w_key, w_value, w_out)
    ]
    slab = (length, features)
    weights_shape = pltpu.VMEM((features, features), jnp.bfloat16)
    half = jnp.bfloat16
    blocks = [pltpu.VMEM((views, *slab), half)] * 6 + [pltpu.VMEM((capacity, *slab), half)] * 3
    sends = 6 * views + 3 * capacity + 3 + views
    receives = 4 * views + 3 * capacity + 3
    return pl.pallas_call(
        functools.partial(sublayer_kernel, degree, capacity),
        out_shape=jax.ShapeDtypeStruct(tokens.shape, tokens.dtype),
        in_specs=[smem] * 3 + [vmem] + [hbm] * 4,
        out_specs=vmem,
        scratch_shapes=[
            weights_shape,
            weights_shape,
            weights_shape,
            weights_shape,
            *blocks,
            pltpu.VMEM((2, *slab), half),
            pltpu.VMEM((3 * capacity, *slab), half),
            pltpu.VMEM(slab, half),
            pltpu.SMEM((1, 3 * capacity), jnp.int32),
            pltpu.SMEM((1, 3 * capacity), jnp.int32),
            pltpu.SMEM((6, entries + 2), jnp.int32),
            pltpu.VMEM(slab, half),
            pltpu.VMEM((length, 2 * features), half),
            pltpu.VMEM((entries + 2, *slab), jnp.float32),
            pltpu.SemaphoreType.DMA((4,)),
            pltpu.SemaphoreType.DMA((sends,)),
            pltpu.SemaphoreType.DMA((receives,)),
        ],
        compiler_params=pltpu.CompilerParams(
            collective_id=0, has_side_effects=True, vmem_limit_bytes=44 * 1024 * 1024
        ),
        name="sublayer",
    )(partners, counts, key_slot, tokens, *stay)


FAR, WIDE = 9, 7
FREE, SLOTS, CROSS, PLAIN = 4, 5, 5 + FAR, 5 + FAR + WIDE


def quick_kernel(degree, *refs):
    partners, counts, key_slot, tokens, wq_in, wk_in, wv_in, wo_in, out_ref, flag_ref = refs[:10]
    w_query, w_key, w_value, w_out = refs[10:14]
    own, queries, near, b0, b1, b2, first_view, far, wide, keys, far_out, wide_out, key_out = refs[14:27]
    ask, asked, union, codes, sources, picks, table, cur, pair, results = refs[27:37]
    load_sem, send_sem, recv_sem = refs[37:40]
    notes = refs[40:]
    views, length, features = tokens.shape
    members, groups = lax.axis_size("member"), lax.axis_size("group")
    entries = views * degree
    size = features // HEADS
    me, group = lax.axis_index("member"), lax.axis_index("group")
    layer, side = me // ROW, me % ROW
    low = layer < LAYERS // 2
    toward = jnp.where(low, ROW, -ROW)
    is_end = jnp.logical_or(layer == 0, layer == LAYERS - 1)
    is_mid = jnp.logical_not(is_end)
    beside = {"member": layer * ROW + 1 - side}
    inner = {"member": me + toward}
    outer = {"member": jnp.clip(me - toward, 0, members - 1)}
    above = {"group": lax.rem(group + 1, groups)}
    below = {"group": lax.rem(group + groups - 1, groups)}
    key_view = key_slot[0]
    cells = 7 * views
    names = {}

    def number(kind, name):
        return names.setdefault((kind, name), sum(1 for k, _ in names if k == kind))

    def remote(name, source, target, landing, device):
        return pltpu.make_async_remote_copy(
            src_ref=source, dst_ref=target, send_sem=send_sem.at[number(0, name)],
            recv_sem=recv_sem.at[number(1, landing)], device_id=device, device_id_type=MESH,
        )

    def to_near(v):
        return remote(("near", v), own.at[v], near.at[v], ("near", v), beside)

    def own_to_b1(v):
        return remote(("in", v), own.at[v], b1.at[v], ("b1", v), inner)

    def own_to_b0(v):
        return remote(("in", v), own.at[v], b0.at[v], ("b0", v), inner)

    def b1_in(v):
        return remote(("in2", v), b1.at[v], b2.at[v], ("b2", v), inner)

    def own_out():
        return remote("free", own.at[0], first_view, "free", outer)

    def far_send(q):
        return remote(("far", q), far_out.at[q], far.at[q], ("far", q), outer)

    def wide_send(k):
        return remote(("wide", k), wide_out.at[k], wide.at[k], ("wide", k), beside)

    def key_send(i):
        return remote(("key", i), key_out, keys.at[i], ("key", i), below if i else above)

    def ask_send():
        return remote("ask", ask, asked, "ask", beside)

    def union_send():
        return remote("union", union, union, "union", inner)

    def note(i, device):
        return remote(("note", i), notes[2 * i], notes[2 * i + 1], ("note", i), device)

    loads = [
        pltpu.make_async_copy(source, target, load_sem.at[i])
        for i, (source, target) in enumerate(
            ((wq_in, w_query), (wk_in, w_key), (wv_in, w_value), (wo_in, w_out))
        )
    ]
    for load in loads:
        load.start()
    barrier = pltpu.get_barrier_semaphore()
    for device in (beside, inner, above, below):
        pl.semaphore_signal(barrier, inc=1, device_id=device, device_id_type=MESH)

    @pl.when(is_mid)
    def _():
        pl.semaphore_signal(barrier, inc=1, device_id=outer, device_id_type=MESH)

    def mirror(value):
        return jnp.where(low, value, LAYERS - 1 - value)

    here = mirror(layer)

    def read(e, carry):
        partner = partners[lax.div(e, degree), lax.rem(e, degree)]
        peer = lax.rem(lax.div(partner, views), members)
        there = mirror(lax.div(peer, ROW))
        inside = jnp.where(there == 0, 1, jnp.where(there == 2, 0, 2))
        turn = jnp.where(here == 0, there - 1, inside)
        across = (lax.rem(peer, ROW) != side).astype(jnp.int32)
        block = jnp.where(there == here, 0, 1 + 2 * turn + across)
        live = lax.rem(e, degree) < counts[lax.div(e, degree)]
        codes[0, e] = jnp.where(live, block * views + lax.rem(partner, views), 0)
        return carry

    lax.fori_loop(0, entries, read, 0)

    def mark(cell, carry):
        found = jnp.int32(0)
        for e in range(entries):
            found = jnp.where(codes[0, e] == cell, 1, found)
        ask[0, cell] = found
        return carry

    lax.fori_loop(0, cells, mark, 0)
    own[0] = layer_norm(tokens[0]).astype(jnp.bfloat16)

    @pl.when(is_mid)
    def _():
        pl.semaphore_wait(barrier, 5)

    @pl.when(is_end)
    def _():
        pl.semaphore_wait(barrier, 4)

    ask_send().start()
    for v in range(views):
        if v:
            own[v] = layer_norm(tokens[v]).astype(jnp.bfloat16)
        to_near(v).start()

        @pl.when(is_mid)
        def _():
            own_to_b0(v).start()
            if v == 0:
                own_out().start()

    key_out[...] = own[key_view]
    count = 3 * views

    def same(ref, c):
        return ref[0, (1 + 2 * (c // views)) * views + c % views]

    def cross(ref, c):
        return ref[0, (2 + 2 * (c // views)) * views + c % views]

    ask_send().wait_recv()

    @pl.when(is_end)
    def _():
        for c in range(count):
            union[0, c] = jnp.maximum(same(ask, c), cross(asked, c))
        union_send().start()
        for v in range(views):
            own_to_b1(v).start()

    loads[0].wait()
    for v in range(views):
        queries[v] = project(own[v], w_query[...]).astype(jnp.bfloat16) * jnp.bfloat16(size**-0.5)
    for i in range(2):
        key_send(i).start()

    @pl.when(is_mid)
    def _():
        union_send().wait_recv()

    def line_up(flags, ready):
        spots, last = [], jnp.int32(-1)
        for flag, at in zip(flags, ready):
            spot = jnp.maximum(last + 1, at)
            spots.append(spot)
            last = jnp.where(flag == 1, spot, last)
        return spots, last

    far_ready = [0] * views + [v + 1 for v in range(views)] + [v + 1 + views for v in range(views)]

    def far_slots(flags):
        spots, last = line_up(flags[1:], far_ready[1:])
        return [jnp.int32(-1)] + spots, last

    def wide_slots(flags, behind):
        ready = []
        for c in range(count):
            late = 0 if c < 2 * views else c - 2 * views + 1
            ready.append(jnp.where(is_end, jnp.maximum(behind[c] - 2, 0), late))
        return line_up(flags, ready)

    def found(c, spots):
        return jnp.where(is_end, FREE if c == 0 else SLOTS + spots[c], PLAIN + c)

    mine = [union[0, c] for c in range(count)]
    my_far, far_last = far_slots(mine)
    beside_far, _ = far_slots([jnp.maximum(same(asked, c), cross(ask, c)) for c in range(count)])
    out_flags = [cross(asked, c) for c in range(count)]
    my_wide, out_last = wide_slots(out_flags, my_far)
    beside_wide, in_last = wide_slots([cross(ask, c) for c in range(count)], beside_far)
    for q in range(FAR):
        pick = jnp.int32(0)
        for c in range(1, count):
            pick = jnp.where((mine[c] == 1) & (my_far[c] == q), c, pick)
        picks[0, q] = pick
    for k in range(WIDE):
        pick = jnp.where(is_end, FREE, PLAIN)
        for c in range(count):
            pick = jnp.where((out_flags[c] == 1) & (my_wide[c] == k), found(c, my_far), pick)
        picks[0, FAR + k] = pick
    for v in range(views):
        sources[0, v] = v
    for c in range(count):
        sources[0, (1 + 2 * (c // views)) * views + c % views] = found(c, my_far)
        sources[0, (2 + 2 * (c // views)) * views + c % views] = CROSS + beside_wide[c]
    full = (far_last >= FAR) | (out_last >= WIDE) | (in_last >= WIDE)
    notes[0][0, 0] = full.astype(jnp.int32)

    def choose(choice, options):
        value = None
        for key, load in options:
            value = load() if value is None else jnp.where(choice == key, load(), value)
        return value

    def far_stage(q):
        options = [(c, functools.partial(own.__getitem__, c)) for c in range(min(views, q + views))]
        options += [(views + v, functools.partial(b0.__getitem__, v)) for v in range(views) if v < q]
        options += [
            (2 * views + v, functools.partial(b2.__getitem__, v)) for v in range(views) if v + views < q
        ]
        far_out[q] = choose(picks[0, q], options)
        far_send(q).start()

    def far_turn(q):
        @pl.when(is_mid)
        def _():
            if 1 <= q <= views:
                own_to_b0(q - 1).wait_recv()
            if q > views:
                b1_in(q - 1 - views).wait_recv()
            far_stage(q)
            if 1 <= q <= views:
                own_to_b1(q - 1).wait_recv()
                b1_in(q - 1).start()

    def wide_stage(k):
        choice = picks[0, FAR + k]

        @pl.when(is_end)
        def _():
            options = [(FREE, lambda: first_view[...])]
            options += [(SLOTS + q, functools.partial(far.__getitem__, q)) for q in range(k + 3)]
            wide_out[k] = choose(choice, options)

        @pl.when(is_mid)
        def _():
            options = [(PLAIN + v, functools.partial(b0.__getitem__, v)) for v in range(views)]
            options += [(PLAIN + views + v, functools.partial(b1.__getitem__, v)) for v in range(views)]
            options += [
                (PLAIN + 2 * views + v, functools.partial(b2.__getitem__, v))
                for v in range(views)
                if v < k
            ]
            wide_out[k] = choose(choice, options)

        wide_send(k).start()

    def far_arrive(q):
        @pl.when(is_end)
        def _():
            far_send(q).wait_recv()

    def wide_turn(k):
        far_arrive(k + 2)
        wide_stage(k)

    def note_value(i, value):
        notes[2 * i][0, 0] = value

    def seen(i):
        return notes[2 * i + 1][0, 0]

    rounds = groups // 2

    def note_step(i):
        if i == 0:
            note(0, beside).start()
        if i == 1:
            note(0, beside).wait_recv()
            note_value(1, jnp.maximum(notes[0][0, 0], seen(0)))

            @pl.when(is_end)
            def _():
                note(1, inner).start()
        if i == 2:
            @pl.when(is_mid)
            def _():
                note(1, inner).wait_recv()
                note_value(2, jnp.maximum(notes[2][0, 0], seen(1)))
                note(2, inner).start()
        if i == 3:
            @pl.when(is_mid)
            def _():
                note(2, inner).wait_recv()
                note_value(3, jnp.maximum(notes[4][0, 0], seen(2)))
                note(3, outer).start()
                note_value(4, notes[6][0, 0])
        if i == 4:
            @pl.when(is_end)
            def _():
                note(3, outer).wait_recv()
                note_value(4, seen(3))

            note_value(5, notes[8][0, 0])
            note(4, above).start()
            note(5, below).start()
        if i > 4:
            j = 2 * i - 6
            note(j, above).wait_recv()
            note(j + 1, below).wait_recv()
            value = jnp.maximum(notes[2 * j][0, 0], jnp.maximum(seen(j), seen(j + 1)))
            if i < 4 + rounds:
                note_value(j + 2, value)
                note_value(j + 3, value)
                note(j + 2, above).start()
                note(j + 3, below).start()
            else:
                flag_ref[0, 0] = value

    far_turn(0)
    note_step(0)

    def rank(e, carry):
        code = codes[0, e] * entries + e
        position = jnp.int32(2)
        for other in range(entries):
            position = position + (codes[0, other] * entries + other < code).astype(jnp.int32)
        table[0, e] = position
        return carry

    lax.fori_loop(0, entries, rank, 0)

    def sort(r, carry):
        cell, view = jnp.int32(0), key_view
        for e in range(entries):
            match = table[0, e] == r
            cell = jnp.where(match, codes[0, e], cell)
            view = jnp.where(match, e // degree, view)
        table[1, r], table[2, r] = sources[0, cell], view
        return carry

    lax.fori_loop(0, entries + 2, sort, 0)
    loads[1].wait()
    loads[2].wait()
    for i in range(2):
        key_send(i).wait_recv()

    late = [2 + max(0, entries - n) for n in (15, 12, 9, 7, 3)]
    turns = {
        1: [lambda: far_turn(1)],
        2: [lambda: far_turn(2), lambda: far_turn(3), lambda: far_turn(4)]
        + [functools.partial(far_arrive, q) for q in range(2)],
        late[0]: [lambda: far_turn(5), lambda: wide_turn(1), lambda: far_turn(6)]
        + [lambda: wide_turn(2)],
        late[1]: [lambda: far_turn(8), lambda: wide_turn(4), lambda: note_step(3)],
        late[2]: [lambda: wide_turn(5)],
        late[3]: [lambda: wide_turn(6)],
        late[4]: [],
    }
    for i in range(1, rounds + 1):
        turns[late[3] + i] = [functools.partial(note_step, 4 + i)]

    def events(t):
        for turn in turns[t]:
            turn()
        if t == 2:
            @pl.when(is_end)
            def _():
                own_out().wait_recv()

            for v in range(views):
                to_near(v).wait_recv()
            wide_turn(0)
            note_step(1)
        if t == late[0]:
            for k in range(3):
                wide_send(k).wait_recv()
            far_turn(7)
            wide_turn(3)
            note_step(2)
        if t == late[2]:
            wide_send(3).wait_recv()
            wide_send(4).wait_recv()
        if t == late[3]:
            wide_send(5).wait_recv()
            note_step(4)
        if t == late[4]:
            wide_send(6).wait_recv()

    def entry(t, carry):
        for when in turns:
            @pl.when(t == when)
            def _():
                events(when)

        source, view = table[1, t], table[2, t]

        def take(condition, key, load):
            @pl.when(condition)
            def _():
                cur[...] = jnp.where(source == key, load(), cur[...])

        def take_any(condition, start, ref):
            spot = source - start
            held = ref.shape[0]

            @pl.when(condition)
            def _():
                value = ref[jnp.clip(spot, 0, held - 1)]
                cur[...] = jnp.where((spot >= 0) & (spot < held), value, cur[...])

        @pl.when(t < 2)
        def _():
            cur[...] = keys[jnp.minimum(t, 1)]

        take_any(t >= 2, 0, near)
        for j, ref in enumerate((b0, b1)):
            take_any((t >= 2) & is_mid, PLAIN + j * views, ref)
        take_any((t >= late[1]) & is_mid, PLAIN + 2 * views, b2)
        take((t >= 2) & is_end, FREE, lambda: first_view[...])
        for q in range(FAR - 2):
            since = 2 if q < 3 else late[1]
            take(
                (t >= since) & (t < late[3]) & is_end, SLOTS + q,
                functools.partial(far.__getitem__, q),
            )
        take_any((t >= late[3]) & is_end, SLOTS, far)
        for k in range(WIDE - 1):
            since = late[0] if k < 3 else (late[2] if k < 5 else late[3])
            take((t >= since) & (t < late[4]), CROSS + k, functools.partial(wide.__getitem__, k))
        take_any(t >= late[4], CROSS, wide)

        def store(cols, value):
            results[t, :, cols] = value

        attend(lambda cols: queries[view, :, cols], cur[...], w_key, w_value, pair, store)
        return carry

    lax.fori_loop(0, entries + 2, entry, 0)
    loads[3].wait()
    for v in range(views):
        is_key = (key_view == v).astype(jnp.int32)
        total = counts[v]
        mixed = is_key.astype(jnp.float32) * (results[0] + results[1])
        for e in range(degree):
            live = (total > e).astype(jnp.int32).astype(jnp.float32)
            mixed += live * results[table[0, v * degree + e]]
        divisor = jnp.full((1, features), total + 2 * is_key, jnp.int32).astype(jnp.float32)
        mixed = mixed * (1.0 / divisor)
        out_ref[v] = (
            tokens[v].astype(jnp.float32) + project(mixed.astype(jnp.bfloat16), w_out[...])
        ).astype(out_ref.dtype)

    for v in range(views):
        to_near(v).wait_send()

        @pl.when(is_end)
        def _():
            own_to_b1(v).wait_send()

        @pl.when(is_mid)
        def _():
            own_to_b0(v).wait_send()
            b1_in(v).wait_send()

    @pl.when(is_mid)
    def _():
        own_out().wait_send()
        for q in range(FAR):
            far_send(q).wait_send()
        note(2, inner).wait_send()
        note(3, outer).wait_send()

    @pl.when(is_end)
    def _():
        union_send().wait_send()
        note(1, inner).wait_send()

    for k in range(WIDE):
        wide_send(k).wait_send()
    for i in range(2):
        key_send(i).wait_send()
    ask_send().wait_send()
    note(0, beside).wait_send()
    for i in range(4, 4 + 2 * rounds):
        note(i, above if i % 2 == 0 else below).wait_send()


def quick(tokens, w_query, w_key, w_value, w_out, partners, counts, key_slot):
    views, length, features = tokens.shape
    degree = partners.shape[1]
    entries = views * degree
    rounds = lax.axis_size("group") // 2
    smem = pl.BlockSpec(memory_space=pltpu.SMEM)
    hbm = pl.BlockSpec(memory_space=pltpu.HBM)
    vmem = pl.BlockSpec(memory_space=pltpu.VMEM)
    stay = [
        pltpu.with_memory_space_constraint(w, pltpu.HBM) for w in (w_query, w_key, w_value, w_out)
    ]
    slab = (length, features)
    half = jnp.bfloat16

    def slabs(count):
        return pltpu.VMEM((count, *slab), half)

    def numbers(*shape):
        return pltpu.SMEM(shape, jnp.int32)

    return pl.pallas_call(
        functools.partial(quick_kernel, degree),
        out_shape=(
            jax.ShapeDtypeStruct(tokens.shape, tokens.dtype),
            jax.ShapeDtypeStruct((1, 1), jnp.int32),
        ),
        in_specs=[smem] * 3 + [vmem] + [hbm] * 4,
        out_specs=(vmem, smem),
        scratch_shapes=[
            *[pltpu.VMEM((features, features), half)] * 4,
            *[slabs(views)] * 6,
            pltpu.VMEM(slab, half),
            slabs(FAR),
            slabs(WIDE),
            slabs(2),
            slabs(FAR),
            slabs(WIDE),
            pltpu.VMEM(slab, half),
            numbers(1, 7 * views),
            numbers(1, 7 * views),
            numbers(1, 3 * views),
            numbers(1, entries),
            numbers(1, 7 * views),
            numbers(1, FAR + WIDE),
            numbers(3, entries + 2),
            pltpu.VMEM(slab, half),
            pltpu.VMEM((length, 2 * features), half),
            pltpu.VMEM((entries + 2, *slab), jnp.float32),
            pltpu.SemaphoreType.DMA((4,)),
            pltpu.SemaphoreType.DMA((5 * views + FAR + WIDE + 16,)),
            pltpu.SemaphoreType.DMA((5 * views + FAR + WIDE + 16,)),
            *[numbers(1, 1)] * (2 * (4 + 2 * rounds)),
        ],
        compiler_params=pltpu.CompilerParams(
            collective_id=1, has_side_effects=True, vmem_limit_bytes=48 * 1024 * 1024
        ),
        name="sublayer_quick",
    )(partners, counts, key_slot, tokens, *stay)


def select_kernel(*arguments):
    result, flag = quick(*arguments)
    return lax.cond(flag[0, 0] > 0, lambda: one_kernel(*arguments), lambda: result)


def local_kernel(table, queries, w_key, w_value, block, inverse, tokens, w_out, out_ref, *scratch):
    held, pair, total, sem = scratch
    copy = pltpu.make_async_copy(block, held, sem)
    copy.start()
    total[...] = jnp.zeros_like(total)
    copy.wait()
    views, length, _ = total.shape

    def entry(e, carry):
        @pl.when(table[0, e] == 1)
        def _():
            place, view = table[1, e], table[2, e]

            def store(cols, value):
                total[view, :, cols] += value

            normed = layer_norm(held[place]).astype(jnp.bfloat16)
            attend(lambda cols: queries[view, :, cols], normed, w_key, w_value, pair, store)

        return carry

    lax.fori_loop(0, table.shape[1], entry, 0)
    for v in range(views):
        mixed = (total[v] * inverse[v]).astype(jnp.bfloat16)
        out_ref[v] = (tokens[v].astype(jnp.float32) + project(mixed, w_out[...])).astype(out_ref.dtype)


def exchange(tokens, w_query, w_key, w_value, w_out, partners, counts, key_slot):
    slot_key = key_slot[0]
    views, length, features = tokens.shape
    members, groups = lax.axis_size("member"), lax.axis_size("group")
    degree = partners.shape[1]
    entry_list = partners.reshape(-1)
    entries = entry_list.shape[0]
    capacity = (entries + members - 2) // (members - 1)
    peers = entry_list // views % members
    places = entry_list % views
    order = jnp.arange(entries, dtype=jnp.int32)
    earlier = (peers[:, None] == peers[None, :]) & (order[None, :] < order[:, None])
    cells = peers * capacity + jnp.sum(earlier.astype(jnp.int32), axis=1)
    requests = jnp.zeros((members * capacity,), jnp.int32).at[cells].set(places)
    asked = lax.all_to_all(
        requests.reshape(members, capacity), "member", split_axis=0, concat_axis=0, tiled=True
    )
    outgoing = tokens[asked.reshape(-1)].reshape(members, capacity, length, features)
    arrived = lax.all_to_all(outgoing, "member", split_axis=0, concat_axis=0, tiled=True)
    own_key = lax.dynamic_slice_in_dim(tokens, slot_key, 1, 0)
    below = lax.ppermute(own_key, "group", [(g, (g + 1) % groups) for g in range(groups)])
    above = lax.ppermute(own_key, "group", [((g + 1) % groups, g) for g in range(groups)])
    block = jnp.concatenate((arrived.reshape(members * capacity, length, features), below, above))
    normed = layer_norm(tokens).astype(jnp.bfloat16)
    queries = project(normed.reshape(views * length, features), w_query).astype(jnp.bfloat16)
    queries = queries.reshape(tokens.shape) * jnp.bfloat16((features // HEADS) ** -0.5)
    is_key = (jnp.arange(views, dtype=jnp.int32) == slot_key).astype(jnp.int32)
    inverse = 1.0 / (counts + 2 * is_key).astype(jnp.float32)
    live = (jnp.arange(degree, dtype=jnp.int32)[None, :] < counts[:, None]).reshape(-1)
    two = jnp.arange(2, dtype=jnp.int32)
    table = jnp.stack(
        (
            jnp.concatenate((live.astype(jnp.int32), jnp.ones_like(two))),
            jnp.concatenate((cells, members * capacity + two)),
            jnp.concatenate((order // degree, jnp.full_like(two, slot_key))),
        )
    )
    vmem = pl.BlockSpec(memory_space=pltpu.VMEM)
    smem = pl.BlockSpec(memory_space=pltpu.SMEM)
    hbm = pl.BlockSpec(memory_space=pl.ANY)
    return pl.pallas_call(
        local_kernel,
        out_shape=jax.ShapeDtypeStruct(tokens.shape, tokens.dtype),
        in_specs=[smem, vmem, vmem, vmem, hbm, smem, vmem, vmem],
        out_specs=vmem,
        scratch_shapes=[
            pltpu.VMEM(block.shape, block.dtype),
            pltpu.VMEM((length, 2 * features), jnp.bfloat16),
            pltpu.VMEM(tokens.shape, jnp.float32),
            pltpu.SemaphoreType.DMA,
        ],
        compiler_params=pltpu.CompilerParams(vmem_limit_bytes=60 * 1024 * 1024),
        name="attend_all",
    )(table, queries, w_key, w_value, block, inverse, tokens, w_out)


def sublayer(tokens, w_query, w_key, w_value, w_out, partners, counts, key_slot):
    views = tokens.shape[0]
    members = lax.axis_size("member")
    entries = partners.shape[0] * partners.shape[1]
    capacity = (entries + members - 2) // (members - 1)
    grid = members == LAYERS * ROW and views == capacity + 1
    run = select_kernel if grid else exchange
    return run(tokens, w_query, w_key, w_value, w_out, partners, counts, key_slot)


def solution(mesh):
    return jax.shard_map(
        sublayer,
        mesh=mesh,
        in_specs=(
            P(("group", "member"), None, None),
            P(),
            P(),
            P(),
            P(),
            P(("group", "member"), None),
            P(("group", "member")),
            P(("group", "member")),
        ),
        out_specs=P(("group", "member"), None, None),
        check_vma=False,
    )
```

```python
import functools

import jax
import jax.numpy as jnp
from jax import lax
from jax.experimental import pallas as pl
from jax.experimental.pallas import tpu as pltpu
from jax.sharding import PartitionSpec as P

HEADS = 12
ROW = 2
LAYERS = 4
MESH = pl.DeviceIdType.MESH


def layer_norm(values_in):
    values_in = values_in.astype(jnp.float32)
    centre = jnp.mean(values_in, axis=-1, keepdims=True)
    spread = jnp.mean((values_in - centre) ** 2, axis=-1, keepdims=True)
    return (values_in - centre) * lax.rsqrt(spread + 1e-05)


def project(rows, weights):
    return jnp.dot(rows, weights, preferred_element_type=jnp.float32)


def attend(query, normed, w_key, w_value, pair, store):
    features = normed.shape[1]
    pair[:, :features] = project(normed, w_key[...]).astype(jnp.bfloat16)
    pair[:, features:] = project(normed, w_value[...]).astype(jnp.bfloat16)
    heads(query, pair, features, store)


def heads(query, pair, features, store):
    size = features // HEADS
    lower = lax.broadcasted_iota(jnp.int32, (1, 2 * size), 1) < size
    for h in range(HEADS // 2):
        cols = pl.ds(2 * h * size, 2 * size)
        rows = query(cols)
        key = pair[:, cols]
        value = pair[:, pl.ds(features + 2 * h * size, 2 * size)]
        halves = []
        for keep in (lower, jnp.logical_not(lower)):
            part = jnp.where(keep, rows, jnp.zeros_like(rows))
            scores = lax.dot_general(
                part, key, (((1,), (1,)), ((), ())), preferred_element_type=jnp.float32
            )
            top = jnp.max(scores, axis=-1, keepdims=True)
            weights = jnp.exp(scores - top)
            mass = jnp.sum(weights, axis=-1, keepdims=True)
            halves.append(project(weights.astype(jnp.bfloat16), value) / mass)
        store(cols, jnp.where(lower, halves[0], halves[1]))


RAW_BLOCK, RAW_PLACE, POSITION, BLOCK, PLACE, VIEW = range(6)


def build_tables(layer, side, degree, capacity, views, members, partners, key_view, ask, table):
    entries = views * degree
    low = layer < LAYERS // 2

    def mirror(value):
        return jnp.where(low, value, LAYERS - 1 - value)

    here = mirror(layer)

    def read(e, flags):
        partner = partners[lax.div(e, degree), lax.rem(e, degree)]
        peer = lax.rem(lax.div(partner, views), members)
        place = lax.rem(partner, views)
        there = mirror(lax.div(peer, ROW))
        inside = jnp.where(there == 0, 1, jnp.where(there == 2, 0, 2))
        turn = jnp.where(here == 0, there - 1, inside)
        across = (lax.rem(peer, ROW) != side).astype(jnp.int32)
        block = jnp.where(there == here, 0, 1 + 2 * turn + across)
        table[RAW_BLOCK, e] = block
        table[RAW_PLACE, e] = place
        return tuple(
            jnp.where((block == 2 + 2 * (i // views)) & (place == i % views), 1, flag)
            for i, flag in enumerate(flags)
        )

    flags = lax.fori_loop(0, entries, read, (jnp.int32(0),) * (3 * views))
    slots = []
    for j in range(3):
        wanted = flags[j * views : (j + 1) * views]
        slot = capacity - sum(wanted)
        for v in range(views):
            slots.append(slot)
            slot = slot + wanted[v]
        for k in range(capacity):
            ask[0, j * capacity + k] = sum(
                jnp.where((wanted[v] == 1) & (slots[j * views + v] == k), v, 0) for v in range(views)
            )

    def rank(e, carry):
        block, place = table[RAW_BLOCK, e], table[RAW_PLACE, e]
        position = jnp.int32(2)
        for other in range(entries):
            ahead = (table[RAW_BLOCK, other] * entries + other) < block * entries + e
            position = position + ahead.astype(jnp.int32)
        table[POSITION, e] = position
        spot = place
        for i, slot in enumerate(slots):
            spot = jnp.where((block == 2 + 2 * (i // views)) & (place == i % views), slot, spot)
        table[RAW_PLACE, e] = spot
        return carry

    lax.fori_loop(0, entries, rank, 0)

    def sort(r, carry):
        block, place, view = jnp.int32(-1), jnp.int32(0), key_view
        for e in range(entries):
            match = table[POSITION, e] == r
            block = jnp.where(match, table[RAW_BLOCK, e], block)
            place = jnp.where(match, table[RAW_PLACE, e], place)
            view = jnp.where(match, e // degree, view)
        table[BLOCK, r], table[PLACE, r], table[VIEW, r] = block, place, view
        return carry

    lax.fori_loop(0, entries + 2, sort, 0)


def sublayer_kernel(degree, capacity, *refs):
    partners, counts, key_slot, tokens, wq_in, wk_in, wv_in, wo_in, out_ref = refs[:9]
    w_query, w_key, w_value, w_out = refs[9:13]
    own, queries, near, b0, b1, b2, s0, s1, s2, keys, staged, key_out = refs[13:25]
    ask, asked, table, cur, pair, results, load_sem, send_sem, recv_sem = refs[25:]
    views, length, features = tokens.shape
    members, groups = lax.axis_size("member"), lax.axis_size("group")
    entries = views * degree
    peers = members - 1
    size = features // HEADS
    me, group = lax.axis_index("member"), lax.axis_index("group")
    layer, side = me // ROW, me % ROW
    low = layer < LAYERS // 2
    toward = jnp.where(low, ROW, -ROW)
    is_end = jnp.logical_or(layer == 0, layer == LAYERS - 1)
    is_mid = jnp.logical_not(is_end)
    beside = {"member": layer * ROW + 1 - side}
    inner = {"member": me + toward}
    outer = {"member": jnp.clip(me - toward, 0, members - 1)}
    above = {"group": lax.rem(group + 1, groups)}
    below = {"group": lax.rem(group + groups - 1, groups)}

    blocks = (near, b0, s0, b1, s1, b2, s2)
    base, total = {}, 0
    for name, ref in (("near", near), ("b0", b0), ("b1", b1), ("b2", b2), ("s0", s0),
                      ("s1", s1), ("s2", s2), ("keys", keys)):
        base[name] = total
        total += ref.shape[0]

    def remote(source, target, send, recv, device):
        return pltpu.make_async_remote_copy(
            src_ref=source, dst_ref=target, send_sem=send_sem.at[send],
            recv_sem=recv_sem.at[recv], device_id=device, device_id_type=MESH,
        )

    sends = {}

    def slot(name, index):
        return sends.setdefault((name, index), len(sends))

    def hop(name, source, v, target, target_name, device):
        return remote(source.at[v], target.at[v], slot(name, v), base[target_name] + v, device)

    def to_near(v):
        return hop("near", own, v, near, "near", beside)

    def own_to_b1(v):
        return hop("in", own, v, b1, "b1", inner)

    def own_to_b0(v):
        return hop("in", own, v, b0, "b0", inner)

    def own_out(v):
        return hop("out", own, v, b0, "b0", outer)

    def b1_in(v):
        return hop("in2", b1, v, b2, "b2", inner)

    def b0_out(v):
        return hop("out1", b0, v, b1, "b1", outer)

    def b2_out(v):
        return hop("out2", b2, v, b2, "b2", outer)

    swaps = (s0, s1, s2)

    def swap(j, k):
        return remote(
            staged.at[j * capacity + k], swaps[j].at[k], slot("swap", j * capacity + k),
            base[f"s{j}"] + k, beside,
        )

    def key_send(i):
        return remote(
            key_out, keys.at[i], slot("key", i), base["keys"] + i, above if i == 0 else below
        )

    def ask_send():
        return remote(ask, asked, slot("ask", 0), total, beside)

    loads = [
        pltpu.make_async_copy(source, target, load_sem.at[i])
        for i, (source, target) in enumerate(
            ((wq_in, w_query), (wk_in, w_key), (wv_in, w_value), (wo_in, w_out))
        )
    ]
    for load in loads:
        load.start()

    barrier = pltpu.get_barrier_semaphore()
    for device in (beside, inner, above, below):
        pl.semaphore_signal(barrier, inc=1, device_id=device, device_id_type=MESH)

    @pl.when(is_mid)
    def _():
        pl.semaphore_signal(barrier, inc=1, device_id=outer, device_id_type=MESH)

    own[0] = layer_norm(tokens[0]).astype(jnp.bfloat16)

    @pl.when(is_mid)
    def _():
        pl.semaphore_wait(barrier, 5)

    @pl.when(is_end)
    def _():
        pl.semaphore_wait(barrier, 4)

    for v in range(views):
        if v:
            own[v] = layer_norm(tokens[v]).astype(jnp.bfloat16)
        to_near(v).start()

        @pl.when(is_end)
        def _():
            own_to_b1(v).start()

        @pl.when(is_mid)
        def _():
            own_to_b0(v).start()
            own_out(v).start()

    key_view = key_slot[0]
    key_out[...] = own[key_view]
    loads[0].wait()
    for v in range(views):
        queries[v] = project(own[v], w_query[...]).astype(jnp.bfloat16) * jnp.bfloat16(size**-0.5)
    for i in range(2):
        key_send(i).start()
    build_tables(layer, side, degree, capacity, views, members, partners, key_view, ask, table)
    ask_send().start()
    loads[1].wait()
    loads[2].wait()
    for i in range(2):
        key_send(i).wait_recv()

    def stage(j, k, source):
        choice = asked[0, j * capacity + k]
        value = source[0]
        for v in range(1, k + views - capacity + 1):
            value = jnp.where(choice == v, source[v], value)
        staged[j * capacity + k] = value
        swap(j, k).start()

    def events(t):
        def far(v):
            @pl.when(is_end)
            def _():
                b0_out(v).wait_recv()

            @pl.when(is_mid)
            def _():
                b1_in(v).wait_recv()
                b2_out(v).start()

        def last(v):
            @pl.when(is_end)
            def _():
                b2_out(v).wait_recv()

        def arrive(j):
            for k in range(capacity):
                swap(j, k).wait_recv()

        extra = views - capacity

        def spread(wait, j, source, v):
            wait(v)
            if v >= extra:
                stage(j, v - extra, source)

        if t == first[0]:
            for v in range(views):
                own_to_b0(v).wait_recv()

                @pl.when(is_mid)
                def _():
                    b0_out(v).start()
                    own_to_b1(v).wait_recv()
                    b1_in(v).start()

                if v >= extra:
                    stage(0, v - extra, b0)
            for v in range(views):
                to_near(v).wait_recv()
        if t == first[2]:
            for v in range(views - 2):
                spread(far, 1, b1, v)
            arrive(0)
        if t == first[2] + 1:
            spread(far, 1, b1, views - 2)
        if t == first[3]:
            spread(far, 1, b1, views - 1)
        if t == first[4]:
            for v in range(views - 2):
                spread(last, 2, b2, v)
            arrive(1)
        if t == first[4] + 1:
            spread(last, 2, b2, views - 2)
        if t == first[5]:
            spread(last, 2, b2, views - 1)
        if t == first[6]:
            arrive(2)

    first = [2 + max(0, entries - capacity * (peers - j)) for j in range(peers)]

    def entry(t, carry):
        for when in sorted({first[0], first[2], first[2] + 1, first[3], first[4], first[4] + 1,
                            first[5], first[6]}):
            @pl.when(t == when)
            def _():
                events(when)

        @pl.when(t < 2)
        def _():
            cur[...] = keys[jnp.minimum(t, 1)]

        block, place, view = table[BLOCK, t], table[PLACE, t], table[VIEW, t]
        for j, ref in enumerate(blocks):
            @pl.when(t >= first[j])
            def _():
                value = ref[jnp.minimum(place, ref.shape[0] - 1)]
                cur[...] = jnp.where(block == j, value, cur[...])

        def store(cols, value):
            results[t, :, cols] = value

        attend(lambda cols: queries[view, :, cols], cur[...], w_key, w_value, pair, store)
        return carry

    ask_send().wait_recv()
    lax.fori_loop(0, entries + 2, entry, 0)
    loads[3].wait()
    for v in range(views):
        is_key = (key_view == v).astype(jnp.int32)
        count = counts[v]
        mixed = is_key.astype(jnp.float32) * (results[0] + results[1])
        for e in range(degree):
            live = (count > e).astype(jnp.int32).astype(jnp.float32)
            mixed += live * results[table[POSITION, v * degree + e]]
        divisor = jnp.full((1, features), count + 2 * is_key, jnp.int32).astype(jnp.float32)
        mixed = mixed * (1.0 / divisor)
        out_ref[v] = (
            tokens[v].astype(jnp.float32) + project(mixed.astype(jnp.bfloat16), w_out[...])
        ).astype(out_ref.dtype)

    for v in range(views):
        to_near(v).wait_send()

        @pl.when(is_end)
        def _():
            own_to_b1(v).wait_send()

        @pl.when(is_mid)
        def _():
            own_to_b0(v).wait_send()
            own_out(v).wait_send()
            b1_in(v).wait_send()
            b0_out(v).wait_send()
            b2_out(v).wait_send()

    for j in range(3):
        for k in range(capacity):
            swap(j, k).wait_send()
    for i in range(2):
        key_send(i).wait_send()
    ask_send().wait_send()


def one_kernel(tokens, w_query, w_key, w_value, w_out, partners, counts, key_slot):
    views, length, features = tokens.shape
    members = lax.axis_size("member")
    degree = partners.shape[1]
    entries = views * degree
    capacity = (entries + members - 2) // (members - 1)
    smem = pl.BlockSpec(memory_space=pltpu.SMEM)
    hbm = pl.BlockSpec(memory_space=pltpu.HBM)
    vmem = pl.BlockSpec(memory_space=pltpu.VMEM)
    stay = [
        pltpu.with_memory_space_constraint(w, pltpu.HBM) for w in (w_query, w_key, w_value, w_out)
    ]
    slab = (length, features)
    weights_shape = pltpu.VMEM((features, features), jnp.bfloat16)
    half = jnp.bfloat16
    blocks = [pltpu.VMEM((views, *slab), half)] * 6 + [pltpu.VMEM((capacity, *slab), half)] * 3
    sends = 6 * views + 3 * capacity + 3 + views
    receives = 4 * views + 3 * capacity + 3
    return pl.pallas_call(
        functools.partial(sublayer_kernel, degree, capacity),
        out_shape=jax.ShapeDtypeStruct(tokens.shape, tokens.dtype),
        in_specs=[smem] * 3 + [vmem] + [hbm] * 4,
        out_specs=vmem,
        scratch_shapes=[
            weights_shape,
            weights_shape,
            weights_shape,
            weights_shape,
            *blocks,
            pltpu.VMEM((2, *slab), half),
            pltpu.VMEM((3 * capacity, *slab), half),
            pltpu.VMEM(slab, half),
            pltpu.SMEM((1, 3 * capacity), jnp.int32),
            pltpu.SMEM((1, 3 * capacity), jnp.int32),
            pltpu.SMEM((6, entries + 2), jnp.int32),
            pltpu.VMEM(slab, half),
            pltpu.VMEM((length, 2 * features), half),
            pltpu.VMEM((entries + 2, *slab), jnp.float32),
            pltpu.SemaphoreType.DMA((4,)),
            pltpu.SemaphoreType.DMA((sends,)),
            pltpu.SemaphoreType.DMA((receives,)),
        ],
        compiler_params=pltpu.CompilerParams(
            collective_id=0, has_side_effects=True, vmem_limit_bytes=44 * 1024 * 1024
        ),
        name="sublayer",
    )(partners, counts, key_slot, tokens, *stay)


FAR, WIDE = 9, 7
FREE, SLOTS, PLAIN, CROSS = 4, 5, 4, 16
KEYS = CROSS + WIDE


def quick_kernel(degree, *refs):
    partners, counts, key_slot, tokens, wq_in, wk_in, wv_in, wo_in, out_ref, flag_ref = refs[:10]
    w_query, w_key, w_value, w_out = refs[10:14]
    own, queries, near, landing, wide, keys, far_out, wide_out, key_out = refs[14:23]
    ask, asked, union, codes, sources, picks, table, pairs, results = refs[23:32]
    load_sem, send_sem, recv_sem = refs[32:35]
    notes = refs[35:]
    views, length, features = tokens.shape
    members, groups = lax.axis_size("member"), lax.axis_size("group")
    entries = views * degree
    size = features // HEADS
    me, group = lax.axis_index("member"), lax.axis_index("group")
    layer, side = me // ROW, me % ROW
    low = layer < LAYERS // 2
    toward = jnp.where(low, ROW, -ROW)
    is_end = jnp.logical_or(layer == 0, layer == LAYERS - 1)
    is_mid = jnp.logical_not(is_end)
    beside = {"member": layer * ROW + 1 - side}
    inner = {"member": me + toward}
    outer = {"member": jnp.clip(me - toward, 0, members - 1)}
    above = {"group": lax.rem(group + 1, groups)}
    below = {"group": lax.rem(group + groups - 1, groups)}
    key_view = key_slot[0]
    cells = 7 * views
    b0, b1, b2 = (landing.at[pl.ds(i * views, views)] for i in range(3))
    first_view, far = landing.at[pl.ds(0, 1)], landing.at[pl.ds(1, FAR)]
    names = {}

    def number(kind, name):
        return names.setdefault((kind, name), sum(1 for k, _ in names if k == kind))

    def remote(name, source, target, landing, device):
        return pltpu.make_async_remote_copy(
            src_ref=source, dst_ref=target, send_sem=send_sem.at[number(0, name)],
            recv_sem=recv_sem.at[number(1, landing)], device_id=device, device_id_type=MESH,
        )

    def to_near(v):
        return remote(("near", v), own.at[v], near.at[v], ("near", v), beside)

    def own_to_b1(v):
        return remote(("in", v), own.at[v], b1.at[v], ("b1", v), inner)

    def own_to_b0(v):
        return remote(("in", v), own.at[v], b0.at[v], ("b0", v), inner)

    def b1_in(v):
        return remote(("in2", v), b1.at[v], b2.at[v], ("b2", v), inner)

    def own_out():
        return remote("free", own.at[0], first_view.at[0], "free", outer)

    def far_send(q):
        return remote(("far", q), far_out.at[q], far.at[q], ("far", q), outer)

    def wide_send(k):
        return remote(("wide", k), wide_out.at[k], wide.at[k], ("wide", k), beside)

    def key_send(i):
        return remote(("key", i), key_out, keys.at[i], ("key", i), below if i else above)

    def ask_send():
        return remote("ask", ask, asked, "ask", beside)

    def union_send():
        return remote("union", union, union, "union", inner)

    def note(i, device):
        return remote(("note", i), notes[2 * i], notes[2 * i + 1], ("note", i), device)

    loads = [
        pltpu.make_async_copy(source, target, load_sem.at[i])
        for i, (source, target) in enumerate(
            ((wq_in, w_query), (wk_in, w_key), (wv_in, w_value), (wo_in, w_out))
        )
    ]
    for load in loads:
        load.start()
    barrier = pltpu.get_barrier_semaphore()
    for device in (beside, inner, above, below):
        pl.semaphore_signal(barrier, inc=1, device_id=device, device_id_type=MESH)

    @pl.when(is_mid)
    def _():
        pl.semaphore_signal(barrier, inc=1, device_id=outer, device_id_type=MESH)

    def mirror(value):
        return jnp.where(low, value, LAYERS - 1 - value)

    here = mirror(layer)

    def read(e, carry):
        partner = partners[lax.div(e, degree), lax.rem(e, degree)]
        peer = lax.rem(lax.div(partner, views), members)
        there = mirror(lax.div(peer, ROW))
        inside = jnp.where(there == 0, 1, jnp.where(there == 2, 0, 2))
        turn = jnp.where(here == 0, there - 1, inside)
        across = (lax.rem(peer, ROW) != side).astype(jnp.int32)
        block = jnp.where(there == here, 0, 1 + 2 * turn + across)
        live = lax.rem(e, degree) < counts[lax.div(e, degree)]
        codes[0, e] = jnp.where(live, block * views + lax.rem(partner, views), 0)
        return carry

    lax.fori_loop(0, entries, read, 0)

    def mark(cell, carry):
        found = jnp.int32(0)
        for e in range(entries):
            found = jnp.where(codes[0, e] == cell, 1, found)
        ask[0, cell] = found
        return carry

    lax.fori_loop(0, cells, mark, 0)
    own[0] = layer_norm(tokens[0]).astype(jnp.bfloat16)

    @pl.when(is_mid)
    def _():
        pl.semaphore_wait(barrier, 5)

    @pl.when(is_end)
    def _():
        pl.semaphore_wait(barrier, 4)

    ask_send().start()
    for v in range(views):
        if v:
            own[v] = layer_norm(tokens[v]).astype(jnp.bfloat16)
        to_near(v).start()

        @pl.when(is_mid)
        def _():
            own_to_b0(v).start()
            if v == 0:
                own_out().start()

    key_out[...] = own[key_view]
    count = 3 * views

    def same(ref, c):
        return ref[0, (1 + 2 * (c // views)) * views + c % views]

    def cross(ref, c):
        return ref[0, (2 + 2 * (c // views)) * views + c % views]

    ask_send().wait_recv()

    @pl.when(is_end)
    def _():
        for c in range(count):
            union[0, c] = jnp.maximum(same(ask, c), cross(asked, c))
        union_send().start()
        for v in range(views):
            own_to_b1(v).start()

    loads[0].wait()
    for v in range(views):
        queries[v] = project(own[v], w_query[...]).astype(jnp.bfloat16) * jnp.bfloat16(size**-0.5)
    for i in range(2):
        key_send(i).start()

    @pl.when(is_mid)
    def _():
        union_send().wait_recv()

    def line_up(flags, ready):
        spots, last = [], jnp.int32(-1)
        for flag, at in zip(flags, ready):
            spot = jnp.maximum(last + 1, at)
            spots.append(spot)
            last = jnp.where(flag == 1, spot, last)
        return spots, last

    far_ready = [0] * views + [v + 1 for v in range(views)] + [v + 1 + views for v in range(views)]

    def far_slots(flags):
        spots, last = line_up(flags[1:], far_ready[1:])
        return [jnp.int32(-1)] + spots, last

    def wide_slots(flags, behind):
        ready = []
        for c in range(count):
            late = 0 if c < 2 * views else c - 2 * views + 1
            ready.append(jnp.where(is_end, jnp.maximum(behind[c] - 2, 0), late))
        return line_up(flags, ready)

    def found(c, spots):
        return jnp.where(is_end, FREE if c == 0 else SLOTS + spots[c], PLAIN + c)

    mine = [union[0, c] for c in range(count)]
    my_far, far_last = far_slots(mine)
    beside_far, _ = far_slots([jnp.maximum(same(asked, c), cross(ask, c)) for c in range(count)])
    out_flags = [cross(asked, c) for c in range(count)]
    my_wide, out_last = wide_slots(out_flags, my_far)
    beside_wide, in_last = wide_slots([cross(ask, c) for c in range(count)], beside_far)
    for q in range(FAR):
        pick = jnp.int32(0)
        for c in range(1, count):
            pick = jnp.where((mine[c] == 1) & (my_far[c] == q), c, pick)
        picks[0, q] = pick
    for k in range(WIDE):
        pick = jnp.where(is_end, FREE, PLAIN)
        for c in range(count):
            pick = jnp.where((out_flags[c] == 1) & (my_wide[c] == k), found(c, my_far), pick)
        picks[0, FAR + k] = pick
    for v in range(views):
        sources[0, v] = v
    for c in range(count):
        sources[0, (1 + 2 * (c // views)) * views + c % views] = found(c, my_far)
        sources[0, (2 + 2 * (c // views)) * views + c % views] = CROSS + beside_wide[c]
    full = (far_last >= FAR) | (out_last >= WIDE) | (in_last >= WIDE)
    notes[0][0, 0] = full.astype(jnp.int32)

    def view_of(ref, index):
        return ref[index]

    def choose(choice, options):
        value = None
        for key, load in options:
            value = load() if value is None else jnp.where(choice == key, load(), value)
        return value

    def far_stage(q):
        options = [(c, functools.partial(view_of, own, c)) for c in range(min(views, q + views))]
        options += [(views + v, functools.partial(view_of, b0, v)) for v in range(views) if v < q]
        options += [
            (2 * views + v, functools.partial(view_of, b2, v)) for v in range(views) if v + views < q
        ]
        far_out[q] = choose(picks[0, q], options)
        far_send(q).start()

    def far_turn(q):
        @pl.when(is_mid)
        def _():
            if 1 <= q <= views:
                own_to_b0(q - 1).wait_recv()
            if q > views:
                b1_in(q - 1 - views).wait_recv()
            far_stage(q)
            if 1 <= q <= views:
                own_to_b1(q - 1).wait_recv()
                b1_in(q - 1).start()

    def wide_stage(k):
        choice = picks[0, FAR + k]

        @pl.when(is_end)
        def _():
            options = [(FREE, lambda: first_view[0])]
            options += [(SLOTS + q, functools.partial(view_of, far, q)) for q in range(k + 3)]
            wide_out[k] = choose(choice, options)

        @pl.when(is_mid)
        def _():
            options = [(PLAIN + v, functools.partial(view_of, b0, v)) for v in range(views)]
            options += [(PLAIN + views + v, functools.partial(view_of, b1, v)) for v in range(views)]
            options += [
                (PLAIN + 2 * views + v, functools.partial(view_of, b2, v))
                for v in range(views)
                if v < k
            ]
            wide_out[k] = choose(choice, options)

        wide_send(k).start()

    def far_arrive(q):
        @pl.when(is_end)
        def _():
            far_send(q).wait_recv()

    def wide_turn(k):
        far_arrive(k + 2)
        wide_stage(k)

    def note_value(i, value):
        notes[2 * i][0, 0] = value

    def seen(i):
        return notes[2 * i + 1][0, 0]

    rounds = groups // 2

    def note_step(i):
        if i == 0:
            note(0, beside).start()
        if i == 1:
            note(0, beside).wait_recv()
            note_value(1, jnp.maximum(notes[0][0, 0], seen(0)))

            @pl.when(is_end)
            def _():
                note(1, inner).start()
        if i == 2:
            @pl.when(is_mid)
            def _():
                note(1, inner).wait_recv()
                note_value(2, jnp.maximum(notes[2][0, 0], seen(1)))
                note(2, inner).start()
        if i == 3:
            @pl.when(is_mid)
            def _():
                note(2, inner).wait_recv()
                note_value(3, jnp.maximum(notes[4][0, 0], seen(2)))
                note(3, outer).start()
                note_value(4, notes[6][0, 0])
        if i == 4:
            @pl.when(is_end)
            def _():
                note(3, outer).wait_recv()
                note_value(4, seen(3))

            note_value(5, notes[8][0, 0])
            note(4, above).start()
            note(5, below).start()
        if i > 4:
            j = 2 * i - 6
            note(j, above).wait_recv()
            note(j + 1, below).wait_recv()
            value = jnp.maximum(notes[2 * j][0, 0], jnp.maximum(seen(j), seen(j + 1)))
            if i < 4 + rounds:
                note_value(j + 2, value)
                note_value(j + 3, value)
                note(j + 2, above).start()
                note(j + 3, below).start()
            else:
                flag_ref[0, 0] = value

    far_turn(0)
    note_step(0)

    def rank(e, carry):
        code = codes[0, e] * entries + e
        position = jnp.int32(2)
        for other in range(entries):
            position = position + (codes[0, other] * entries + other < code).astype(jnp.int32)
        table[0, e] = position
        return carry

    lax.fori_loop(0, entries, rank, 0)

    def sort(r, carry):
        cell, view = jnp.int32(0), key_view
        for e in range(entries):
            match = table[0, e] == r
            cell = jnp.where(match, codes[0, e], cell)
            view = jnp.where(match, e // degree, view)
        table[1, r], table[2, r] = jnp.where(r < 2, KEYS + r, sources[0, cell]), view
        return carry

    lax.fori_loop(0, entries + 2, sort, 0)
    loads[1].wait()
    loads[2].wait()
    for i in range(2):
        key_send(i).wait_recv()

    def learn(place, ref, start, count):
        def one(i, carry):
            rows = ref[start + i]
            pairs[place + i, :, :features] = project(rows, w_key[...]).astype(jnp.bfloat16)
            pairs[place + i, :, features:] = project(rows, w_value[...]).astype(jnp.bfloat16)
            return carry

        lax.fori_loop(0, count, one, 0)

    def learn_far(first, last):
        @pl.when(is_end)
        def _():
            learn(SLOTS + first, far, first, last - first)

    def learn_last(first, last):
        @pl.when(is_mid)
        def _():
            learn(PLAIN + 2 * views + first, b2, first, last - first)

    learn(KEYS, keys, 0, 2)

    late = [2 + max(0, entries - n) for n in (15, 12, 9, 7, 3)]
    turns = {
        1: [lambda: far_turn(1)],
        2: [lambda: far_turn(2), lambda: far_turn(3), lambda: far_turn(4)]
        + [functools.partial(far_arrive, q) for q in range(2)],
        late[0]: [lambda: far_turn(5), lambda: wide_turn(1), lambda: far_turn(6)]
        + [lambda: wide_turn(2)],
        late[1]: [lambda: far_turn(8), lambda: wide_turn(4), lambda: note_step(3)],
        late[2]: [lambda: wide_turn(5)],
        late[3]: [lambda: wide_turn(6)],
        late[4]: [],
    }
    for i in range(1, rounds + 1):
        turns[late[3] + i] = [functools.partial(note_step, 4 + i)]

    def events(t):
        for turn in turns[t]:
            turn()
        if t == 2:
            @pl.when(is_end)
            def _():
                own_out().wait_recv()

            for v in range(views):
                to_near(v).wait_recv()
            wide_turn(0)
            note_step(1)
            learn(0, near, 0, views)

            @pl.when(is_end)
            def _():
                learn(FREE, first_view, 0, 1)

            @pl.when(is_mid)
            def _():
                learn(PLAIN, b0, 0, views)
                learn(PLAIN + views, b1, 0, views)

            learn_far(0, 3)
        if t == late[0]:
            learn_far(3, 5)
            learn_last(0, 2)
            for k in range(3):
                wide_send(k).wait_recv()
            far_turn(7)
            wide_turn(3)
            note_step(2)
            learn(CROSS, wide, 0, 3)
            learn_far(5, 6)
            learn_last(2, 3)
        if t == late[1]:
            learn_far(6, 7)
            learn_last(3, 4)
        if t == late[2]:
            wide_send(3).wait_recv()
            wide_send(4).wait_recv()
            learn(CROSS + 3, wide, 3, 2)
            learn_far(7, 8)
        if t == late[3]:
            wide_send(5).wait_recv()
            note_step(4)
            learn(CROSS + 5, wide, 5, 1)
            learn_far(8, 9)
        if t == late[4]:
            wide_send(6).wait_recv()
            learn(CROSS + 6, wide, 6, 1)

    def entry(t, carry):
        for when in turns:
            @pl.when(t == when)
            def _():
                events(when)

        source, view = table[1, t], table[2, t]

        def store(cols, value):
            results[t, :, cols] = value

        heads(lambda cols: queries[view, :, cols], pairs.at[source], features, store)
        return carry

    lax.fori_loop(0, entries + 2, entry, 0)
    loads[3].wait()
    for v in range(views):
        is_key = (key_view == v).astype(jnp.int32)
        total = counts[v]
        mixed = is_key.astype(jnp.float32) * (results[0] + results[1])
        for e in range(degree):
            live = (total > e).astype(jnp.int32).astype(jnp.float32)
            mixed += live * results[table[0, v * degree + e]]
        divisor = jnp.full((1, features), total + 2 * is_key, jnp.int32).astype(jnp.float32)
        mixed = mixed * (1.0 / divisor)
        out_ref[v] = (
            tokens[v].astype(jnp.float32) + project(mixed.astype(jnp.bfloat16), w_out[...])
        ).astype(out_ref.dtype)

    for v in range(views):
        to_near(v).wait_send()

        @pl.when(is_end)
        def _():
            own_to_b1(v).wait_send()

        @pl.when(is_mid)
        def _():
            own_to_b0(v).wait_send()
            b1_in(v).wait_send()

    @pl.when(is_mid)
    def _():
        own_out().wait_send()
        for q in range(FAR):
            far_send(q).wait_send()
        note(2, inner).wait_send()
        note(3, outer).wait_send()

    @pl.when(is_end)
    def _():
        union_send().wait_send()
        note(1, inner).wait_send()

    for k in range(WIDE):
        wide_send(k).wait_send()
    for i in range(2):
        key_send(i).wait_send()
    ask_send().wait_send()
    note(0, beside).wait_send()
    for i in range(4, 4 + 2 * rounds):
        note(i, above if i % 2 == 0 else below).wait_send()


def quick(tokens, w_query, w_key, w_value, w_out, partners, counts, key_slot):
    views, length, features = tokens.shape
    degree = partners.shape[1]
    entries = views * degree
    rounds = lax.axis_size("group") // 2
    smem = pl.BlockSpec(memory_space=pltpu.SMEM)
    hbm = pl.BlockSpec(memory_space=pltpu.HBM)
    vmem = pl.BlockSpec(memory_space=pltpu.VMEM)
    stay = [
        pltpu.with_memory_space_constraint(w, pltpu.HBM) for w in (w_query, w_key, w_value, w_out)
    ]
    slab = (length, features)
    half = jnp.bfloat16

    def slabs(count):
        return pltpu.VMEM((count, *slab), half)

    def numbers(*shape):
        return pltpu.SMEM(shape, jnp.int32)

    return pl.pallas_call(
        functools.partial(quick_kernel, degree),
        out_shape=(
            jax.ShapeDtypeStruct(tokens.shape, tokens.dtype),
            jax.ShapeDtypeStruct((1, 1), jnp.int32),
        ),
        in_specs=[smem] * 3 + [vmem] + [hbm] * 4,
        out_specs=(vmem, smem),
        scratch_shapes=[
            *[pltpu.VMEM((features, features), half)] * 4,
            *[slabs(views)] * 3,
            slabs(3 * views),
            slabs(WIDE),
            slabs(2),
            slabs(FAR),
            slabs(WIDE),
            pltpu.VMEM(slab, half),
            numbers(1, 7 * views),
            numbers(1, 7 * views),
            numbers(1, 3 * views),
            numbers(1, entries),
            numbers(1, 7 * views),
            numbers(1, FAR + WIDE),
            numbers(3, entries + 2),
            pltpu.VMEM((KEYS + 2, length, 2 * features), half),
            pltpu.VMEM((entries + 2, *slab), jnp.float32),
            pltpu.SemaphoreType.DMA((4,)),
            pltpu.SemaphoreType.DMA((5 * views + FAR + WIDE + 16,)),
            pltpu.SemaphoreType.DMA((5 * views + FAR + WIDE + 16,)),
            *[numbers(1, 1)] * (2 * (4 + 2 * rounds)),
        ],
        compiler_params=pltpu.CompilerParams(
            collective_id=1, has_side_effects=True, vmem_limit_bytes=50 * 1024 * 1024
        ),
        name="sublayer_quick",
    )(partners, counts, key_slot, tokens, *stay)


def select_kernel(*arguments):
    result, flag = quick(*arguments)
    return lax.cond(flag[0, 0] > 0, lambda: one_kernel(*arguments), lambda: result)


def local_kernel(table, queries, w_key, w_value, block, inverse, tokens, w_out, out_ref, *scratch):
    held, pair, total, sem = scratch
    copy = pltpu.make_async_copy(block, held, sem)
    copy.start()
    total[...] = jnp.zeros_like(total)
    copy.wait()
    views, length, _ = total.shape

    def entry(e, carry):
        @pl.when(table[0, e] == 1)
        def _():
            place, view = table[1, e], table[2, e]

            def store(cols, value):
                total[view, :, cols] += value

            normed = layer_norm(held[place]).astype(jnp.bfloat16)
            attend(lambda cols: queries[view, :, cols], normed, w_key, w_value, pair, store)

        return carry

    lax.fori_loop(0, table.shape[1], entry, 0)
    for v in range(views):
        mixed = (total[v] * inverse[v]).astype(jnp.bfloat16)
        out_ref[v] = (tokens[v].astype(jnp.float32) + project(mixed, w_out[...])).astype(out_ref.dtype)


def exchange(tokens, w_query, w_key, w_value, w_out, partners, counts, key_slot):
    slot_key = key_slot[0]
    views, length, features = tokens.shape
    members, groups = lax.axis_size("member"), lax.axis_size("group")
    degree = partners.shape[1]
    entry_list = partners.reshape(-1)
    entries = entry_list.shape[0]
    capacity = (entries + members - 2) // (members - 1)
    peers = entry_list // views % members
    places = entry_list % views
    order = jnp.arange(entries, dtype=jnp.int32)
    earlier = (peers[:, None] == peers[None, :]) & (order[None, :] < order[:, None])
    cells = peers * capacity + jnp.sum(earlier.astype(jnp.int32), axis=1)
    requests = jnp.zeros((members * capacity,), jnp.int32).at[cells].set(places)
    asked = lax.all_to_all(
        requests.reshape(members, capacity), "member", split_axis=0, concat_axis=0, tiled=True
    )
    outgoing = tokens[asked.reshape(-1)].reshape(members, capacity, length, features)
    arrived = lax.all_to_all(outgoing, "member", split_axis=0, concat_axis=0, tiled=True)
    own_key = lax.dynamic_slice_in_dim(tokens, slot_key, 1, 0)
    below = lax.ppermute(own_key, "group", [(g, (g + 1) % groups) for g in range(groups)])
    above = lax.ppermute(own_key, "group", [((g + 1) % groups, g) for g in range(groups)])
    block = jnp.concatenate((arrived.reshape(members * capacity, length, features), below, above))
    normed = layer_norm(tokens).astype(jnp.bfloat16)
    queries = project(normed.reshape(views * length, features), w_query).astype(jnp.bfloat16)
    queries = queries.reshape(tokens.shape) * jnp.bfloat16((features // HEADS) ** -0.5)
    is_key = (jnp.arange(views, dtype=jnp.int32) == slot_key).astype(jnp.int32)
    inverse = 1.0 / (counts + 2 * is_key).astype(jnp.float32)
    live = (jnp.arange(degree, dtype=jnp.int32)[None, :] < counts[:, None]).reshape(-1)
    two = jnp.arange(2, dtype=jnp.int32)
    table = jnp.stack(
        (
            jnp.concatenate((live.astype(jnp.int32), jnp.ones_like(two))),
            jnp.concatenate((cells, members * capacity + two)),
            jnp.concatenate((order // degree, jnp.full_like(two, slot_key))),
        )
    )
    vmem = pl.BlockSpec(memory_space=pltpu.VMEM)
    smem = pl.BlockSpec(memory_space=pltpu.SMEM)
    hbm = pl.BlockSpec(memory_space=pl.ANY)
    return pl.pallas_call(
        local_kernel,
        out_shape=jax.ShapeDtypeStruct(tokens.shape, tokens.dtype),
        in_specs=[smem, vmem, vmem, vmem, hbm, smem, vmem, vmem],
        out_specs=vmem,
        scratch_shapes=[
            pltpu.VMEM(block.shape, block.dtype),
            pltpu.VMEM((length, 2 * features), jnp.bfloat16),
            pltpu.VMEM(tokens.shape, jnp.float32),
            pltpu.SemaphoreType.DMA,
        ],
        compiler_params=pltpu.CompilerParams(vmem_limit_bytes=60 * 1024 * 1024),
        name="attend_all",
    )(table, queries, w_key, w_value, block, inverse, tokens, w_out)


def sublayer(tokens, w_query, w_key, w_value, w_out, partners, counts, key_slot):
    views = tokens.shape[0]
    members = lax.axis_size("member")
    entries = partners.shape[0] * partners.shape[1]
    capacity = (entries + members - 2) // (members - 1)
    grid = members == LAYERS * ROW and views == capacity + 1
    run = select_kernel if grid else exchange
    return run(tokens, w_query, w_key, w_value, w_out, partners, counts, key_slot)


def solution(mesh):
    return jax.shard_map(
        sublayer,
        mesh=mesh,
        in_specs=(
            P(("group", "member"), None, None),
            P(),
            P(),
            P(),
            P(),
            P(("group", "member"), None),
            P(("group", "member")),
            P(("group", "member")),
        ),
        out_specs=P(("group", "member"), None, None),
        check_vma=False,
    )
```

```python
import functools

import jax
import jax.numpy as jnp
from jax import lax
from jax.experimental import pallas as pl
from jax.experimental.pallas import tpu as pltpu
from jax.sharding import PartitionSpec as P

HEADS = 12
ROW = 2
LAYERS = 4
MESH = pl.DeviceIdType.MESH


def layer_norm(values_in):
    values_in = values_in.astype(jnp.float32)
    centre = jnp.mean(values_in, axis=-1, keepdims=True)
    spread = jnp.mean((values_in - centre) ** 2, axis=-1, keepdims=True)
    return (values_in - centre) * lax.rsqrt(spread + 1e-05)


def project(rows, weights):
    return jnp.dot(rows, weights, preferred_element_type=jnp.float32)


def attend(query, normed, w_key, w_value, pair, store):
    features = normed.shape[1]
    pair[:, :features] = project(normed, w_key[...]).astype(jnp.bfloat16)
    pair[:, features:] = project(normed, w_value[...]).astype(jnp.bfloat16)
    heads(query, pair, features, store)


def heads(query, pair, features, store):
    size = features // HEADS
    lower = lax.broadcasted_iota(jnp.int32, (1, 2 * size), 1) < size
    for h in range(HEADS // 2):
        cols = pl.ds(2 * h * size, 2 * size)
        rows = query(cols)
        key = pair[:, cols]
        value = pair[:, pl.ds(features + 2 * h * size, 2 * size)]
        halves = []
        for keep in (lower, jnp.logical_not(lower)):
            part = jnp.where(keep, rows, jnp.zeros_like(rows))
            scores = lax.dot_general(
                part, key, (((1,), (1,)), ((), ())), preferred_element_type=jnp.float32
            )
            top = jnp.max(scores, axis=-1, keepdims=True)
            weights = jnp.exp(scores - top)
            mass = jnp.sum(weights, axis=-1, keepdims=True)
            halves.append(project(weights.astype(jnp.bfloat16), value) / mass)
        store(cols, jnp.where(lower, halves[0], halves[1]))


RAW_BLOCK, RAW_PLACE, POSITION, BLOCK, PLACE, VIEW = range(6)


def build_tables(layer, side, degree, capacity, views, members, partners, key_view, ask, table):
    entries = views * degree
    low = layer < LAYERS // 2

    def mirror(value):
        return jnp.where(low, value, LAYERS - 1 - value)

    here = mirror(layer)

    def read(e, flags):
        partner = partners[lax.div(e, degree), lax.rem(e, degree)]
        peer = lax.rem(lax.div(partner, views), members)
        place = lax.rem(partner, views)
        there = mirror(lax.div(peer, ROW))
        inside = jnp.where(there == 0, 1, jnp.where(there == 2, 0, 2))
        turn = jnp.where(here == 0, there - 1, inside)
        across = (lax.rem(peer, ROW) != side).astype(jnp.int32)
        block = jnp.where(there == here, 0, 1 + 2 * turn + across)
        table[RAW_BLOCK, e] = block
        table[RAW_PLACE, e] = place
        return tuple(
            jnp.where((block == 2 + 2 * (i // views)) & (place == i % views), 1, flag)
            for i, flag in enumerate(flags)
        )

    flags = lax.fori_loop(0, entries, read, (jnp.int32(0),) * (3 * views))
    slots = []
    for j in range(3):
        wanted = flags[j * views : (j + 1) * views]
        slot = capacity - sum(wanted)
        for v in range(views):
            slots.append(slot)
            slot = slot + wanted[v]
        for k in range(capacity):
            ask[0, j * capacity + k] = sum(
                jnp.where((wanted[v] == 1) & (slots[j * views + v] == k), v, 0) for v in range(views)
            )

    def rank(e, carry):
        block, place = table[RAW_BLOCK, e], table[RAW_PLACE, e]
        position = jnp.int32(2)
        for other in range(entries):
            ahead = (table[RAW_BLOCK, other] * entries + other) < block * entries + e
            position = position + ahead.astype(jnp.int32)
        table[POSITION, e] = position
        spot = place
        for i, slot in enumerate(slots):
            spot = jnp.where((block == 2 + 2 * (i // views)) & (place == i % views), slot, spot)
        table[RAW_PLACE, e] = spot
        return carry

    lax.fori_loop(0, entries, rank, 0)

    def sort(r, carry):
        block, place, view = jnp.int32(-1), jnp.int32(0), key_view
        for e in range(entries):
            match = table[POSITION, e] == r
            block = jnp.where(match, table[RAW_BLOCK, e], block)
            place = jnp.where(match, table[RAW_PLACE, e], place)
            view = jnp.where(match, e // degree, view)
        table[BLOCK, r], table[PLACE, r], table[VIEW, r] = block, place, view
        return carry

    lax.fori_loop(0, entries + 2, sort, 0)


def sublayer_kernel(degree, capacity, *refs):
    partners, counts, key_slot, tokens, wq_in, wk_in, wv_in, wo_in, out_ref = refs[:9]
    w_query, w_key, w_value, w_out = refs[9:13]
    own, queries, near, b0, b1, b2, s0, s1, s2, keys, staged, key_out = refs[13:25]
    ask, asked, table, cur, pair, results, load_sem, send_sem, recv_sem = refs[25:]
    views, length, features = tokens.shape
    members, groups = lax.axis_size("member"), lax.axis_size("group")
    entries = views * degree
    peers = members - 1
    size = features // HEADS
    me, group = lax.axis_index("member"), lax.axis_index("group")
    layer, side = me // ROW, me % ROW
    low = layer < LAYERS // 2
    toward = jnp.where(low, ROW, -ROW)
    is_end = jnp.logical_or(layer == 0, layer == LAYERS - 1)
    is_mid = jnp.logical_not(is_end)
    beside = {"member": layer * ROW + 1 - side}
    inner = {"member": me + toward}
    outer = {"member": jnp.clip(me - toward, 0, members - 1)}
    above = {"group": lax.rem(group + 1, groups)}
    below = {"group": lax.rem(group + groups - 1, groups)}

    blocks = (near, b0, s0, b1, s1, b2, s2)
    base, total = {}, 0
    for name, ref in (("near", near), ("b0", b0), ("b1", b1), ("b2", b2), ("s0", s0),
                      ("s1", s1), ("s2", s2), ("keys", keys)):
        base[name] = total
        total += ref.shape[0]

    def remote(source, target, send, recv, device):
        return pltpu.make_async_remote_copy(
            src_ref=source, dst_ref=target, send_sem=send_sem.at[send],
            recv_sem=recv_sem.at[recv], device_id=device, device_id_type=MESH,
        )

    sends = {}

    def slot(name, index):
        return sends.setdefault((name, index), len(sends))

    def hop(name, source, v, target, target_name, device):
        return remote(source.at[v], target.at[v], slot(name, v), base[target_name] + v, device)

    def to_near(v):
        return hop("near", own, v, near, "near", beside)

    def own_to_b1(v):
        return hop("in", own, v, b1, "b1", inner)

    def own_to_b0(v):
        return hop("in", own, v, b0, "b0", inner)

    def own_out(v):
        return hop("out", own, v, b0, "b0", outer)

    def b1_in(v):
        return hop("in2", b1, v, b2, "b2", inner)

    def b0_out(v):
        return hop("out1", b0, v, b1, "b1", outer)

    def b2_out(v):
        return hop("out2", b2, v, b2, "b2", outer)

    swaps = (s0, s1, s2)

    def swap(j, k):
        return remote(
            staged.at[j * capacity + k], swaps[j].at[k], slot("swap", j * capacity + k),
            base[f"s{j}"] + k, beside,
        )

    def key_send(i):
        return remote(
            key_out, keys.at[i], slot("key", i), base["keys"] + i, above if i == 0 else below
        )

    def ask_send():
        return remote(ask, asked, slot("ask", 0), total, beside)

    loads = [
        pltpu.make_async_copy(source, target, load_sem.at[i])
        for i, (source, target) in enumerate(
            ((wq_in, w_query), (wk_in, w_key), (wv_in, w_value), (wo_in, w_out))
        )
    ]
    for load in loads:
        load.start()

    barrier = pltpu.get_barrier_semaphore()
    for device in (beside, inner, above, below):
        pl.semaphore_signal(barrier, inc=1, device_id=device, device_id_type=MESH)

    @pl.when(is_mid)
    def _():
        pl.semaphore_signal(barrier, inc=1, device_id=outer, device_id_type=MESH)

    own[0] = layer_norm(tokens[0]).astype(jnp.bfloat16)

    @pl.when(is_mid)
    def _():
        pl.semaphore_wait(barrier, 5)

    @pl.when(is_end)
    def _():
        pl.semaphore_wait(barrier, 4)

    for v in range(views):
        if v:
            own[v] = layer_norm(tokens[v]).astype(jnp.bfloat16)
        to_near(v).start()

        @pl.when(is_end)
        def _():
            own_to_b1(v).start()

        @pl.when(is_mid)
        def _():
            own_to_b0(v).start()
            own_out(v).start()

    key_view = key_slot[0]
    key_out[...] = own[key_view]
    loads[0].wait()
    for v in range(views):
        queries[v] = project(own[v], w_query[...]).astype(jnp.bfloat16) * jnp.bfloat16(size**-0.5)
    for i in range(2):
        key_send(i).start()
    build_tables(layer, side, degree, capacity, views, members, partners, key_view, ask, table)
    ask_send().start()
    loads[1].wait()
    loads[2].wait()
    for i in range(2):
        key_send(i).wait_recv()

    def stage(j, k, source):
        choice = asked[0, j * capacity + k]
        value = source[0]
        for v in range(1, k + views - capacity + 1):
            value = jnp.where(choice == v, source[v], value)
        staged[j * capacity + k] = value
        swap(j, k).start()

    def events(t):
        def far(v):
            @pl.when(is_end)
            def _():
                b0_out(v).wait_recv()

            @pl.when(is_mid)
            def _():
                b1_in(v).wait_recv()
                b2_out(v).start()

        def last(v):
            @pl.when(is_end)
            def _():
                b2_out(v).wait_recv()

        def arrive(j):
            for k in range(capacity):
                swap(j, k).wait_recv()

        extra = views - capacity

        def spread(wait, j, source, v):
            wait(v)
            if v >= extra:
                stage(j, v - extra, source)

        if t == first[0]:
            for v in range(views):
                own_to_b0(v).wait_recv()

                @pl.when(is_mid)
                def _():
                    b0_out(v).start()
                    own_to_b1(v).wait_recv()
                    b1_in(v).start()

                if v >= extra:
                    stage(0, v - extra, b0)
            for v in range(views):
                to_near(v).wait_recv()
        if t == first[2]:
            for v in range(views - 2):
                spread(far, 1, b1, v)
            arrive(0)
        if t == first[2] + 1:
            spread(far, 1, b1, views - 2)
        if t == first[3]:
            spread(far, 1, b1, views - 1)
        if t == first[4]:
            for v in range(views - 2):
                spread(last, 2, b2, v)
            arrive(1)
        if t == first[4] + 1:
            spread(last, 2, b2, views - 2)
        if t == first[5]:
            spread(last, 2, b2, views - 1)
        if t == first[6]:
            arrive(2)

    first = [2 + max(0, entries - capacity * (peers - j)) for j in range(peers)]

    def entry(t, carry):
        for when in sorted({first[0], first[2], first[2] + 1, first[3], first[4], first[4] + 1,
                            first[5], first[6]}):
            @pl.when(t == when)
            def _():
                events(when)

        @pl.when(t < 2)
        def _():
            cur[...] = keys[jnp.minimum(t, 1)]

        block, place, view = table[BLOCK, t], table[PLACE, t], table[VIEW, t]
        for j, ref in enumerate(blocks):
            @pl.when(t >= first[j])
            def _():
                value = ref[jnp.minimum(place, ref.shape[0] - 1)]
                cur[...] = jnp.where(block == j, value, cur[...])

        def store(cols, value):
            results[t, :, cols] = value

        attend(lambda cols: queries[view, :, cols], cur[...], w_key, w_value, pair, store)
        return carry

    ask_send().wait_recv()
    lax.fori_loop(0, entries + 2, entry, 0)
    loads[3].wait()
    for v in range(views):
        is_key = (key_view == v).astype(jnp.int32)
        count = counts[v]
        mixed = is_key.astype(jnp.float32) * (results[0] + results[1])
        for e in range(degree):
            live = (count > e).astype(jnp.int32).astype(jnp.float32)
            mixed += live * results[table[POSITION, v * degree + e]]
        divisor = jnp.full((1, features), count + 2 * is_key, jnp.int32).astype(jnp.float32)
        mixed = mixed * (1.0 / divisor)
        out_ref[v] = (
            tokens[v].astype(jnp.float32) + project(mixed.astype(jnp.bfloat16), w_out[...])
        ).astype(out_ref.dtype)

    for v in range(views):
        to_near(v).wait_send()

        @pl.when(is_end)
        def _():
            own_to_b1(v).wait_send()

        @pl.when(is_mid)
        def _():
            own_to_b0(v).wait_send()
            own_out(v).wait_send()
            b1_in(v).wait_send()
            b0_out(v).wait_send()
            b2_out(v).wait_send()

    for j in range(3):
        for k in range(capacity):
            swap(j, k).wait_send()
    for i in range(2):
        key_send(i).wait_send()
    ask_send().wait_send()


def one_kernel(tokens, w_query, w_key, w_value, w_out, partners, counts, key_slot):
    views, length, features = tokens.shape
    members = lax.axis_size("member")
    degree = partners.shape[1]
    entries = views * degree
    capacity = (entries + members - 2) // (members - 1)
    smem = pl.BlockSpec(memory_space=pltpu.SMEM)
    hbm = pl.BlockSpec(memory_space=pltpu.HBM)
    vmem = pl.BlockSpec(memory_space=pltpu.VMEM)
    stay = [
        pltpu.with_memory_space_constraint(w, pltpu.HBM) for w in (w_query, w_key, w_value, w_out)
    ]
    slab = (length, features)
    weights_shape = pltpu.VMEM((features, features), jnp.bfloat16)
    half = jnp.bfloat16
    blocks = [pltpu.VMEM((views, *slab), half)] * 6 + [pltpu.VMEM((capacity, *slab), half)] * 3
    sends = 6 * views + 3 * capacity + 3 + views
    receives = 4 * views + 3 * capacity + 3
    return pl.pallas_call(
        functools.partial(sublayer_kernel, degree, capacity),
        out_shape=jax.ShapeDtypeStruct(tokens.shape, tokens.dtype),
        in_specs=[smem] * 3 + [vmem] + [hbm] * 4,
        out_specs=vmem,
        scratch_shapes=[
            weights_shape,
            weights_shape,
            weights_shape,
            weights_shape,
            *blocks,
            pltpu.VMEM((2, *slab), half),
            pltpu.VMEM((3 * capacity, *slab), half),
            pltpu.VMEM(slab, half),
            pltpu.SMEM((1, 3 * capacity), jnp.int32),
            pltpu.SMEM((1, 3 * capacity), jnp.int32),
            pltpu.SMEM((6, entries + 2), jnp.int32),
            pltpu.VMEM(slab, half),
            pltpu.VMEM((length, 2 * features), half),
            pltpu.VMEM((entries + 2, *slab), jnp.float32),
            pltpu.SemaphoreType.DMA((4,)),
            pltpu.SemaphoreType.DMA((sends,)),
            pltpu.SemaphoreType.DMA((receives,)),
        ],
        compiler_params=pltpu.CompilerParams(
            collective_id=0, has_side_effects=True, vmem_limit_bytes=44 * 1024 * 1024
        ),
        name="sublayer",
    )(partners, counts, key_slot, tokens, *stay)


FAR, WIDE = 9, 7
FREE, SLOTS, PLAIN, CROSS = 4, 5, 4, 16
KEYS = CROSS + WIDE


def quick_kernel(degree, *refs):
    partners, counts, key_slot, tokens, wq_in, wk_in, wv_in, wo_in, out_ref, flag_ref = refs[:10]
    w_query, w_key, w_value, w_out = refs[10:14]
    own, queries, arrived, far_out, wide_out, key_out = refs[14:20]
    ask, asked, union, codes, sources, picks, table, pairs, results = refs[20:29]
    load_sem, send_sem, recv_sem = refs[29:32]
    notes = refs[32:]
    views, length, features = tokens.shape
    members, groups = lax.axis_size("member"), lax.axis_size("group")
    entries = views * degree
    size = features // HEADS
    me, group = lax.axis_index("member"), lax.axis_index("group")
    layer, side = me // ROW, me % ROW
    low = layer < LAYERS // 2
    toward = jnp.where(low, ROW, -ROW)
    is_end = jnp.logical_or(layer == 0, layer == LAYERS - 1)
    is_mid = jnp.logical_not(is_end)
    beside = {"member": layer * ROW + 1 - side}
    inner = {"member": me + toward}
    outer = {"member": jnp.clip(me - toward, 0, members - 1)}
    above = {"group": lax.rem(group + 1, groups)}
    below = {"group": lax.rem(group + groups - 1, groups)}
    key_view = key_slot[0]
    cells = 7 * views
    near, b0, b1, b2 = (arrived.at[pl.ds(i * views, views)] for i in range(4))
    first_view, far = arrived.at[pl.ds(FREE, 1)], arrived.at[pl.ds(SLOTS, FAR)]
    wide, keys = arrived.at[pl.ds(CROSS, WIDE)], arrived.at[pl.ds(KEYS, 2)]
    names = {}

    def number(kind, name):
        return names.setdefault((kind, name), sum(1 for k, _ in names if k == kind))

    def remote(name, source, target, landing, device):
        return pltpu.make_async_remote_copy(
            src_ref=source, dst_ref=target, send_sem=send_sem.at[number(0, name)],
            recv_sem=recv_sem.at[number(1, landing)], device_id=device, device_id_type=MESH,
        )

    def to_near(v):
        return remote(("near", v), own.at[v], near.at[v], ("near", v), beside)

    def own_to_b1(v):
        return remote(("in", v), own.at[v], b1.at[v], ("b1", v), inner)

    def own_to_b0(v):
        return remote(("in", v), own.at[v], b0.at[v], ("b0", v), inner)

    def b1_in(v):
        return remote(("in2", v), b1.at[v], b2.at[v], ("b2", v), inner)

    def own_out():
        return remote("free", own.at[0], first_view.at[0], "free", outer)

    def far_send(q):
        return remote(("far", q), far_out.at[q], far.at[q], ("far", q), outer)

    def wide_send(k):
        return remote(("wide", k), wide_out.at[k], wide.at[k], ("wide", k), beside)

    def key_send(i):
        return remote(("key", i), key_out, keys.at[i], ("key", i), below if i else above)

    def ask_send():
        return remote("ask", ask, asked, "ask", beside)

    def union_send():
        return remote("union", union, union, "union", inner)

    def note(i, device):
        return remote(("note", i), notes[2 * i], notes[2 * i + 1], ("note", i), device)

    loads = [
        pltpu.make_async_copy(source, target, load_sem.at[i])
        for i, (source, target) in enumerate(
            ((wq_in, w_query), (wk_in, w_key), (wv_in, w_value), (wo_in, w_out))
        )
    ]
    for load in loads:
        load.start()
    barrier = pltpu.get_barrier_semaphore()
    for device in (beside, inner, above, below):
        pl.semaphore_signal(barrier, inc=1, device_id=device, device_id_type=MESH)

    @pl.when(is_mid)
    def _():
        pl.semaphore_signal(barrier, inc=1, device_id=outer, device_id_type=MESH)

    def mirror(value):
        return jnp.where(low, value, LAYERS - 1 - value)

    here = mirror(layer)

    def read(e, carry):
        partner = partners[lax.div(e, degree), lax.rem(e, degree)]
        peer = lax.rem(lax.div(partner, views), members)
        there = mirror(lax.div(peer, ROW))
        inside = jnp.where(there == 0, 1, jnp.where(there == 2, 0, 2))
        turn = jnp.where(here == 0, there - 1, inside)
        across = (lax.rem(peer, ROW) != side).astype(jnp.int32)
        block = jnp.where(there == here, 0, 1 + 2 * turn + across)
        live = lax.rem(e, degree) < counts[lax.div(e, degree)]
        codes[0, e] = jnp.where(live, block * views + lax.rem(partner, views), 0)
        return carry

    lax.fori_loop(0, entries, read, 0)

    def mark(cell, carry):
        found = jnp.int32(0)
        for e in range(entries):
            found = jnp.where(codes[0, e] == cell, 1, found)
        ask[0, cell] = found
        return carry

    lax.fori_loop(0, cells, mark, 0)
    own[0] = layer_norm(tokens[0]).astype(jnp.bfloat16)

    @pl.when(is_mid)
    def _():
        pl.semaphore_wait(barrier, 5)

    @pl.when(is_end)
    def _():
        pl.semaphore_wait(barrier, 4)

    ask_send().start()
    for v in range(views):
        if v:
            own[v] = layer_norm(tokens[v]).astype(jnp.bfloat16)
        to_near(v).start()

        @pl.when(is_mid)
        def _():
            own_to_b0(v).start()
            if v == 0:
                own_out().start()

    key_out[...] = own[key_view]
    count = 3 * views

    def same(ref, c):
        return ref[0, (1 + 2 * (c // views)) * views + c % views]

    def cross(ref, c):
        return ref[0, (2 + 2 * (c // views)) * views + c % views]

    ask_send().wait_recv()

    @pl.when(is_end)
    def _():
        for c in range(count):
            union[0, c] = jnp.maximum(same(ask, c), cross(asked, c))
        union_send().start()
        for v in range(views):
            own_to_b1(v).start()

    loads[0].wait()
    for v in range(views):
        queries[v] = project(own[v], w_query[...]).astype(jnp.bfloat16) * jnp.bfloat16(size**-0.5)
    for i in range(2):
        key_send(i).start()

    @pl.when(is_mid)
    def _():
        union_send().wait_recv()

    def line_up(flags, ready):
        spots, last = [], jnp.int32(-1)
        for flag, at in zip(flags, ready):
            spot = jnp.maximum(last + 1, at)
            spots.append(spot)
            last = jnp.where(flag == 1, spot, last)
        return spots, last

    far_ready = [0] * views + [v + 1 for v in range(views)] + [v + 1 + views for v in range(views)]

    def far_slots(flags):
        spots, last = line_up(flags[1:], far_ready[1:])
        return [jnp.int32(-1)] + spots, last

    def wide_slots(flags, behind):
        ready = []
        for c in range(count):
            late = 0 if c < 2 * views else c - 2 * views + 1
            ready.append(jnp.where(is_end, jnp.maximum(behind[c] - 2, 0), late))
        return line_up(flags, ready)

    def found(c, spots):
        return jnp.where(is_end, FREE if c == 0 else SLOTS + spots[c], PLAIN + c)

    mine = [union[0, c] for c in range(count)]
    my_far, far_last = far_slots(mine)
    beside_far, _ = far_slots([jnp.maximum(same(asked, c), cross(ask, c)) for c in range(count)])
    out_flags = [cross(asked, c) for c in range(count)]
    my_wide, out_last = wide_slots(out_flags, my_far)
    beside_wide, in_last = wide_slots([cross(ask, c) for c in range(count)], beside_far)
    for q in range(FAR):
        pick = jnp.int32(0)
        for c in range(1, count):
            pick = jnp.where((mine[c] == 1) & (my_far[c] == q), c, pick)
        picks[0, q] = pick
    for k in range(WIDE):
        pick = jnp.where(is_end, FREE, PLAIN)
        for c in range(count):
            pick = jnp.where((out_flags[c] == 1) & (my_wide[c] == k), found(c, my_far), pick)
        picks[0, FAR + k] = pick
    for v in range(views):
        sources[0, v] = v
    for c in range(count):
        sources[0, (1 + 2 * (c // views)) * views + c % views] = found(c, my_far)
        sources[0, (2 + 2 * (c // views)) * views + c % views] = CROSS + beside_wide[c]
    full = (far_last >= FAR) | (out_last >= WIDE) | (in_last >= WIDE)
    notes[0][0, 0] = full.astype(jnp.int32)

    def view_of(ref, index):
        return ref[index]

    def choose(choice, options):
        value = None
        for key, load in options:
            value = load() if value is None else jnp.where(choice == key, load(), value)
        return value

    def far_stage(q):
        options = [(c, functools.partial(view_of, own, c)) for c in range(min(views, q + views))]
        options += [(views + v, functools.partial(view_of, b0, v)) for v in range(views) if v < q]
        options += [
            (2 * views + v, functools.partial(view_of, b2, v)) for v in range(views) if v + views < q
        ]
        far_out[q] = choose(picks[0, q], options)
        far_send(q).start()

    def far_turn(q):
        @pl.when(is_mid)
        def _():
            if 1 <= q <= views:
                own_to_b0(q - 1).wait_recv()
            if q > views:
                b1_in(q - 1 - views).wait_recv()
            far_stage(q)
            if 1 <= q <= views:
                own_to_b1(q - 1).wait_recv()
                b1_in(q - 1).start()

    def wide_stage(k):
        choice = picks[0, FAR + k]

        @pl.when(is_end)
        def _():
            options = [(FREE, lambda: first_view[0])]
            options += [(SLOTS + q, functools.partial(view_of, far, q)) for q in range(k + 3)]
            wide_out[k] = choose(choice, options)

        @pl.when(is_mid)
        def _():
            options = [(PLAIN + v, functools.partial(view_of, b0, v)) for v in range(views)]
            options += [(PLAIN + views + v, functools.partial(view_of, b1, v)) for v in range(views)]
            options += [
                (PLAIN + 2 * views + v, functools.partial(view_of, b2, v))
                for v in range(views)
                if v < k
            ]
            wide_out[k] = choose(choice, options)

        wide_send(k).start()

    def far_arrive(q):
        @pl.when(is_end)
        def _():
            far_send(q).wait_recv()

    def wide_turn(k):
        far_arrive(k + 2)
        wide_stage(k)

    def note_value(i, value):
        notes[2 * i][0, 0] = value

    def seen(i):
        return notes[2 * i + 1][0, 0]

    rounds = groups // 2

    def note_step(i):
        if i == 0:
            note(0, beside).start()
        if i == 1:
            note(0, beside).wait_recv()
            note_value(1, jnp.maximum(notes[0][0, 0], seen(0)))

            @pl.when(is_end)
            def _():
                note(1, inner).start()
        if i == 2:
            @pl.when(is_mid)
            def _():
                note(1, inner).wait_recv()
                note_value(2, jnp.maximum(notes[2][0, 0], seen(1)))
                note(2, inner).start()
        if i == 3:
            @pl.when(is_mid)
            def _():
                note(2, inner).wait_recv()
                note_value(3, jnp.maximum(notes[4][0, 0], seen(2)))
                note(3, outer).start()
                note_value(4, notes[6][0, 0])
        if i == 4:
            @pl.when(is_end)
            def _():
                note(3, outer).wait_recv()
                note_value(4, seen(3))

            note_value(5, notes[8][0, 0])
            note(4, above).start()
            note(5, below).start()
        if i > 4:
            j = 2 * i - 6
            note(j, above).wait_recv()
            note(j + 1, below).wait_recv()
            value = jnp.maximum(notes[2 * j][0, 0], jnp.maximum(seen(j), seen(j + 1)))
            if i < 4 + rounds:
                note_value(j + 2, value)
                note_value(j + 3, value)
                note(j + 2, above).start()
                note(j + 3, below).start()
            else:
                flag_ref[0, 0] = value

    far_turn(0)
    note_step(0)

    def rank(e, carry):
        code = codes[0, e] * entries + e
        position = jnp.int32(2)
        for other in range(entries):
            position = position + (codes[0, other] * entries + other < code).astype(jnp.int32)
        table[0, e] = position
        return carry

    lax.fori_loop(0, entries, rank, 0)

    def sort(r, carry):
        cell, view = jnp.int32(0), key_view
        for e in range(entries):
            match = table[0, e] == r
            cell = jnp.where(match, codes[0, e], cell)
            view = jnp.where(match, e // degree, view)
        table[1, r], table[2, r] = jnp.where(r < 2, KEYS + r, sources[0, cell]), view
        return carry

    lax.fori_loop(0, entries + 2, sort, 0)
    loads[1].wait()
    loads[2].wait()
    plan = []

    def do(*actions):
        plan.append([list(actions), None, None])

    def learn(end, mid):
        plan.append([[], (end, mid), None])

    def attends(first, last, *actions):
        for r in range(first, last):
            plan.append([[], None, r + 2])
        for i, action in enumerate(actions):
            plan[i - len(actions)][0].append(action)

    def key_arrive():
        for i in range(2):
            key_send(i).wait_recv()

    def near_arrive(v):
        to_near(v).wait_recv()
        if v == 0:
            @pl.when(is_end)
            def _():
                own_out().wait_recv()
        elif v < views - 1:
            far_arrive(v - 1)

    def wide_arrive(k):
        wide_send(k).wait_recv()

    run = functools.partial
    for v in range(views):
        do(run(far_turn, v + 1), run(near_arrive, v))
        if v == views - 1:
            do(run(wide_turn, 0))
        learn(v, v)
        learn(FREE + v, PLAIN + v)
        learn(None, PLAIN + views + v)
        if v == 0:
            do(key_arrive)
            learn(KEYS, KEYS)
            learn(KEYS + 1, KEYS + 1)
            attends(-2, -1)
        if v == 1:
            attends(-1, 0)
    bounds = [max(0, entries - n) for n in (15, 15, 15, 12, 9, 7, 3, 0)]
    attends(0, bounds[0])
    for k in range(1, WIDE):
        if views + k < FAR:
            do(run(far_turn, views + k))
        do(run(wide_turn, k))
        if k < 5:
            do(run(note_step, k - 1) if k > 1 else (lambda: None))
        learn(FREE + views - 1 + k, PLAIN + 2 * views + k - 1 if k <= views else None)
        do(run(wide_arrive, k - 1))
        learn(CROSS + k - 1, CROSS + k - 1)
        attends(bounds[k - 1], bounds[k])
    plan[-3][0].append(run(note_step, 4))
    for i in range(1, rounds + 1):
        plan[i - 3][0].append(run(note_step, 4 + i))
    do(run(wide_arrive, WIDE - 1))
    learn(CROSS + WIDE - 1, CROSS + WIDE - 1)
    attends(bounds[WIDE - 1], bounds[WIDE])
    steps = []
    waiting = []
    for actions, views_to_learn, r in plan:
        waiting += actions
        if views_to_learn is not None or r is not None:
            steps.append((waiting, views_to_learn, r))
            waiting = []

    def number_at(u, values):
        value = jnp.int32(-1)
        for i, wanted in enumerate(values):
            if wanted is not None:
                value = jnp.where(u == i, wanted, value)
        return value

    def store_to(t):
        def store(cols, value):
            results[t, :, cols] = value

        return store

    def step(u, carry):
        for i, (actions, _, _) in enumerate(steps):
            if actions:
                @pl.when(u == i)
                def _():
                    for action in actions:
                        action()

        end = number_at(u, [pick and pick[0] for _, pick, _ in steps])
        mid = number_at(u, [pick and pick[1] for _, pick, _ in steps])
        place = jnp.where(is_end, end, mid)

        @pl.when(place >= 0)
        def _():
            rows = arrived[place]
            pairs[place, :, :features] = project(rows, w_key[...]).astype(jnp.bfloat16)
            pairs[place, :, features:] = project(rows, w_value[...]).astype(jnp.bfloat16)

        t = number_at(u, [r for _, _, r in steps])

        @pl.when(t >= 0)
        def _():
            source, view = table[1, t], table[2, t]
            heads(lambda cols: queries[view, :, cols], pairs.at[source], features, store_to(t))

        return carry

    lax.fori_loop(0, len(steps), step, 0)
    loads[3].wait()
    for v in range(views):
        is_key = (key_view == v).astype(jnp.int32)
        total = counts[v]
        mixed = is_key.astype(jnp.float32) * (results[0] + results[1])
        for e in range(degree):
            live = (total > e).astype(jnp.int32).astype(jnp.float32)
            mixed += live * results[table[0, v * degree + e]]
        divisor = jnp.full((1, features), total + 2 * is_key, jnp.int32).astype(jnp.float32)
        mixed = mixed * (1.0 / divisor)
        out_ref[v] = (
            tokens[v].astype(jnp.float32) + project(mixed.astype(jnp.bfloat16), w_out[...])
        ).astype(out_ref.dtype)

    for v in range(views):
        to_near(v).wait_send()

        @pl.when(is_end)
        def _():
            own_to_b1(v).wait_send()

        @pl.when(is_mid)
        def _():
            own_to_b0(v).wait_send()
            b1_in(v).wait_send()

    @pl.when(is_mid)
    def _():
        own_out().wait_send()
        for q in range(FAR):
            far_send(q).wait_send()
        note(2, inner).wait_send()
        note(3, outer).wait_send()

    @pl.when(is_end)
    def _():
        union_send().wait_send()
        note(1, inner).wait_send()

    for k in range(WIDE):
        wide_send(k).wait_send()
    for i in range(2):
        key_send(i).wait_send()
    ask_send().wait_send()
    note(0, beside).wait_send()
    for i in range(4, 4 + 2 * rounds):
        note(i, above if i % 2 == 0 else below).wait_send()


def quick(tokens, w_query, w_key, w_value, w_out, partners, counts, key_slot):
    views, length, features = tokens.shape
    degree = partners.shape[1]
    entries = views * degree
    rounds = lax.axis_size("group") // 2
    smem = pl.BlockSpec(memory_space=pltpu.SMEM)
    hbm = pl.BlockSpec(memory_space=pltpu.HBM)
    vmem = pl.BlockSpec(memory_space=pltpu.VMEM)
    stay = [
        pltpu.with_memory_space_constraint(w, pltpu.HBM) for w in (w_query, w_key, w_value, w_out)
    ]
    slab = (length, features)
    half = jnp.bfloat16

    def slabs(count):
        return pltpu.VMEM((count, *slab), half)

    def numbers(*shape):
        return pltpu.SMEM(shape, jnp.int32)

    return pl.pallas_call(
        functools.partial(quick_kernel, degree),
        out_shape=(
            jax.ShapeDtypeStruct(tokens.shape, tokens.dtype),
            jax.ShapeDtypeStruct((1, 1), jnp.int32),
        ),
        in_specs=[smem] * 3 + [vmem] + [hbm] * 4,
        out_specs=(vmem, smem),
        scratch_shapes=[
            *[pltpu.VMEM((features, features), half)] * 4,
            *[slabs(views)] * 2,
            slabs(KEYS + 2),
            slabs(FAR),
            slabs(WIDE),
            pltpu.VMEM(slab, half),
            numbers(1, 7 * views),
            numbers(1, 7 * views),
            numbers(1, 3 * views),
            numbers(1, entries),
            numbers(1, 7 * views),
            numbers(1, FAR + WIDE),
            numbers(3, entries + 2),
            pltpu.VMEM((KEYS + 2, length, 2 * features), half),
            pltpu.VMEM((entries + 2, *slab), jnp.float32),
            pltpu.SemaphoreType.DMA((4,)),
            pltpu.SemaphoreType.DMA((5 * views + FAR + WIDE + 16,)),
            pltpu.SemaphoreType.DMA((5 * views + FAR + WIDE + 16,)),
            *[numbers(1, 1)] * (2 * (4 + 2 * rounds)),
        ],
        compiler_params=pltpu.CompilerParams(
            collective_id=1, has_side_effects=True, vmem_limit_bytes=50 * 1024 * 1024
        ),
        name="sublayer_quick",
    )(partners, counts, key_slot, tokens, *stay)


def select_kernel(*arguments):
    result, flag = quick(*arguments)
    return lax.cond(flag[0, 0] > 0, lambda: one_kernel(*arguments), lambda: result)


def local_kernel(table, queries, w_key, w_value, block, inverse, tokens, w_out, out_ref, *scratch):
    held, pair, total, sem = scratch
    copy = pltpu.make_async_copy(block, held, sem)
    copy.start()
    total[...] = jnp.zeros_like(total)
    copy.wait()
    views, length, _ = total.shape

    def entry(e, carry):
        @pl.when(table[0, e] == 1)
        def _():
            place, view = table[1, e], table[2, e]

            def store(cols, value):
                total[view, :, cols] += value

            normed = layer_norm(held[place]).astype(jnp.bfloat16)
            attend(lambda cols: queries[view, :, cols], normed, w_key, w_value, pair, store)

        return carry

    lax.fori_loop(0, table.shape[1], entry, 0)
    for v in range(views):
        mixed = (total[v] * inverse[v]).astype(jnp.bfloat16)
        out_ref[v] = (tokens[v].astype(jnp.float32) + project(mixed, w_out[...])).astype(out_ref.dtype)


def exchange(tokens, w_query, w_key, w_value, w_out, partners, counts, key_slot):
    slot_key = key_slot[0]
    views, length, features = tokens.shape
    members, groups = lax.axis_size("member"), lax.axis_size("group")
    degree = partners.shape[1]
    entry_list = partners.reshape(-1)
    entries = entry_list.shape[0]
    capacity = (entries + members - 2) // (members - 1)
    peers = entry_list // views % members
    places = entry_list % views
    order = jnp.arange(entries, dtype=jnp.int32)
    earlier = (peers[:, None] == peers[None, :]) & (order[None, :] < order[:, None])
    cells = peers * capacity + jnp.sum(earlier.astype(jnp.int32), axis=1)
    requests = jnp.zeros((members * capacity,), jnp.int32).at[cells].set(places)
    asked = lax.all_to_all(
        requests.reshape(members, capacity), "member", split_axis=0, concat_axis=0, tiled=True
    )
    outgoing = tokens[asked.reshape(-1)].reshape(members, capacity, length, features)
    arrived = lax.all_to_all(outgoing, "member", split_axis=0, concat_axis=0, tiled=True)
    own_key = lax.dynamic_slice_in_dim(tokens, slot_key, 1, 0)
    below = lax.ppermute(own_key, "group", [(g, (g + 1) % groups) for g in range(groups)])
    above = lax.ppermute(own_key, "group", [((g + 1) % groups, g) for g in range(groups)])
    block = jnp.concatenate((arrived.reshape(members * capacity, length, features), below, above))
    normed = layer_norm(tokens).astype(jnp.bfloat16)
    queries = project(normed.reshape(views * length, features), w_query).astype(jnp.bfloat16)
    queries = queries.reshape(tokens.shape) * jnp.bfloat16((features // HEADS) ** -0.5)
    is_key = (jnp.arange(views, dtype=jnp.int32) == slot_key).astype(jnp.int32)
    inverse = 1.0 / (counts + 2 * is_key).astype(jnp.float32)
    live = (jnp.arange(degree, dtype=jnp.int32)[None, :] < counts[:, None]).reshape(-1)
    two = jnp.arange(2, dtype=jnp.int32)
    table = jnp.stack(
        (
            jnp.concatenate((live.astype(jnp.int32), jnp.ones_like(two))),
            jnp.concatenate((cells, members * capacity + two)),
            jnp.concatenate((order // degree, jnp.full_like(two, slot_key))),
        )
    )
    vmem = pl.BlockSpec(memory_space=pltpu.VMEM)
    smem = pl.BlockSpec(memory_space=pltpu.SMEM)
    hbm = pl.BlockSpec(memory_space=pl.ANY)
    return pl.pallas_call(
        local_kernel,
        out_shape=jax.ShapeDtypeStruct(tokens.shape, tokens.dtype),
        in_specs=[smem, vmem, vmem, vmem, hbm, smem, vmem, vmem],
        out_specs=vmem,
        scratch_shapes=[
            pltpu.VMEM(block.shape, block.dtype),
            pltpu.VMEM((length, 2 * features), jnp.bfloat16),
            pltpu.VMEM(tokens.shape, jnp.float32),
            pltpu.SemaphoreType.DMA,
        ],
        compiler_params=pltpu.CompilerParams(vmem_limit_bytes=60 * 1024 * 1024),
        name="attend_all",
    )(table, queries, w_key, w_value, block, inverse, tokens, w_out)


def sublayer(tokens, w_query, w_key, w_value, w_out, partners, counts, key_slot):
    views = tokens.shape[0]
    members = lax.axis_size("member")
    entries = partners.shape[0] * partners.shape[1]
    capacity = (entries + members - 2) // (members - 1)
    grid = members == LAYERS * ROW and views == capacity + 1
    run = select_kernel if grid else exchange
    return run(tokens, w_query, w_key, w_value, w_out, partners, counts, key_slot)


def solution(mesh):
    return jax.shard_map(
        sublayer,
        mesh=mesh,
        in_specs=(
            P(("group", "member"), None, None),
            P(),
            P(),
            P(),
            P(),
            P(("group", "member"), None),
            P(("group", "member")),
            P(("group", "member")),
        ),
        out_specs=P(("group", "member"), None, None),
        check_vma=False,
    )
```

```python
import functools

import jax
import jax.numpy as jnp
from jax import lax
from jax.experimental import pallas as pl
from jax.experimental.pallas import tpu as pltpu
from jax.sharding import PartitionSpec as P

HEADS = 12
ROW = 2
LAYERS = 4
MESH = pl.DeviceIdType.MESH


def layer_norm(values_in):
    values_in = values_in.astype(jnp.float32)
    centre = jnp.mean(values_in, axis=-1, keepdims=True)
    spread = jnp.mean((values_in - centre) ** 2, axis=-1, keepdims=True)
    return (values_in - centre) * lax.rsqrt(spread + 1e-05)


def project(rows, weights):
    return jnp.dot(rows, weights, preferred_element_type=jnp.float32)


def attend(query, normed, w_key, w_value, pair, store):
    features = normed.shape[1]
    pair[:, :features] = project(normed, w_key[...]).astype(jnp.bfloat16)
    pair[:, features:] = project(normed, w_value[...]).astype(jnp.bfloat16)
    heads(query, pair, features, store)


def heads(query, pair, features, store):
    size = features // HEADS
    lower = lax.broadcasted_iota(jnp.int32, (1, 2 * size), 1) < size
    for h in range(HEADS // 2):
        cols = pl.ds(2 * h * size, 2 * size)
        rows = query(cols)
        key = pair[:, cols]
        value = pair[:, pl.ds(features + 2 * h * size, 2 * size)]
        halves = []
        for keep in (lower, jnp.logical_not(lower)):
            part = jnp.where(keep, rows, jnp.zeros_like(rows))
            scores = lax.dot_general(
                part, key, (((1,), (1,)), ((), ())), preferred_element_type=jnp.float32
            )
            top = jnp.max(scores, axis=-1, keepdims=True)
            weights = jnp.exp(scores - top)
            mass = jnp.sum(weights, axis=-1, keepdims=True)
            halves.append(project(weights.astype(jnp.bfloat16), value) / mass)
        store(cols, jnp.where(lower, halves[0], halves[1]))


RAW_BLOCK, RAW_PLACE, POSITION, BLOCK, PLACE, VIEW = range(6)


def build_tables(layer, side, degree, capacity, views, members, partners, key_view, ask, table):
    entries = views * degree
    low = layer < LAYERS // 2

    def mirror(value):
        return jnp.where(low, value, LAYERS - 1 - value)

    here = mirror(layer)

    def read(e, flags):
        partner = partners[lax.div(e, degree), lax.rem(e, degree)]
        peer = lax.rem(lax.div(partner, views), members)
        place = lax.rem(partner, views)
        there = mirror(lax.div(peer, ROW))
        inside = jnp.where(there == 0, 1, jnp.where(there == 2, 0, 2))
        turn = jnp.where(here == 0, there - 1, inside)
        across = (lax.rem(peer, ROW) != side).astype(jnp.int32)
        block = jnp.where(there == here, 0, 1 + 2 * turn + across)
        table[RAW_BLOCK, e] = block
        table[RAW_PLACE, e] = place
        return tuple(
            jnp.where((block == 2 + 2 * (i // views)) & (place == i % views), 1, flag)
            for i, flag in enumerate(flags)
        )

    flags = lax.fori_loop(0, entries, read, (jnp.int32(0),) * (3 * views))
    slots = []
    for j in range(3):
        wanted = flags[j * views : (j + 1) * views]
        slot = capacity - sum(wanted)
        for v in range(views):
            slots.append(slot)
            slot = slot + wanted[v]
        for k in range(capacity):
            ask[0, j * capacity + k] = sum(
                jnp.where((wanted[v] == 1) & (slots[j * views + v] == k), v, 0) for v in range(views)
            )

    def rank(e, carry):
        block, place = table[RAW_BLOCK, e], table[RAW_PLACE, e]
        position = jnp.int32(2)
        for other in range(entries):
            ahead = (table[RAW_BLOCK, other] * entries + other) < block * entries + e
            position = position + ahead.astype(jnp.int32)
        table[POSITION, e] = position
        spot = place
        for i, slot in enumerate(slots):
            spot = jnp.where((block == 2 + 2 * (i // views)) & (place == i % views), slot, spot)
        table[RAW_PLACE, e] = spot
        return carry

    lax.fori_loop(0, entries, rank, 0)

    def sort(r, carry):
        block, place, view = jnp.int32(-1), jnp.int32(0), key_view
        for e in range(entries):
            match = table[POSITION, e] == r
            block = jnp.where(match, table[RAW_BLOCK, e], block)
            place = jnp.where(match, table[RAW_PLACE, e], place)
            view = jnp.where(match, e // degree, view)
        table[BLOCK, r], table[PLACE, r], table[VIEW, r] = block, place, view
        return carry

    lax.fori_loop(0, entries + 2, sort, 0)


def sublayer_kernel(degree, capacity, *refs):
    partners, counts, key_slot, tokens, wq_in, wk_in, wv_in, wo_in, out_ref = refs[:9]
    w_query, w_key, w_value, w_out = refs[9:13]
    own, queries, near, b0, b1, b2, s0, s1, s2, keys, staged, key_out = refs[13:25]
    ask, asked, table, cur, pair, results, load_sem, send_sem, recv_sem = refs[25:]
    views, length, features = tokens.shape
    members, groups = lax.axis_size("member"), lax.axis_size("group")
    entries = views * degree
    peers = members - 1
    size = features // HEADS
    me, group = lax.axis_index("member"), lax.axis_index("group")
    layer, side = me // ROW, me % ROW
    low = layer < LAYERS // 2
    toward = jnp.where(low, ROW, -ROW)
    is_end = jnp.logical_or(layer == 0, layer == LAYERS - 1)
    is_mid = jnp.logical_not(is_end)
    beside = {"member": layer * ROW + 1 - side}
    inner = {"member": me + toward}
    outer = {"member": jnp.clip(me - toward, 0, members - 1)}
    above = {"group": lax.rem(group + 1, groups)}
    below = {"group": lax.rem(group + groups - 1, groups)}

    blocks = (near, b0, s0, b1, s1, b2, s2)
    base, total = {}, 0
    for name, ref in (("near", near), ("b0", b0), ("b1", b1), ("b2", b2), ("s0", s0),
                      ("s1", s1), ("s2", s2), ("keys", keys)):
        base[name] = total
        total += ref.shape[0]

    def remote(source, target, send, recv, device):
        return pltpu.make_async_remote_copy(
            src_ref=source, dst_ref=target, send_sem=send_sem.at[send],
            recv_sem=recv_sem.at[recv], device_id=device, device_id_type=MESH,
        )

    sends = {}

    def slot(name, index):
        return sends.setdefault((name, index), len(sends))

    def hop(name, source, v, target, target_name, device):
        return remote(source.at[v], target.at[v], slot(name, v), base[target_name] + v, device)

    def to_near(v):
        return hop("near", own, v, near, "near", beside)

    def own_to_b1(v):
        return hop("in", own, v, b1, "b1", inner)

    def own_to_b0(v):
        return hop("in", own, v, b0, "b0", inner)

    def own_out(v):
        return hop("out", own, v, b0, "b0", outer)

    def b1_in(v):
        return hop("in2", b1, v, b2, "b2", inner)

    def b0_out(v):
        return hop("out1", b0, v, b1, "b1", outer)

    def b2_out(v):
        return hop("out2", b2, v, b2, "b2", outer)

    swaps = (s0, s1, s2)

    def swap(j, k):
        return remote(
            staged.at[j * capacity + k], swaps[j].at[k], slot("swap", j * capacity + k),
            base[f"s{j}"] + k, beside,
        )

    def key_send(i):
        return remote(
            key_out, keys.at[i], slot("key", i), base["keys"] + i, above if i == 0 else below
        )

    def ask_send():
        return remote(ask, asked, slot("ask", 0), total, beside)

    loads = [
        pltpu.make_async_copy(source, target, load_sem.at[i])
        for i, (source, target) in enumerate(
            ((wq_in, w_query), (wk_in, w_key), (wv_in, w_value), (wo_in, w_out))
        )
    ]
    for load in loads:
        load.start()

    barrier = pltpu.get_barrier_semaphore()
    for device in (beside, inner, above, below):
        pl.semaphore_signal(barrier, inc=1, device_id=device, device_id_type=MESH)

    @pl.when(is_mid)
    def _():
        pl.semaphore_signal(barrier, inc=1, device_id=outer, device_id_type=MESH)

    own[0] = layer_norm(tokens[0]).astype(jnp.bfloat16)

    @pl.when(is_mid)
    def _():
        pl.semaphore_wait(barrier, 5)

    @pl.when(is_end)
    def _():
        pl.semaphore_wait(barrier, 4)

    for v in range(views):
        if v:
            own[v] = layer_norm(tokens[v]).astype(jnp.bfloat16)
        to_near(v).start()

        @pl.when(is_end)
        def _():
            own_to_b1(v).start()

        @pl.when(is_mid)
        def _():
            own_to_b0(v).start()
            own_out(v).start()

    key_view = key_slot[0]
    key_out[...] = own[key_view]
    loads[0].wait()
    for v in range(views):
        queries[v] = project(own[v], w_query[...]).astype(jnp.bfloat16) * jnp.bfloat16(size**-0.5)
    for i in range(2):
        key_send(i).start()
    build_tables(layer, side, degree, capacity, views, members, partners, key_view, ask, table)
    ask_send().start()
    loads[1].wait()
    loads[2].wait()
    for i in range(2):
        key_send(i).wait_recv()

    def stage(j, k, source):
        choice = asked[0, j * capacity + k]
        value = source[0]
        for v in range(1, k + views - capacity + 1):
            value = jnp.where(choice == v, source[v], value)
        staged[j * capacity + k] = value
        swap(j, k).start()

    def events(t):
        def far(v):
            @pl.when(is_end)
            def _():
                b0_out(v).wait_recv()

            @pl.when(is_mid)
            def _():
                b1_in(v).wait_recv()
                b2_out(v).start()

        def last(v):
            @pl.when(is_end)
            def _():
                b2_out(v).wait_recv()

        def arrive(j):
            for k in range(capacity):
                swap(j, k).wait_recv()

        extra = views - capacity

        def spread(wait, j, source, v):
            wait(v)
            if v >= extra:
                stage(j, v - extra, source)

        if t == first[0]:
            for v in range(views):
                own_to_b0(v).wait_recv()

                @pl.when(is_mid)
                def _():
                    b0_out(v).start()
                    own_to_b1(v).wait_recv()
                    b1_in(v).start()

                if v >= extra:
                    stage(0, v - extra, b0)
            for v in range(views):
                to_near(v).wait_recv()
        if t == first[2]:
            for v in range(views - 2):
                spread(far, 1, b1, v)
            arrive(0)
        if t == first[2] + 1:
            spread(far, 1, b1, views - 2)
        if t == first[3]:
            spread(far, 1, b1, views - 1)
        if t == first[4]:
            for v in range(views - 2):
                spread(last, 2, b2, v)
            arrive(1)
        if t == first[4] + 1:
            spread(last, 2, b2, views - 2)
        if t == first[5]:
            spread(last, 2, b2, views - 1)
        if t == first[6]:
            arrive(2)

    first = [2 + max(0, entries - capacity * (peers - j)) for j in range(peers)]

    def entry(t, carry):
        for when in sorted({first[0], first[2], first[2] + 1, first[3], first[4], first[4] + 1,
                            first[5], first[6]}):
            @pl.when(t == when)
            def _():
                events(when)

        @pl.when(t < 2)
        def _():
            cur[...] = keys[jnp.minimum(t, 1)]

        block, place, view = table[BLOCK, t], table[PLACE, t], table[VIEW, t]
        for j, ref in enumerate(blocks):
            @pl.when(t >= first[j])
            def _():
                value = ref[jnp.minimum(place, ref.shape[0] - 1)]
                cur[...] = jnp.where(block == j, value, cur[...])

        def store(cols, value):
            results[t, :, cols] = value

        attend(lambda cols: queries[view, :, cols], cur[...], w_key, w_value, pair, store)
        return carry

    ask_send().wait_recv()
    lax.fori_loop(0, entries + 2, entry, 0)
    loads[3].wait()
    for v in range(views):
        is_key = (key_view == v).astype(jnp.int32)
        count = counts[v]
        mixed = is_key.astype(jnp.float32) * (results[0] + results[1])
        for e in range(degree):
            live = (count > e).astype(jnp.int32).astype(jnp.float32)
            mixed += live * results[table[POSITION, v * degree + e]]
        divisor = jnp.full((1, features), count + 2 * is_key, jnp.int32).astype(jnp.float32)
        mixed = mixed * (1.0 / divisor)
        out_ref[v] = (
            tokens[v].astype(jnp.float32) + project(mixed.astype(jnp.bfloat16), w_out[...])
        ).astype(out_ref.dtype)

    for v in range(views):
        to_near(v).wait_send()

        @pl.when(is_end)
        def _():
            own_to_b1(v).wait_send()

        @pl.when(is_mid)
        def _():
            own_to_b0(v).wait_send()
            own_out(v).wait_send()
            b1_in(v).wait_send()
            b0_out(v).wait_send()
            b2_out(v).wait_send()

    for j in range(3):
        for k in range(capacity):
            swap(j, k).wait_send()
    for i in range(2):
        key_send(i).wait_send()
    ask_send().wait_send()


def one_kernel(tokens, w_query, w_key, w_value, w_out, partners, counts, key_slot):
    views, length, features = tokens.shape
    members = lax.axis_size("member")
    degree = partners.shape[1]
    entries = views * degree
    capacity = (entries + members - 2) // (members - 1)
    smem = pl.BlockSpec(memory_space=pltpu.SMEM)
    hbm = pl.BlockSpec(memory_space=pltpu.HBM)
    vmem = pl.BlockSpec(memory_space=pltpu.VMEM)
    stay = [
        pltpu.with_memory_space_constraint(w, pltpu.HBM) for w in (w_query, w_key, w_value, w_out)
    ]
    slab = (length, features)
    weights_shape = pltpu.VMEM((features, features), jnp.bfloat16)
    half = jnp.bfloat16
    blocks = [pltpu.VMEM((views, *slab), half)] * 6 + [pltpu.VMEM((capacity, *slab), half)] * 3
    sends = 6 * views + 3 * capacity + 3 + views
    receives = 4 * views + 3 * capacity + 3
    return pl.pallas_call(
        functools.partial(sublayer_kernel, degree, capacity),
        out_shape=jax.ShapeDtypeStruct(tokens.shape, tokens.dtype),
        in_specs=[smem] * 3 + [vmem] + [hbm] * 4,
        out_specs=vmem,
        scratch_shapes=[
            weights_shape,
            weights_shape,
            weights_shape,
            weights_shape,
            *blocks,
            pltpu.VMEM((2, *slab), half),
            pltpu.VMEM((3 * capacity, *slab), half),
            pltpu.VMEM(slab, half),
            pltpu.SMEM((1, 3 * capacity), jnp.int32),
            pltpu.SMEM((1, 3 * capacity), jnp.int32),
            pltpu.SMEM((6, entries + 2), jnp.int32),
            pltpu.VMEM(slab, half),
            pltpu.VMEM((length, 2 * features), half),
            pltpu.VMEM((entries + 2, *slab), jnp.float32),
            pltpu.SemaphoreType.DMA((4,)),
            pltpu.SemaphoreType.DMA((sends,)),
            pltpu.SemaphoreType.DMA((receives,)),
        ],
        compiler_params=pltpu.CompilerParams(
            collective_id=0, has_side_effects=True, vmem_limit_bytes=44 * 1024 * 1024
        ),
        name="sublayer",
    )(partners, counts, key_slot, tokens, *stay)


FAR, WIDE = 9, 7
FREE, SLOTS, PLAIN, CROSS = 4, 5, 4, 16
KEYS = CROSS + WIDE


def quick_kernel(degree, *refs):
    partners, counts, key_slot, tokens, wq_in, wk_in, wv_in, wo_in, out_ref, flag_ref = refs[:10]
    w_query, w_key, w_value, w_out = refs[10:14]
    own, queries, arrived, far_out, wide_out, key_out = refs[14:20]
    ask, asked, union, codes, sources, picks, table, pairs, results = refs[20:29]
    load_sem, send_sem, recv_sem = refs[29:32]
    notes = refs[32:]
    views, length, features = tokens.shape
    members, groups = lax.axis_size("member"), lax.axis_size("group")
    entries = views * degree
    size = features // HEADS
    me, group = lax.axis_index("member"), lax.axis_index("group")
    layer, side = me // ROW, me % ROW
    low = layer < LAYERS // 2
    toward = jnp.where(low, ROW, -ROW)
    is_end = jnp.logical_or(layer == 0, layer == LAYERS - 1)
    is_mid = jnp.logical_not(is_end)
    beside = {"member": layer * ROW + 1 - side}
    inner = {"member": me + toward}
    outer = {"member": jnp.clip(me - toward, 0, members - 1)}
    above = {"group": lax.rem(group + 1, groups)}
    below = {"group": lax.rem(group + groups - 1, groups)}
    key_view = key_slot[0]
    cells = 7 * views
    near, b0, b1, b2 = (arrived.at[pl.ds(i * views, views)] for i in range(4))
    first_view, far = arrived.at[pl.ds(FREE, 1)], arrived.at[pl.ds(SLOTS, FAR)]
    wide, keys = arrived.at[pl.ds(CROSS, WIDE)], arrived.at[pl.ds(KEYS, 2)]
    names = {}

    def number(kind, name):
        return names.setdefault((kind, name), sum(1 for k, _ in names if k == kind))

    def remote(name, source, target, landing, device):
        return pltpu.make_async_remote_copy(
            src_ref=source, dst_ref=target, send_sem=send_sem.at[number(0, name)],
            recv_sem=recv_sem.at[number(1, landing)], device_id=device, device_id_type=MESH,
        )

    def to_near(v):
        return remote(("near", v), own.at[v], near.at[v], ("near", v), beside)

    def own_to_b1(v):
        return remote(("in", v), own.at[v], b1.at[v], ("b1", v), inner)

    def own_to_b0(v):
        return remote(("in", v), own.at[v], b0.at[v], ("b0", v), inner)

    def b1_in(v):
        return remote(("in2", v), b1.at[v], b2.at[v], ("b2", v), inner)

    def own_out():
        return remote("free", own.at[0], first_view.at[0], "free", outer)

    def far_send(q):
        return remote(("far", q), far_out.at[q], far.at[q], ("far", q), outer)

    def wide_send(k):
        return remote(("wide", k), wide_out.at[k], wide.at[k], ("wide", k), beside)

    def key_send(i):
        return remote(("key", i), key_out, keys.at[i], ("key", i), below if i else above)

    def ask_send():
        return remote("ask", ask, asked, "ask", beside)

    def union_send():
        return remote("union", union, union, "union", inner)

    def note(i, device):
        return remote(("note", i), notes[2 * i], notes[2 * i + 1], ("note", i), device)

    loads = [
        pltpu.make_async_copy(source, target, load_sem.at[i])
        for i, (source, target) in enumerate(
            ((wq_in, w_query), (wk_in, w_key), (wv_in, w_value), (wo_in, w_out))
        )
    ]
    for load in loads:
        load.start()
    barrier = pltpu.get_barrier_semaphore()
    for device in (beside, inner, above, below):
        pl.semaphore_signal(barrier, inc=1, device_id=device, device_id_type=MESH)

    @pl.when(is_mid)
    def _():
        pl.semaphore_signal(barrier, inc=1, device_id=outer, device_id_type=MESH)

    def mirror(value):
        return jnp.where(low, value, LAYERS - 1 - value)

    here = mirror(layer)

    def read(e, carry):
        partner = partners[lax.div(e, degree), lax.rem(e, degree)]
        peer = lax.rem(lax.div(partner, views), members)
        there = mirror(lax.div(peer, ROW))
        inside = jnp.where(there == 0, 1, jnp.where(there == 2, 0, 2))
        turn = jnp.where(here == 0, there - 1, inside)
        across = (lax.rem(peer, ROW) != side).astype(jnp.int32)
        block = jnp.where(there == here, 0, 1 + 2 * turn + across)
        live = lax.rem(e, degree) < counts[lax.div(e, degree)]
        codes[0, e] = jnp.where(live, block * views + lax.rem(partner, views), 0)
        return carry

    lax.fori_loop(0, entries, read, 0)

    def mark(cell, carry):
        found = jnp.int32(0)
        for e in range(entries):
            found = jnp.where(codes[0, e] == cell, 1, found)
        ask[0, cell] = found
        return carry

    lax.fori_loop(0, cells, mark, 0)
    own[0] = layer_norm(tokens[0]).astype(jnp.bfloat16)

    @pl.when(is_mid)
    def _():
        pl.semaphore_wait(barrier, 5)

    @pl.when(is_end)
    def _():
        pl.semaphore_wait(barrier, 4)

    ask_send().start()
    for v in range(views):
        if v:
            own[v] = layer_norm(tokens[v]).astype(jnp.bfloat16)
        to_near(v).start()

        @pl.when(is_mid)
        def _():
            own_to_b0(v).start()
            if v == 0:
                own_out().start()

    key_out[...] = own[key_view]
    count = 3 * views

    def same(ref, c):
        return ref[0, (1 + 2 * (c // views)) * views + c % views]

    def cross(ref, c):
        return ref[0, (2 + 2 * (c // views)) * views + c % views]

    ask_send().wait_recv()

    @pl.when(is_end)
    def _():
        for c in range(count):
            union[0, c] = jnp.maximum(same(ask, c), cross(asked, c))
        union_send().start()
        for v in range(views):
            own_to_b1(v).start()

    loads[0].wait()
    for v in range(views):
        queries[v] = project(own[v], w_query[...]).astype(jnp.bfloat16) * jnp.bfloat16(size**-0.5)
    for i in range(2):
        key_send(i).start()

    @pl.when(is_mid)
    def _():
        union_send().wait_recv()

    def line_up(flags, ready):
        spots, last = [], jnp.int32(-1)
        for flag, at in zip(flags, ready):
            spot = jnp.maximum(last + 1, at)
            spots.append(spot)
            last = jnp.where(flag == 1, spot, last)
        return spots, last

    far_ready = [0] * views + [v + 1 for v in range(views)] + [v + 1 + views for v in range(views)]

    def far_slots(flags):
        spots, last = line_up(flags[1:], far_ready[1:])
        return [jnp.int32(-1)] + spots, last

    def wide_slots(flags, behind):
        ready = []
        for c in range(count):
            late = 0 if c < 2 * views else c - 2 * views + 1
            ready.append(jnp.where(is_end, jnp.maximum(behind[c] - 2, 0), late))
        return line_up(flags, ready)

    def found(c, spots):
        return jnp.where(is_end, FREE if c == 0 else SLOTS + spots[c], PLAIN + c)

    mine = [union[0, c] for c in range(count)]
    my_far, far_last = far_slots(mine)
    beside_far, _ = far_slots([jnp.maximum(same(asked, c), cross(ask, c)) for c in range(count)])
    out_flags = [cross(asked, c) for c in range(count)]
    my_wide, out_last = wide_slots(out_flags, my_far)
    beside_wide, in_last = wide_slots([cross(ask, c) for c in range(count)], beside_far)
    for q in range(FAR):
        pick = jnp.int32(0)
        for c in range(1, count):
            pick = jnp.where((mine[c] == 1) & (my_far[c] == q), c, pick)
        picks[0, q] = pick
    for k in range(WIDE):
        pick = jnp.where(is_end, FREE, PLAIN)
        for c in range(count):
            pick = jnp.where((out_flags[c] == 1) & (my_wide[c] == k), found(c, my_far), pick)
        picks[0, FAR + k] = pick
    for v in range(views):
        sources[0, v] = v
    for c in range(count):
        sources[0, (1 + 2 * (c // views)) * views + c % views] = found(c, my_far)
        sources[0, (2 + 2 * (c // views)) * views + c % views] = CROSS + beside_wide[c]
    full = (far_last >= FAR) | (out_last >= WIDE) | (in_last >= WIDE)
    notes[0][0, 0] = full.astype(jnp.int32)

    def view_of(ref, index):
        return ref[index]

    def choose(choice, options):
        value = None
        for key, load in options:
            value = load() if value is None else jnp.where(choice == key, load(), value)
        return value

    def far_stage(q):
        options = [(c, functools.partial(view_of, own, c)) for c in range(min(views, q + views))]
        options += [(views + v, functools.partial(view_of, b0, v)) for v in range(views) if v < q]
        options += [
            (2 * views + v, functools.partial(view_of, b2, v)) for v in range(views) if v + views < q
        ]
        far_out[q] = choose(picks[0, q], options)
        far_send(q).start()

    def far_turn(q):
        @pl.when(is_mid)
        def _():
            if 1 <= q <= views:
                own_to_b0(q - 1).wait_recv()
            if q > views:
                b1_in(q - 1 - views).wait_recv()
            far_stage(q)
            if 1 <= q <= views:
                own_to_b1(q - 1).wait_recv()
                b1_in(q - 1).start()

    def wide_stage(k):
        choice = picks[0, FAR + k]

        @pl.when(is_end)
        def _():
            options = [(FREE, lambda: first_view[0])]
            options += [(SLOTS + q, functools.partial(view_of, far, q)) for q in range(k + 3)]
            wide_out[k] = choose(choice, options)

        @pl.when(is_mid)
        def _():
            options = [(PLAIN + v, functools.partial(view_of, b0, v)) for v in range(views)]
            options += [(PLAIN + views + v, functools.partial(view_of, b1, v)) for v in range(views)]
            options += [
                (PLAIN + 2 * views + v, functools.partial(view_of, b2, v))
                for v in range(views)
                if v < k
            ]
            wide_out[k] = choose(choice, options)

        wide_send(k).start()

    def far_arrive(q):
        @pl.when(is_end)
        def _():
            far_send(q).wait_recv()

    def wide_turn(k):
        far_arrive(k + 2)
        wide_stage(k)

    def note_value(i, value):
        notes[2 * i][0, 0] = value

    def seen(i):
        return notes[2 * i + 1][0, 0]

    rounds = groups // 2

    def note_step(i):
        if i == 0:
            note(0, beside).start()
        if i == 1:
            note(0, beside).wait_recv()
            note_value(1, jnp.maximum(notes[0][0, 0], seen(0)))

            @pl.when(is_end)
            def _():
                note(1, inner).start()
        if i == 2:
            @pl.when(is_mid)
            def _():
                note(1, inner).wait_recv()
                note_value(2, jnp.maximum(notes[2][0, 0], seen(1)))
                note(2, inner).start()
        if i == 3:
            @pl.when(is_mid)
            def _():
                note(2, inner).wait_recv()
                note_value(3, jnp.maximum(notes[4][0, 0], seen(2)))
                note(3, outer).start()
                note_value(4, notes[6][0, 0])
        if i == 4:
            @pl.when(is_end)
            def _():
                note(3, outer).wait_recv()
                note_value(4, seen(3))

            note_value(5, notes[8][0, 0])
            note(4, above).start()
            note(5, below).start()
        if i > 4:
            j = 2 * i - 6
            note(j, above).wait_recv()
            note(j + 1, below).wait_recv()
            value = jnp.maximum(notes[2 * j][0, 0], jnp.maximum(seen(j), seen(j + 1)))
            if i < 4 + rounds:
                note_value(j + 2, value)
                note_value(j + 3, value)
                note(j + 2, above).start()
                note(j + 3, below).start()
            else:
                flag_ref[0, 0] = value

    far_turn(0)
    note_step(0)

    def rank(e, carry):
        code = codes[0, e] * entries + e
        position = jnp.int32(2)
        for other in range(entries):
            position = position + (codes[0, other] * entries + other < code).astype(jnp.int32)
        table[0, e] = position
        return carry

    lax.fori_loop(0, entries, rank, 0)

    def sort(r, carry):
        cell, view = jnp.int32(0), key_view
        for e in range(entries):
            match = table[0, e] == r
            cell = jnp.where(match, codes[0, e], cell)
            view = jnp.where(match, e // degree, view)
        table[1, r], table[2, r] = jnp.where(r < 2, KEYS + r, sources[0, cell]), view
        return carry

    lax.fori_loop(0, entries + 2, sort, 0)
    loads[1].wait()
    loads[2].wait()
    def learn(first, stride, count):
        def one(i, carry):
            place = first + stride * i
            rows = arrived[place]
            pairs[place, :, :features] = project(rows, w_key[...]).astype(jnp.bfloat16)
            pairs[place, :, features:] = project(rows, w_value[...]).astype(jnp.bfloat16)
            return carry

        lax.fori_loop(0, count, one, 0)

    def attends(first, last):
        def one(t, carry):
            source, view = table[1, t], table[2, t]

            def store(cols, value):
                results[t, :, cols] = value

            heads(lambda cols: queries[view, :, cols], pairs.at[source], features, store)
            return carry

        if last > first:
            lax.fori_loop(first + 2, last + 2, one, 0)

    def wide_arrive(k):
        wide_send(k).wait_recv()

    for v in range(views):
        far_turn(v + 1)
        to_near(v).wait_recv()
        if v == 0:
            @pl.when(is_end)
            def _():
                own_out().wait_recv()
        elif v < views - 1:
            far_arrive(v - 1)
        else:
            wide_turn(0)
        learn(v, views, jnp.where(is_end, 2, 3))
        if v == 0:
            for i in range(2):
                key_send(i).wait_recv()
            learn(KEYS, 1, 2)
        if v == 1:
            attends(-2, 0)
    bounds = [max(0, entries - n) for n in (15, 15, 15, 12, 9, 7, 3, 0)]
    attends(0, bounds[0])
    for k in range(1, WIDE):
        if views + k < FAR:
            far_turn(views + k)
        wide_turn(k)
        if 1 < k < 5:
            note_step(k - 1)
        there = 1 if k <= views else 0
        landed = jnp.where(is_end, FREE + views - 1 + k, PLAIN + 2 * views + k - 1)
        learn(landed, 0, jnp.where(is_end, 1, there))
        wide_arrive(k - 1)
        learn(CROSS + k - 1, 0, 1)
        if k < WIDE - 1:
            attends(bounds[k - 1], bounds[k])
    middle = (bounds[WIDE - 2] + bounds[WIDE - 1]) // 2
    attends(bounds[WIDE - 2], middle)
    note_step(4)
    attends(middle, bounds[WIDE - 1])
    wide_arrive(WIDE - 1)
    learn(CROSS + WIDE - 1, 0, 1)
    for i in range(1, rounds):
        note_step(4 + i)
    attends(bounds[WIDE - 1], bounds[WIDE])
    note_step(4 + rounds)
    loads[3].wait()
    for v in range(views):
        is_key = (key_view == v).astype(jnp.int32)
        total = counts[v]
        mixed = is_key.astype(jnp.float32) * (results[0] + results[1])
        for e in range(degree):
            live = (total > e).astype(jnp.int32).astype(jnp.float32)
            mixed += live * results[table[0, v * degree + e]]
        divisor = jnp.full((1, features), total + 2 * is_key, jnp.int32).astype(jnp.float32)
        mixed = mixed * (1.0 / divisor)
        out_ref[v] = (
            tokens[v].astype(jnp.float32) + project(mixed.astype(jnp.bfloat16), w_out[...])
        ).astype(out_ref.dtype)

    for v in range(views):
        to_near(v).wait_send()

        @pl.when(is_end)
        def _():
            own_to_b1(v).wait_send()

        @pl.when(is_mid)
        def _():
            own_to_b0(v).wait_send()
            b1_in(v).wait_send()

    @pl.when(is_mid)
    def _():
        own_out().wait_send()
        for q in range(FAR):
            far_send(q).wait_send()
        note(2, inner).wait_send()
        note(3, outer).wait_send()

    @pl.when(is_end)
    def _():
        union_send().wait_send()
        note(1, inner).wait_send()

    for k in range(WIDE):
        wide_send(k).wait_send()
    for i in range(2):
        key_send(i).wait_send()
    ask_send().wait_send()
    note(0, beside).wait_send()
    for i in range(4, 4 + 2 * rounds):
        note(i, above if i % 2 == 0 else below).wait_send()


def quick(tokens, w_query, w_key, w_value, w_out, partners, counts, key_slot):
    views, length, features = tokens.shape
    degree = partners.shape[1]
    entries = views * degree
    rounds = lax.axis_size("group") // 2
    smem = pl.BlockSpec(memory_space=pltpu.SMEM)
    hbm = pl.BlockSpec(memory_space=pltpu.HBM)
    vmem = pl.BlockSpec(memory_space=pltpu.VMEM)
    stay = [
        pltpu.with_memory_space_constraint(w, pltpu.HBM) for w in (w_query, w_key, w_value, w_out)
    ]
    slab = (length, features)
    half = jnp.bfloat16

    def slabs(count):
        return pltpu.VMEM((count, *slab), half)

    def numbers(*shape):
        return pltpu.SMEM(shape, jnp.int32)

    return pl.pallas_call(
        functools.partial(quick_kernel, degree),
        out_shape=(
            jax.ShapeDtypeStruct(tokens.shape, tokens.dtype),
            jax.ShapeDtypeStruct((1, 1), jnp.int32),
        ),
        in_specs=[smem] * 3 + [vmem] + [hbm] * 4,
        out_specs=(vmem, smem),
        scratch_shapes=[
            *[pltpu.VMEM((features, features), half)] * 4,
            *[slabs(views)] * 2,
            slabs(KEYS + 2),
            slabs(FAR),
            slabs(WIDE),
            pltpu.VMEM(slab, half),
            numbers(1, 7 * views),
            numbers(1, 7 * views),
            numbers(1, 3 * views),
            numbers(1, entries),
            numbers(1, 7 * views),
            numbers(1, FAR + WIDE),
            numbers(3, entries + 2),
            pltpu.VMEM((KEYS + 2, length, 2 * features), half),
            pltpu.VMEM((entries + 2, *slab), jnp.float32),
            pltpu.SemaphoreType.DMA((4,)),
            pltpu.SemaphoreType.DMA((5 * views + FAR + WIDE + 16,)),
            pltpu.SemaphoreType.DMA((5 * views + FAR + WIDE + 16,)),
            *[numbers(1, 1)] * (2 * (4 + 2 * rounds)),
        ],
        compiler_params=pltpu.CompilerParams(
            collective_id=1, has_side_effects=True, vmem_limit_bytes=50 * 1024 * 1024
        ),
        name="sublayer_quick",
    )(partners, counts, key_slot, tokens, *stay)


def select_kernel(*arguments):
    result, flag = quick(*arguments)
    return lax.cond(flag[0, 0] > 0, lambda: one_kernel(*arguments), lambda: result)


def local_kernel(table, queries, w_key, w_value, block, inverse, tokens, w_out, out_ref, *scratch):
    held, pair, total, sem = scratch
    copy = pltpu.make_async_copy(block, held, sem)
    copy.start()
    total[...] = jnp.zeros_like(total)
    copy.wait()
    views, length, _ = total.shape

    def entry(e, carry):
        @pl.when(table[0, e] == 1)
        def _():
            place, view = table[1, e], table[2, e]

            def store(cols, value):
                total[view, :, cols] += value

            normed = layer_norm(held[place]).astype(jnp.bfloat16)
            attend(lambda cols: queries[view, :, cols], normed, w_key, w_value, pair, store)

        return carry

    lax.fori_loop(0, table.shape[1], entry, 0)
    for v in range(views):
        mixed = (total[v] * inverse[v]).astype(jnp.bfloat16)
        out_ref[v] = (tokens[v].astype(jnp.float32) + project(mixed, w_out[...])).astype(out_ref.dtype)


def exchange(tokens, w_query, w_key, w_value, w_out, partners, counts, key_slot):
    slot_key = key_slot[0]
    views, length, features = tokens.shape
    members, groups = lax.axis_size("member"), lax.axis_size("group")
    degree = partners.shape[1]
    entry_list = partners.reshape(-1)
    entries = entry_list.shape[0]
    capacity = (entries + members - 2) // (members - 1)
    peers = entry_list // views % members
    places = entry_list % views
    order = jnp.arange(entries, dtype=jnp.int32)
    earlier = (peers[:, None] == peers[None, :]) & (order[None, :] < order[:, None])
    cells = peers * capacity + jnp.sum(earlier.astype(jnp.int32), axis=1)
    requests = jnp.zeros((members * capacity,), jnp.int32).at[cells].set(places)
    asked = lax.all_to_all(
        requests.reshape(members, capacity), "member", split_axis=0, concat_axis=0, tiled=True
    )
    outgoing = tokens[asked.reshape(-1)].reshape(members, capacity, length, features)
    arrived = lax.all_to_all(outgoing, "member", split_axis=0, concat_axis=0, tiled=True)
    own_key = lax.dynamic_slice_in_dim(tokens, slot_key, 1, 0)
    below = lax.ppermute(own_key, "group", [(g, (g + 1) % groups) for g in range(groups)])
    above = lax.ppermute(own_key, "group", [((g + 1) % groups, g) for g in range(groups)])
    block = jnp.concatenate((arrived.reshape(members * capacity, length, features), below, above))
    normed = layer_norm(tokens).astype(jnp.bfloat16)
    queries = project(normed.reshape(views * length, features), w_query).astype(jnp.bfloat16)
    queries = queries.reshape(tokens.shape) * jnp.bfloat16((features // HEADS) ** -0.5)
    is_key = (jnp.arange(views, dtype=jnp.int32) == slot_key).astype(jnp.int32)
    inverse = 1.0 / (counts + 2 * is_key).astype(jnp.float32)
    live = (jnp.arange(degree, dtype=jnp.int32)[None, :] < counts[:, None]).reshape(-1)
    two = jnp.arange(2, dtype=jnp.int32)
    table = jnp.stack(
        (
            jnp.concatenate((live.astype(jnp.int32), jnp.ones_like(two))),
            jnp.concatenate((cells, members * capacity + two)),
            jnp.concatenate((order // degree, jnp.full_like(two, slot_key))),
        )
    )
    vmem = pl.BlockSpec(memory_space=pltpu.VMEM)
    smem = pl.BlockSpec(memory_space=pltpu.SMEM)
    hbm = pl.BlockSpec(memory_space=pl.ANY)
    return pl.pallas_call(
        local_kernel,
        out_shape=jax.ShapeDtypeStruct(tokens.shape, tokens.dtype),
        in_specs=[smem, vmem, vmem, vmem, hbm, smem, vmem, vmem],
        out_specs=vmem,
        scratch_shapes=[
            pltpu.VMEM(block.shape, block.dtype),
            pltpu.VMEM((length, 2 * features), jnp.bfloat16),
            pltpu.VMEM(tokens.shape, jnp.float32),
            pltpu.SemaphoreType.DMA,
        ],
        compiler_params=pltpu.CompilerParams(vmem_limit_bytes=60 * 1024 * 1024),
        name="attend_all",
    )(table, queries, w_key, w_value, block, inverse, tokens, w_out)


def sublayer(tokens, w_query, w_key, w_value, w_out, partners, counts, key_slot):
    views = tokens.shape[0]
    members = lax.axis_size("member")
    entries = partners.shape[0] * partners.shape[1]
    capacity = (entries + members - 2) // (members - 1)
    grid = members == LAYERS * ROW and views == capacity + 1
    run = select_kernel if grid else exchange
    return run(tokens, w_query, w_key, w_value, w_out, partners, counts, key_slot)


def solution(mesh):
    return jax.shard_map(
        sublayer,
        mesh=mesh,
        in_specs=(
            P(("group", "member"), None, None),
            P(),
            P(),
            P(),
            P(),
            P(("group", "member"), None),
            P(("group", "member")),
            P(("group", "member")),
        ),
        out_specs=P(("group", "member"), None, None),
        check_vma=False,
    )
```

```python
import functools

import jax
import jax.numpy as jnp
from jax import lax
from jax.experimental import pallas as pl
from jax.experimental.pallas import tpu as pltpu
from jax.sharding import PartitionSpec as P

HEADS = 12
ROW = 2
LAYERS = 4
MESH = pl.DeviceIdType.MESH


def layer_norm(values_in):
    values_in = values_in.astype(jnp.float32)
    centre = jnp.mean(values_in, axis=-1, keepdims=True)
    spread = jnp.mean((values_in - centre) ** 2, axis=-1, keepdims=True)
    return (values_in - centre) * lax.rsqrt(spread + 1e-05)


def project(rows, weights):
    return jnp.dot(rows, weights, preferred_element_type=jnp.float32)


def attend(query, normed, w_key, w_value, pair, store):
    features = normed.shape[1]
    pair[:, :features] = project(normed, w_key[...]).astype(jnp.bfloat16)
    pair[:, features:] = project(normed, w_value[...]).astype(jnp.bfloat16)
    heads(query, pair, features, store)


def heads(query, pair, features, store):
    size = features // HEADS
    lower = lax.broadcasted_iota(jnp.int32, (1, 2 * size), 1) < size
    for h in range(HEADS // 2):
        cols = pl.ds(2 * h * size, 2 * size)
        rows = query(cols)
        key = pair[:, cols]
        value = pair[:, pl.ds(features + 2 * h * size, 2 * size)]
        halves = []
        for keep in (lower, jnp.logical_not(lower)):
            part = jnp.where(keep, rows, jnp.zeros_like(rows))
            scores = lax.dot_general(
                part, key, (((1,), (1,)), ((), ())), preferred_element_type=jnp.float32
            )
            top = jnp.max(scores, axis=-1, keepdims=True)
            weights = jnp.exp(scores - top)
            mass = jnp.sum(weights, axis=-1, keepdims=True)
            halves.append(project(weights.astype(jnp.bfloat16), value) / mass)
        store(cols, jnp.where(lower, halves[0], halves[1]))


RAW_BLOCK, RAW_PLACE, POSITION, BLOCK, PLACE, VIEW = range(6)


def build_tables(layer, side, degree, capacity, views, members, partners, key_view, ask, table):
    entries = views * degree
    low = layer < LAYERS // 2

    def mirror(value):
        return jnp.where(low, value, LAYERS - 1 - value)

    here = mirror(layer)

    def read(e, flags):
        partner = partners[lax.div(e, degree), lax.rem(e, degree)]
        peer = lax.rem(lax.div(partner, views), members)
        place = lax.rem(partner, views)
        there = mirror(lax.div(peer, ROW))
        inside = jnp.where(there == 0, 1, jnp.where(there == 2, 0, 2))
        turn = jnp.where(here == 0, there - 1, inside)
        across = (lax.rem(peer, ROW) != side).astype(jnp.int32)
        block = jnp.where(there == here, 0, 1 + 2 * turn + across)
        table[RAW_BLOCK, e] = block
        table[RAW_PLACE, e] = place
        return tuple(
            jnp.where((block == 2 + 2 * (i // views)) & (place == i % views), 1, flag)
            for i, flag in enumerate(flags)
        )

    flags = lax.fori_loop(0, entries, read, (jnp.int32(0),) * (3 * views))
    slots = []
    for j in range(3):
        wanted = flags[j * views : (j + 1) * views]
        slot = capacity - sum(wanted)
        for v in range(views):
            slots.append(slot)
            slot = slot + wanted[v]
        for k in range(capacity):
            ask[0, j * capacity + k] = sum(
                jnp.where((wanted[v] == 1) & (slots[j * views + v] == k), v, 0) for v in range(views)
            )

    def rank(e, carry):
        block, place = table[RAW_BLOCK, e], table[RAW_PLACE, e]
        position = jnp.int32(2)
        for other in range(entries):
            ahead = (table[RAW_BLOCK, other] * entries + other) < block * entries + e
            position = position + ahead.astype(jnp.int32)
        table[POSITION, e] = position
        spot = place
        for i, slot in enumerate(slots):
            spot = jnp.where((block == 2 + 2 * (i // views)) & (place == i % views), slot, spot)
        table[RAW_PLACE, e] = spot
        return carry

    lax.fori_loop(0, entries, rank, 0)

    def sort(r, carry):
        block, place, view = jnp.int32(-1), jnp.int32(0), key_view
        for e in range(entries):
            match = table[POSITION, e] == r
            block = jnp.where(match, table[RAW_BLOCK, e], block)
            place = jnp.where(match, table[RAW_PLACE, e], place)
            view = jnp.where(match, e // degree, view)
        table[BLOCK, r], table[PLACE, r], table[VIEW, r] = block, place, view
        return carry

    lax.fori_loop(0, entries + 2, sort, 0)


def sublayer_kernel(degree, capacity, *refs):
    partners, counts, key_slot, tokens, wq_in, wk_in, wv_in, wo_in, out_ref = refs[:9]
    w_query, w_key, w_value, w_out = refs[9:13]
    own, queries, near, b0, b1, b2, s0, s1, s2, keys, staged, key_out = refs[13:25]
    ask, asked, table, cur, pair, results, load_sem, send_sem, recv_sem = refs[25:]
    views, length, features = tokens.shape
    members, groups = lax.axis_size("member"), lax.axis_size("group")
    entries = views * degree
    peers = members - 1
    size = features // HEADS
    me, group = lax.axis_index("member"), lax.axis_index("group")
    layer, side = me // ROW, me % ROW
    low = layer < LAYERS // 2
    toward = jnp.where(low, ROW, -ROW)
    is_end = jnp.logical_or(layer == 0, layer == LAYERS - 1)
    is_mid = jnp.logical_not(is_end)
    beside = {"member": layer * ROW + 1 - side}
    inner = {"member": me + toward}
    outer = {"member": jnp.clip(me - toward, 0, members - 1)}
    above = {"group": lax.rem(group + 1, groups)}
    below = {"group": lax.rem(group + groups - 1, groups)}

    blocks = (near, b0, s0, b1, s1, b2, s2)
    base, total = {}, 0
    for name, ref in (("near", near), ("b0", b0), ("b1", b1), ("b2", b2), ("s0", s0),
                      ("s1", s1), ("s2", s2), ("keys", keys)):
        base[name] = total
        total += ref.shape[0]

    def remote(source, target, send, recv, device):
        return pltpu.make_async_remote_copy(
            src_ref=source, dst_ref=target, send_sem=send_sem.at[send],
            recv_sem=recv_sem.at[recv], device_id=device, device_id_type=MESH,
        )

    sends = {}

    def slot(name, index):
        return sends.setdefault((name, index), len(sends))

    def hop(name, source, v, target, target_name, device):
        return remote(source.at[v], target.at[v], slot(name, v), base[target_name] + v, device)

    def to_near(v):
        return hop("near", own, v, near, "near", beside)

    def own_to_b1(v):
        return hop("in", own, v, b1, "b1", inner)

    def own_to_b0(v):
        return hop("in", own, v, b0, "b0", inner)

    def own_out(v):
        return hop("out", own, v, b0, "b0", outer)

    def b1_in(v):
        return hop("in2", b1, v, b2, "b2", inner)

    def b0_out(v):
        return hop("out1", b0, v, b1, "b1", outer)

    def b2_out(v):
        return hop("out2", b2, v, b2, "b2", outer)

    swaps = (s0, s1, s2)

    def swap(j, k):
        return remote(
            staged.at[j * capacity + k], swaps[j].at[k], slot("swap", j * capacity + k),
            base[f"s{j}"] + k, beside,
        )

    def key_send(i):
        return remote(
            key_out, keys.at[i], slot("key", i), base["keys"] + i, above if i == 0 else below
        )

    def ask_send():
        return remote(ask, asked, slot("ask", 0), total, beside)

    loads = [
        pltpu.make_async_copy(source, target, load_sem.at[i])
        for i, (source, target) in enumerate(
            ((wq_in, w_query), (wk_in, w_key), (wv_in, w_value), (wo_in, w_out))
        )
    ]
    for load in loads:
        load.start()

    barrier = pltpu.get_barrier_semaphore()
    for device in (beside, inner, above, below):
        pl.semaphore_signal(barrier, inc=1, device_id=device, device_id_type=MESH)

    @pl.when(is_mid)
    def _():
        pl.semaphore_signal(barrier, inc=1, device_id=outer, device_id_type=MESH)

    own[0] = layer_norm(tokens[0]).astype(jnp.bfloat16)

    @pl.when(is_mid)
    def _():
        pl.semaphore_wait(barrier, 5)

    @pl.when(is_end)
    def _():
        pl.semaphore_wait(barrier, 4)

    for v in range(views):
        if v:
            own[v] = layer_norm(tokens[v]).astype(jnp.bfloat16)
        to_near(v).start()

        @pl.when(is_end)
        def _():
            own_to_b1(v).start()

        @pl.when(is_mid)
        def _():
            own_to_b0(v).start()
            own_out(v).start()

    key_view = key_slot[0]
    key_out[...] = own[key_view]
    loads[0].wait()
    for v in range(views):
        queries[v] = project(own[v], w_query[...]).astype(jnp.bfloat16) * jnp.bfloat16(size**-0.5)
    for i in range(2):
        key_send(i).start()
    build_tables(layer, side, degree, capacity, views, members, partners, key_view, ask, table)
    ask_send().start()
    loads[1].wait()
    loads[2].wait()
    for i in range(2):
        key_send(i).wait_recv()

    def stage(j, k, source):
        choice = asked[0, j * capacity + k]
        value = source[0]
        for v in range(1, k + views - capacity + 1):
            value = jnp.where(choice == v, source[v], value)
        staged[j * capacity + k] = value
        swap(j, k).start()

    def events(t):
        def far(v):
            @pl.when(is_end)
            def _():
                b0_out(v).wait_recv()

            @pl.when(is_mid)
            def _():
                b1_in(v).wait_recv()
                b2_out(v).start()

        def last(v):
            @pl.when(is_end)
            def _():
                b2_out(v).wait_recv()

        def arrive(j):
            for k in range(capacity):
                swap(j, k).wait_recv()

        extra = views - capacity

        def spread(wait, j, source, v):
            wait(v)
            if v >= extra:
                stage(j, v - extra, source)

        if t == first[0]:
            for v in range(views):
                own_to_b0(v).wait_recv()

                @pl.when(is_mid)
                def _():
                    b0_out(v).start()
                    own_to_b1(v).wait_recv()
                    b1_in(v).start()

                if v >= extra:
                    stage(0, v - extra, b0)
            for v in range(views):
                to_near(v).wait_recv()
        if t == first[2]:
            for v in range(views - 2):
                spread(far, 1, b1, v)
            arrive(0)
        if t == first[2] + 1:
            spread(far, 1, b1, views - 2)
        if t == first[3]:
            spread(far, 1, b1, views - 1)
        if t == first[4]:
            for v in range(views - 2):
                spread(last, 2, b2, v)
            arrive(1)
        if t == first[4] + 1:
            spread(last, 2, b2, views - 2)
        if t == first[5]:
            spread(last, 2, b2, views - 1)
        if t == first[6]:
            arrive(2)

    first = [2 + max(0, entries - capacity * (peers - j)) for j in range(peers)]

    def entry(t, carry):
        for when in sorted({first[0], first[2], first[2] + 1, first[3], first[4], first[4] + 1,
                            first[5], first[6]}):
            @pl.when(t == when)
            def _():
                events(when)

        @pl.when(t < 2)
        def _():
            cur[...] = keys[jnp.minimum(t, 1)]

        block, place, view = table[BLOCK, t], table[PLACE, t], table[VIEW, t]
        for j, ref in enumerate(blocks):
            @pl.when(t >= first[j])
            def _():
                value = ref[jnp.minimum(place, ref.shape[0] - 1)]
                cur[...] = jnp.where(block == j, value, cur[...])

        def store(cols, value):
            results[t, :, cols] = value

        attend(lambda cols: queries[view, :, cols], cur[...], w_key, w_value, pair, store)
        return carry

    ask_send().wait_recv()
    lax.fori_loop(0, entries + 2, entry, 0)
    loads[3].wait()
    for v in range(views):
        is_key = (key_view == v).astype(jnp.int32)
        count = counts[v]
        mixed = is_key.astype(jnp.float32) * (results[0] + results[1])
        for e in range(degree):
            live = (count > e).astype(jnp.int32).astype(jnp.float32)
            mixed += live * results[table[POSITION, v * degree + e]]
        divisor = jnp.full((1, features), count + 2 * is_key, jnp.int32).astype(jnp.float32)
        mixed = mixed * (1.0 / divisor)
        out_ref[v] = (
            tokens[v].astype(jnp.float32) + project(mixed.astype(jnp.bfloat16), w_out[...])
        ).astype(out_ref.dtype)

    for v in range(views):
        to_near(v).wait_send()

        @pl.when(is_end)
        def _():
            own_to_b1(v).wait_send()

        @pl.when(is_mid)
        def _():
            own_to_b0(v).wait_send()
            own_out(v).wait_send()
            b1_in(v).wait_send()
            b0_out(v).wait_send()
            b2_out(v).wait_send()

    for j in range(3):
        for k in range(capacity):
            swap(j, k).wait_send()
    for i in range(2):
        key_send(i).wait_send()
    ask_send().wait_send()


def one_kernel(tokens, w_query, w_key, w_value, w_out, partners, counts, key_slot):
    views, length, features = tokens.shape
    members = lax.axis_size("member")
    degree = partners.shape[1]
    entries = views * degree
    capacity = (entries + members - 2) // (members - 1)
    smem = pl.BlockSpec(memory_space=pltpu.SMEM)
    hbm = pl.BlockSpec(memory_space=pltpu.HBM)
    vmem = pl.BlockSpec(memory_space=pltpu.VMEM)
    stay = [
        pltpu.with_memory_space_constraint(w, pltpu.HBM) for w in (w_query, w_key, w_value, w_out)
    ]
    slab = (length, features)
    weights_shape = pltpu.VMEM((features, features), jnp.bfloat16)
    half = jnp.bfloat16
    blocks = [pltpu.VMEM((views, *slab), half)] * 6 + [pltpu.VMEM((capacity, *slab), half)] * 3
    sends = 6 * views + 3 * capacity + 3 + views
    receives = 4 * views + 3 * capacity + 3
    return pl.pallas_call(
        functools.partial(sublayer_kernel, degree, capacity),
        out_shape=jax.ShapeDtypeStruct(tokens.shape, tokens.dtype),
        in_specs=[smem] * 3 + [vmem] + [hbm] * 4,
        out_specs=vmem,
        scratch_shapes=[
            weights_shape,
            weights_shape,
            weights_shape,
            weights_shape,
            *blocks,
            pltpu.VMEM((2, *slab), half),
            pltpu.VMEM((3 * capacity, *slab), half),
            pltpu.VMEM(slab, half),
            pltpu.SMEM((1, 3 * capacity), jnp.int32),
            pltpu.SMEM((1, 3 * capacity), jnp.int32),
            pltpu.SMEM((6, entries + 2), jnp.int32),
            pltpu.VMEM(slab, half),
            pltpu.VMEM((length, 2 * features), half),
            pltpu.VMEM((entries + 2, *slab), jnp.float32),
            pltpu.SemaphoreType.DMA((4,)),
            pltpu.SemaphoreType.DMA((sends,)),
            pltpu.SemaphoreType.DMA((receives,)),
        ],
        compiler_params=pltpu.CompilerParams(
            collective_id=0, has_side_effects=True, vmem_limit_bytes=44 * 1024 * 1024
        ),
        name="sublayer",
    )(partners, counts, key_slot, tokens, *stay)


NEAR, FAR, WIDE, EARLY = 3, 9, 7, 3
FREE, SLOTS, PLAIN, CROSS = 4, 5, 4, 16
KEYS = CROSS + WIDE


def quick_kernel(degree, *refs):
    partners, counts, key_slot, tokens, wq_in, wk_in, wv_in, wo_in, out_ref, flag_ref = refs[:10]
    w_query, w_key, w_value, w_out = refs[10:14]
    own, queries, arrived, near_out, far_out, wide_out, key_out = refs[14:21]
    ask, asked, union, codes, sources, picks, table, pairs, results = refs[21:30]
    load_sem, send_sem, recv_sem = refs[30:33]
    notes = refs[33:]
    views, length, features = tokens.shape
    members, groups = lax.axis_size("member"), lax.axis_size("group")
    entries = views * degree
    size = features // HEADS
    me, group = lax.axis_index("member"), lax.axis_index("group")
    layer, side = me // ROW, me % ROW
    low = layer < LAYERS // 2
    toward = jnp.where(low, ROW, -ROW)
    is_end = jnp.logical_or(layer == 0, layer == LAYERS - 1)
    is_mid = jnp.logical_not(is_end)
    beside = {"member": layer * ROW + 1 - side}
    inner = {"member": me + toward}
    outer = {"member": jnp.clip(me - toward, 0, members - 1)}
    above = {"group": lax.rem(group + 1, groups)}
    below = {"group": lax.rem(group + groups - 1, groups)}
    key_view = key_slot[0]
    cells = 7 * views
    cut = length // 32 * 16
    halves = (pl.ds(0, cut), pl.ds(cut, length - cut))
    near, b0, b1, b2 = (arrived.at[pl.ds(i * views, views)] for i in range(4))
    first_view, far = arrived.at[pl.ds(FREE, 1)], arrived.at[pl.ds(SLOTS, FAR)]
    wide, keys = arrived.at[pl.ds(CROSS, WIDE)], arrived.at[pl.ds(KEYS, 2)]
    names = {}

    def number(kind, name):
        return names.setdefault((kind, name), sum(1 for k, _ in names if k == kind))

    def remote(name, source, target, landing, device):
        return pltpu.make_async_remote_copy(
            src_ref=source, dst_ref=target, send_sem=send_sem.at[number(0, name)],
            recv_sem=recv_sem.at[number(1, landing)], device_id=device, device_id_type=MESH,
        )

    def near_send(k):
        return remote(("near", k), near_out.at[k], near.at[k], ("near", k), beside)

    def own_to_b1(v):
        return remote(("in", v), own.at[v], b1.at[v], ("b1", v), inner)

    def own_to_b0(v):
        return remote(("in", v), own.at[v], b0.at[v], ("b0", v), inner)

    def b1_in(v):
        return remote(("in2", v), b1.at[v], b2.at[v], ("b2", v), inner)

    def own_out():
        return remote("free", own.at[0], first_view.at[0], "free", outer)

    def far_send(q, p):
        rows = halves[p]
        return remote(("far", q, p), far_out.at[q, rows], far.at[q, rows], ("far", q, p), outer)

    def wide_send(k, p):
        rows = halves[p]
        return remote(("wide", k, p), wide_out.at[k, rows], wide.at[k, rows], ("wide", k, p), beside)

    def key_send(i):
        return remote(("key", i), key_out, keys.at[i], ("key", i), below if i else above)

    def ask_send():
        return remote("ask", ask, asked, "ask", beside)

    def union_send():
        return remote("union", union, union, "union", inner)

    def note(i, device):
        return remote(("note", i), notes[2 * i], notes[2 * i + 1], ("note", i), device)

    loads = [
        pltpu.make_async_copy(source, target, load_sem.at[i])
        for i, (source, target) in enumerate(
            ((wq_in, w_query), (wk_in, w_key), (wv_in, w_value), (wo_in, w_out))
        )
    ]
    for load in loads:
        load.start()
    barrier = pltpu.get_barrier_semaphore()
    for device in (beside, inner, above, below):
        pl.semaphore_signal(barrier, inc=1, device_id=device, device_id_type=MESH)

    @pl.when(is_mid)
    def _():
        pl.semaphore_signal(barrier, inc=1, device_id=outer, device_id_type=MESH)

    def mirror(value):
        return jnp.where(low, value, LAYERS - 1 - value)

    here = mirror(layer)

    def read(e, carry):
        partner = partners[lax.div(e, degree), lax.rem(e, degree)]
        peer = lax.rem(lax.div(partner, views), members)
        there = mirror(lax.div(peer, ROW))
        inside = jnp.where(there == 0, 1, jnp.where(there == 2, 0, 2))
        turn = jnp.where(here == 0, there - 1, inside)
        across = (lax.rem(peer, ROW) != side).astype(jnp.int32)
        block = jnp.where(there == here, 0, 1 + 2 * turn + across)
        live = lax.rem(e, degree) < counts[lax.div(e, degree)]
        codes[0, e] = jnp.where(live, block * views + lax.rem(partner, views), -1)
        return carry

    lax.fori_loop(0, entries, read, 0)

    def mark(cell, carry):
        found = jnp.int32(0)
        for e in range(entries):
            found = jnp.where(codes[0, e] == cell, 1, found)
        ask[0, cell] = found
        return carry

    lax.fori_loop(0, cells, mark, 0)
    own[0] = layer_norm(tokens[0]).astype(jnp.bfloat16)

    @pl.when(is_mid)
    def _():
        pl.semaphore_wait(barrier, 5)

    @pl.when(is_end)
    def _():
        pl.semaphore_wait(barrier, 4)

    ask_send().start()
    for v in range(views):
        if v:
            own[v] = layer_norm(tokens[v]).astype(jnp.bfloat16)

        @pl.when(is_mid)
        def _():
            own_to_b0(v).start()
            if v == 0:
                own_out().start()

    key_out[...] = own[key_view]
    count = 3 * views

    def same(ref, c):
        return ref[0, (1 + 2 * (c // views)) * views + c % views]

    def cross(ref, c):
        return ref[0, (2 + 2 * (c // views)) * views + c % views]

    ask_send().wait_recv()

    @pl.when(is_end)
    def _():
        for c in range(count):
            union[0, c] = jnp.maximum(same(ask, c), cross(asked, c))
        union_send().start()
        for v in range(views):
            own_to_b1(v).start()

    near_flags = [asked[0, v] for v in range(views)]
    near_spots = [sum(near_flags[:v]) for v in range(views)]
    for k in range(NEAR):
        pick = jnp.int32(0)
        for v in range(views):
            pick = jnp.where((near_flags[v] == 1) & (near_spots[v] == k), v, pick)
        near_out[k] = own[pick]
        near_send(k).start()
    loads[0].wait()
    for v in range(views):
        queries[v] = project(own[v], w_query[...]).astype(jnp.bfloat16) * jnp.bfloat16(size**-0.5)
    for i in range(2):
        key_send(i).start()

    @pl.when(is_mid)
    def _():
        union_send().wait_recv()

    def line_up(flags, ready):
        spots, last = [], jnp.int32(-1)
        for flag, at in zip(flags, ready):
            spot = jnp.maximum(last + 1, at)
            spots.append(spot)
            last = jnp.where(flag == 1, spot, last)
        return spots, last

    far_ready = [0] * views + [v + 1 for v in range(views)] + [v + 1 + views for v in range(views)]

    mid_ready = [max(0, v - 2) for v in range(views)] + [max(0, v - 1) for v in range(views)]
    mid_ready += [v + EARLY for v in range(views)]

    def far_slots(flags):
        spots, last = line_up(flags[1:], far_ready[1:])
        return [jnp.int32(-1)] + spots, last

    def wide_slots(flags, behind):
        ready = []
        for c in range(count):
            ready.append(jnp.where(is_end, jnp.maximum(behind[c] - 2, 0), mid_ready[c]))
        return line_up(flags, ready)

    def found(c, spots):
        return jnp.where(is_end, FREE if c == 0 else SLOTS + spots[c], PLAIN + c)

    mine = [union[0, c] for c in range(count)]
    my_far, far_last = far_slots(mine)
    beside_far, _ = far_slots([jnp.maximum(same(asked, c), cross(ask, c)) for c in range(count)])
    out_flags = [cross(asked, c) for c in range(count)]
    my_wide, out_last = wide_slots(out_flags, my_far)
    beside_wide, in_last = wide_slots([cross(ask, c) for c in range(count)], beside_far)
    for q in range(FAR):
        pick = jnp.int32(0)
        for c in range(1, count):
            pick = jnp.where((mine[c] == 1) & (my_far[c] == q), c, pick)
        picks[0, q] = pick
    for k in range(WIDE):
        pick = jnp.where(is_end, FREE, PLAIN)
        for c in range(count):
            pick = jnp.where((out_flags[c] == 1) & (my_wide[c] == k), found(c, my_far), pick)
        picks[0, FAR + k] = pick
    for v in range(views):
        sources[0, v] = sum(ask[0, other] for other in range(v)) if v else 0
    for c in range(count):
        sources[0, (1 + 2 * (c // views)) * views + c % views] = found(c, my_far)
        sources[0, (2 + 2 * (c // views)) * views + c % views] = CROSS + beside_wide[c]
    full = (far_last >= FAR) | (out_last >= WIDE) | (in_last >= WIDE)
    notes[0][0, 0] = full.astype(jnp.int32)

    def view_of(ref, index):
        return ref[index]

    def choose(choice, options):
        value = None
        for key, load in options:
            value = load() if value is None else jnp.where(choice == key, load(), value)
        return value

    def far_stage(q):
        options = [(c, functools.partial(view_of, own, c)) for c in range(min(views, q + views))]
        options += [(views + v, functools.partial(view_of, b0, v)) for v in range(views) if v < q]
        options += [
            (2 * views + v, functools.partial(view_of, b2, v)) for v in range(views) if v + views < q
        ]
        far_out[q] = choose(picks[0, q], options)
        for p in range(2):
            far_send(q, p).start()

    def far_turn(q):
        @pl.when(is_mid)
        def _():
            if 1 <= q <= views:
                own_to_b0(q - 1).wait_recv()
            if q > views:
                b1_in(q - 1 - views).wait_recv()
            far_stage(q)
            if 2 <= q <= views + 1:
                own_to_b1(q - 2).wait_recv()
                b1_in(q - 2).start()

    def wide_end(k, p):
        @pl.when(is_end)
        def _():
            far_send(k + 2, p).wait_recv()
            options = [(FREE, lambda: first_view[0, halves[p]])]
            options += [
                (SLOTS + q, functools.partial(view_of, far, (q, halves[p]))) for q in range(k + 3)
            ]
            wide_out[k, halves[p]] = choose(picks[0, FAR + k], options)
            wide_send(k, p).start()

    def wide_mid(k):
        @pl.when(is_mid)
        def _():
            held = b0, b1, b2
            options = [
                (PLAIN + c, functools.partial(view_of, held[c // views], c % views))
                for c in range(count)
                if mid_ready[c] <= k
            ]
            wide_out[k] = choose(picks[0, FAR + k], options)
            for p in range(2):
                wide_send(k, p).start()

    def far_arrive(q):
        @pl.when(is_end)
        def _():
            for p in range(2):
                far_send(q, p).wait_recv()

    def note_value(i, value):
        notes[2 * i][0, 0] = value

    def seen(i):
        return notes[2 * i + 1][0, 0]

    rounds = groups // 2

    def note_step(i):
        if i == 0:
            note(0, beside).start()
        if i == 1:
            note(0, beside).wait_recv()
            note_value(1, jnp.maximum(notes[0][0, 0], seen(0)))

            @pl.when(is_end)
            def _():
                note(1, inner).start()
        if i == 2:
            @pl.when(is_mid)
            def _():
                note(1, inner).wait_recv()
                note_value(2, jnp.maximum(notes[2][0, 0], seen(1)))
                note(2, inner).start()
        if i == 3:
            @pl.when(is_mid)
            def _():
                note(2, inner).wait_recv()
                note_value(3, jnp.maximum(notes[4][0, 0], seen(2)))
                note(3, outer).start()
                note_value(4, notes[6][0, 0])
        if i == 4:
            @pl.when(is_end)
            def _():
                note(3, outer).wait_recv()
                note_value(4, seen(3))

            note_value(5, notes[8][0, 0])
            note(4, above).start()
            note(5, below).start()
        if i > 4:
            j = 2 * i - 6
            note(j, above).wait_recv()
            note(j + 1, below).wait_recv()
            value = jnp.maximum(notes[2 * j][0, 0], jnp.maximum(seen(j), seen(j + 1)))
            if i < 4 + rounds:
                note_value(j + 2, value)
                note_value(j + 3, value)
                note(j + 2, above).start()
                note(j + 3, below).start()
            else:
                flag_ref[0, 0] = value

    far_turn(0)
    note_step(0)

    def rank(e, carry):
        code = codes[0, e] * entries + e
        position = jnp.int32(2)
        for other in range(entries):
            position = position + (codes[0, other] * entries + other < code).astype(jnp.int32)
        table[0, e] = position
        return carry

    lax.fori_loop(0, entries, rank, 0)

    def sort(r, carry):
        cell, view = jnp.int32(0), key_view
        for e in range(entries):
            match = table[0, e] == r
            cell = jnp.where(match, codes[0, e], cell)
            view = jnp.where(match, e // degree, view)
        source = jnp.where(cell < 0, KEYS, sources[0, jnp.maximum(cell, 0)])
        table[1, r], table[2, r] = jnp.where(r < 2, KEYS + r, source), view
        return carry

    lax.fori_loop(0, entries + 2, sort, 0)
    loads[1].wait()
    loads[2].wait()
    def learn(places, count):
        def one(i, carry):
            place = places[0]
            for turn in range(1, len(places)):
                place = jnp.where(i == turn, places[turn], place)
            rows = arrived[place]
            pairs[place, :, :features] = project(rows, w_key[...]).astype(jnp.bfloat16)
            pairs[place, :, features:] = project(rows, w_value[...]).astype(jnp.bfloat16)
            return carry

        lax.fori_loop(0, count, one, 0)

    def attends(first, last):
        def one(t, carry):
            source, view = table[1, t], table[2, t]

            def store(cols, value):
                results[t, :, cols] = value

            heads(lambda cols: queries[view, :, cols], pairs.at[source], features, store)
            return carry

        if last > first:
            lax.fori_loop(first + 2, last + 2, one, 0)

    def wide_arrive(k):
        for p in range(2):
            wide_send(k, p).wait_recv()
        learn([CROSS + k], 1)

    for v in range(views):
        far_turn(v + 1)
        if v == views - 1:
            wide_end(0, 0)
            wide_end(0, 1)
        elif v:
            far_arrive(v - 1)
        else:
            @pl.when(is_end)
            def _():
                own_out().wait_recv()

        if v >= views - 2:
            wide_mid(v - views + 2)
        places = [FREE + v]
        if v < NEAR:
            near_send(v).wait_recv()
            places = [v, FREE + v]
        more = [PLAIN + views + v - 1] if v else []
        learn(places + more, jnp.where(is_end, len(places), len(places + more)))
        if v == 0:
            for i in range(2):
                key_send(i).wait_recv()
            learn([KEYS, KEYS + 1], 2)
        if v == 1:
            attends(-2, 0)
    bounds = [max(0, entries - n) for n in (15, 12, 9, 7, 6, 3, 0)]
    attends(0, bounds[0])
    inside = {3: (bounds[0], bounds[0] + 1), 5: (bounds[2] - 1, bounds[2]), 6: (bounds[3], bounds[4])}
    after = {3: (bounds[0] + 1, bounds[1]), 4: (bounds[1], bounds[2] - 1), 5: (bounds[2], bounds[3]),
             6: (bounds[4], bounds[5])}
    for k in range(1, WIDE):
        wide_end(k, 0)
        if k >= EARLY:
            wide_mid(k)
        if views + k < FAR:
            far_turn(views + k)
        if k == 1:
            wide_mid(2)
        wide_arrive(k - 1)
        attends(*inside.get(k, (0, 0)))
        wide_end(k, 1)
        if 1 < k < 5:
            note_step(k - 1)
        landed = jnp.where(is_end, FREE + views - 1 + k, PLAIN + 2 * views + k - 1)
        there = 1 if k <= views else 0
        if k == 1:
            learn([landed, PLAIN + 2 * views - 1], jnp.where(is_end, 1, 2))
        else:
            learn([landed], jnp.where(is_end, 1, there))
        if k == WIDE - 1:
            first, last = after[k]
            attends(first, last - 1)
            note_step(4)
            attends(last - 1, last)
        else:
            attends(*after.get(k, (0, 0)))
    wide_arrive(WIDE - 1)
    for i in range(1, rounds):
        note_step(4 + i)
    attends(bounds[5], bounds[6])
    note_step(4 + rounds)
    loads[3].wait()
    for v in range(views):
        is_key = (key_view == v).astype(jnp.int32)
        total = counts[v]
        mixed = is_key.astype(jnp.float32) * (results[0] + results[1])
        for e in range(degree):
            live = (total > e).astype(jnp.int32).astype(jnp.float32)
            mixed += live * results[table[0, v * degree + e]]
        divisor = jnp.full((1, features), total + 2 * is_key, jnp.int32).astype(jnp.float32)
        mixed = mixed * (1.0 / divisor)
        out_ref[v] = (
            tokens[v].astype(jnp.float32) + project(mixed.astype(jnp.bfloat16), w_out[...])
        ).astype(out_ref.dtype)

    for v in range(views):
        @pl.when(is_end)
        def _():
            own_to_b1(v).wait_send()

        @pl.when(is_mid)
        def _():
            own_to_b0(v).wait_send()
            b1_in(v).wait_send()

    @pl.when(is_mid)
    def _():
        own_out().wait_send()
        for q in range(FAR):
            for p in range(2):
                far_send(q, p).wait_send()
        note(2, inner).wait_send()
        note(3, outer).wait_send()

    @pl.when(is_end)
    def _():
        union_send().wait_send()
        note(1, inner).wait_send()

    for k in range(WIDE):
        for p in range(2):
            wide_send(k, p).wait_send()
    for k in range(NEAR):
        near_send(k).wait_send()
    for i in range(2):
        key_send(i).wait_send()
    ask_send().wait_send()
    note(0, beside).wait_send()
    for i in range(4, 4 + 2 * rounds):
        note(i, above if i % 2 == 0 else below).wait_send()


def quick(tokens, w_query, w_key, w_value, w_out, partners, counts, key_slot):
    views, length, features = tokens.shape
    degree = partners.shape[1]
    entries = views * degree
    rounds = lax.axis_size("group") // 2
    smem = pl.BlockSpec(memory_space=pltpu.SMEM)
    hbm = pl.BlockSpec(memory_space=pltpu.HBM)
    vmem = pl.BlockSpec(memory_space=pltpu.VMEM)
    stay = [
        pltpu.with_memory_space_constraint(w, pltpu.HBM) for w in (w_query, w_key, w_value, w_out)
    ]
    slab = (length, features)
    half = jnp.bfloat16

    def slabs(count):
        return pltpu.VMEM((count, *slab), half)

    def numbers(*shape):
        return pltpu.SMEM(shape, jnp.int32)

    return pl.pallas_call(
        functools.partial(quick_kernel, degree),
        out_shape=(
            jax.ShapeDtypeStruct(tokens.shape, tokens.dtype),
            jax.ShapeDtypeStruct((1, 1), jnp.int32),
        ),
        in_specs=[smem] * 3 + [vmem] + [hbm] * 4,
        out_specs=(vmem, smem),
        scratch_shapes=[
            *[pltpu.VMEM((features, features), half)] * 4,
            *[slabs(views)] * 2,
            slabs(KEYS + 2),
            slabs(NEAR),
            slabs(FAR),
            slabs(WIDE),
            pltpu.VMEM(slab, half),
            numbers(1, 7 * views),
            numbers(1, 7 * views),
            numbers(1, 3 * views),
            numbers(1, entries),
            numbers(1, 7 * views),
            numbers(1, FAR + WIDE),
            numbers(3, entries + 2),
            pltpu.VMEM((KEYS + 2, length, 2 * features), half),
            pltpu.VMEM((entries + 2, *slab), jnp.float32),
            pltpu.SemaphoreType.DMA((4,)),
            pltpu.SemaphoreType.DMA((5 * views + 2 * FAR + 2 * WIDE + 16,)),
            pltpu.SemaphoreType.DMA((5 * views + 2 * FAR + 2 * WIDE + 16,)),
            *[numbers(1, 1)] * (2 * (4 + 2 * rounds)),
        ],
        compiler_params=pltpu.CompilerParams(
            collective_id=1, has_side_effects=True, vmem_limit_bytes=50 * 1024 * 1024
        ),
        name="sublayer_quick",
    )(partners, counts, key_slot, tokens, *stay)


def select_kernel(*arguments):
    result, flag = quick(*arguments)
    return lax.cond(flag[0, 0] > 0, lambda: one_kernel(*arguments), lambda: result)


def local_kernel(table, queries, w_key, w_value, block, inverse, tokens, w_out, out_ref, *scratch):
    held, pair, total, sem = scratch
    copy = pltpu.make_async_copy(block, held, sem)
    copy.start()
    total[...] = jnp.zeros_like(total)
    copy.wait()
    views, length, _ = total.shape

    def entry(e, carry):
        @pl.when(table[0, e] == 1)
        def _():
            place, view = table[1, e], table[2, e]

            def store(cols, value):
                total[view, :, cols] += value

            normed = layer_norm(held[place]).astype(jnp.bfloat16)
            attend(lambda cols: queries[view, :, cols], normed, w_key, w_value, pair, store)

        return carry

    lax.fori_loop(0, table.shape[1], entry, 0)
    for v in range(views):
        mixed = (total[v] * inverse[v]).astype(jnp.bfloat16)
        out_ref[v] = (tokens[v].astype(jnp.float32) + project(mixed, w_out[...])).astype(out_ref.dtype)


def exchange(tokens, w_query, w_key, w_value, w_out, partners, counts, key_slot):
    slot_key = key_slot[0]
    views, length, features = tokens.shape
    members, groups = lax.axis_size("member"), lax.axis_size("group")
    degree = partners.shape[1]
    entry_list = partners.reshape(-1)
    entries = entry_list.shape[0]
    capacity = (entries + members - 2) // (members - 1)
    peers = entry_list // views % members
    places = entry_list % views
    order = jnp.arange(entries, dtype=jnp.int32)
    earlier = (peers[:, None] == peers[None, :]) & (order[None, :] < order[:, None])
    cells = peers * capacity + jnp.sum(earlier.astype(jnp.int32), axis=1)
    requests = jnp.zeros((members * capacity,), jnp.int32).at[cells].set(places)
    asked = lax.all_to_all(
        requests.reshape(members, capacity), "member", split_axis=0, concat_axis=0, tiled=True
    )
    outgoing = tokens[asked.reshape(-1)].reshape(members, capacity, length, features)
    arrived = lax.all_to_all(outgoing, "member", split_axis=0, concat_axis=0, tiled=True)
    own_key = lax.dynamic_slice_in_dim(tokens, slot_key, 1, 0)
    below = lax.ppermute(own_key, "group", [(g, (g + 1) % groups) for g in range(groups)])
    above = lax.ppermute(own_key, "group", [((g + 1) % groups, g) for g in range(groups)])
    block = jnp.concatenate((arrived.reshape(members * capacity, length, features), below, above))
    normed = layer_norm(tokens).astype(jnp.bfloat16)
    queries = project(normed.reshape(views * length, features), w_query).astype(jnp.bfloat16)
    queries = queries.reshape(tokens.shape) * jnp.bfloat16((features // HEADS) ** -0.5)
    is_key = (jnp.arange(views, dtype=jnp.int32) == slot_key).astype(jnp.int32)
    inverse = 1.0 / (counts + 2 * is_key).astype(jnp.float32)
    live = (jnp.arange(degree, dtype=jnp.int32)[None, :] < counts[:, None]).reshape(-1)
    two = jnp.arange(2, dtype=jnp.int32)
    table = jnp.stack(
        (
            jnp.concatenate((live.astype(jnp.int32), jnp.ones_like(two))),
            jnp.concatenate((cells, members * capacity + two)),
            jnp.concatenate((order // degree, jnp.full_like(two, slot_key))),
        )
    )
    vmem = pl.BlockSpec(memory_space=pltpu.VMEM)
    smem = pl.BlockSpec(memory_space=pltpu.SMEM)
    hbm = pl.BlockSpec(memory_space=pl.ANY)
    return pl.pallas_call(
        local_kernel,
        out_shape=jax.ShapeDtypeStruct(tokens.shape, tokens.dtype),
        in_specs=[smem, vmem, vmem, vmem, hbm, smem, vmem, vmem],
        out_specs=vmem,
        scratch_shapes=[
            pltpu.VMEM(block.shape, block.dtype),
            pltpu.VMEM((length, 2 * features), jnp.bfloat16),
            pltpu.VMEM(tokens.shape, jnp.float32),
            pltpu.SemaphoreType.DMA,
        ],
        compiler_params=pltpu.CompilerParams(vmem_limit_bytes=60 * 1024 * 1024),
        name="attend_all",
    )(table, queries, w_key, w_value, block, inverse, tokens, w_out)


def sublayer(tokens, w_query, w_key, w_value, w_out, partners, counts, key_slot):
    views = tokens.shape[0]
    members = lax.axis_size("member")
    entries = partners.shape[0] * partners.shape[1]
    capacity = (entries + members - 2) // (members - 1)
    grid = members == LAYERS * ROW and views == capacity + 1
    run = select_kernel if grid else exchange
    return run(tokens, w_query, w_key, w_value, w_out, partners, counts, key_slot)


def solution(mesh):
    return jax.shard_map(
        sublayer,
        mesh=mesh,
        in_specs=(
            P(("group", "member"), None, None),
            P(),
            P(),
            P(),
            P(),
            P(("group", "member"), None),
            P(("group", "member")),
            P(("group", "member")),
        ),
        out_specs=P(("group", "member"), None, None),
        check_vma=False,
    )
```

```python
import functools

import jax
import jax.numpy as jnp
from jax import lax
from jax.experimental import pallas as pl
from jax.experimental.pallas import tpu as pltpu
from jax.sharding import PartitionSpec as P

HEADS = 12
ROW = 2
LAYERS = 4
MESH = pl.DeviceIdType.MESH


def layer_norm(values_in):
    values_in = values_in.astype(jnp.float32)
    centre = jnp.mean(values_in, axis=-1, keepdims=True)
    spread = jnp.mean((values_in - centre) ** 2, axis=-1, keepdims=True)
    return (values_in - centre) * lax.rsqrt(spread + 1e-05)


def project(rows, weights):
    return jnp.dot(rows, weights, preferred_element_type=jnp.float32)


def attend(query, normed, w_key, w_value, pair, store):
    features = normed.shape[1]
    pair[:, :features] = project(normed, w_key[...]).astype(jnp.bfloat16)
    pair[:, features:] = project(normed, w_value[...]).astype(jnp.bfloat16)
    heads(query, pair, features, store)


def heads(query, pair, features, store):
    size = features // HEADS
    lower = lax.broadcasted_iota(jnp.int32, (1, 2 * size), 1) < size
    for h in range(HEADS // 2):
        cols = pl.ds(2 * h * size, 2 * size)
        rows = query(cols)
        key = pair[:, cols]
        value = pair[:, pl.ds(features + 2 * h * size, 2 * size)]
        halves = []
        for keep in (lower, jnp.logical_not(lower)):
            part = jnp.where(keep, rows, jnp.zeros_like(rows))
            scores = lax.dot_general(
                part, key, (((1,), (1,)), ((), ())), preferred_element_type=jnp.float32
            )
            top = jnp.max(scores, axis=-1, keepdims=True)
            weights = jnp.exp(scores - top)
            mass = jnp.sum(weights, axis=-1, keepdims=True)
            halves.append(project(weights.astype(jnp.bfloat16), value) / mass)
        store(cols, jnp.where(lower, halves[0], halves[1]))


RAW_BLOCK, RAW_PLACE, POSITION, BLOCK, PLACE, VIEW = range(6)


def build_tables(layer, side, degree, capacity, views, members, partners, key_view, ask, table):
    entries = views * degree
    low = layer < LAYERS // 2

    def mirror(value):
        return jnp.where(low, value, LAYERS - 1 - value)

    here = mirror(layer)

    def read(e, flags):
        partner = partners[lax.div(e, degree), lax.rem(e, degree)]
        peer = lax.rem(lax.div(partner, views), members)
        place = lax.rem(partner, views)
        there = mirror(lax.div(peer, ROW))
        inside = jnp.where(there == 0, 1, jnp.where(there == 2, 0, 2))
        turn = jnp.where(here == 0, there - 1, inside)
        across = (lax.rem(peer, ROW) != side).astype(jnp.int32)
        block = jnp.where(there == here, 0, 1 + 2 * turn + across)
        table[RAW_BLOCK, e] = block
        table[RAW_PLACE, e] = place
        return tuple(
            jnp.where((block == 2 + 2 * (i // views)) & (place == i % views), 1, flag)
            for i, flag in enumerate(flags)
        )

    flags = lax.fori_loop(0, entries, read, (jnp.int32(0),) * (3 * views))
    slots = []
    for j in range(3):
        wanted = flags[j * views : (j + 1) * views]
        slot = capacity - sum(wanted)
        for v in range(views):
            slots.append(slot)
            slot = slot + wanted[v]
        for k in range(capacity):
            ask[0, j * capacity + k] = sum(
                jnp.where((wanted[v] == 1) & (slots[j * views + v] == k), v, 0) for v in range(views)
            )

    def rank(e, carry):
        block, place = table[RAW_BLOCK, e], table[RAW_PLACE, e]
        position = jnp.int32(2)
        for other in range(entries):
            ahead = (table[RAW_BLOCK, other] * entries + other) < block * entries + e
            position = position + ahead.astype(jnp.int32)
        table[POSITION, e] = position
        spot = place
        for i, slot in enumerate(slots):
            spot = jnp.where((block == 2 + 2 * (i // views)) & (place == i % views), slot, spot)
        table[RAW_PLACE, e] = spot
        return carry

    lax.fori_loop(0, entries, rank, 0)

    def sort(r, carry):
        block, place, view = jnp.int32(-1), jnp.int32(0), key_view
        for e in range(entries):
            match = table[POSITION, e] == r
            block = jnp.where(match, table[RAW_BLOCK, e], block)
            place = jnp.where(match, table[RAW_PLACE, e], place)
            view = jnp.where(match, e // degree, view)
        table[BLOCK, r], table[PLACE, r], table[VIEW, r] = block, place, view
        return carry

    lax.fori_loop(0, entries + 2, sort, 0)


def sublayer_kernel(degree, capacity, *refs):
    partners, counts, key_slot, tokens, wq_in, wk_in, wv_in, wo_in, out_ref = refs[:9]
    w_query, w_key, w_value, w_out = refs[9:13]
    own, queries, near, b0, b1, b2, s0, s1, s2, keys, staged, key_out = refs[13:25]
    ask, asked, table, cur, pair, results, load_sem, send_sem, recv_sem = refs[25:]
    views, length, features = tokens.shape
    members, groups = lax.axis_size("member"), lax.axis_size("group")
    entries = views * degree
    peers = members - 1
    size = features // HEADS
    me, group = lax.axis_index("member"), lax.axis_index("group")
    layer, side = me // ROW, me % ROW
    low = layer < LAYERS // 2
    toward = jnp.where(low, ROW, -ROW)
    is_end = jnp.logical_or(layer == 0, layer == LAYERS - 1)
    is_mid = jnp.logical_not(is_end)
    beside = {"member": layer * ROW + 1 - side}
    inner = {"member": me + toward}
    outer = {"member": jnp.clip(me - toward, 0, members - 1)}
    above = {"group": lax.rem(group + 1, groups)}
    below = {"group": lax.rem(group + groups - 1, groups)}

    blocks = (near, b0, s0, b1, s1, b2, s2)
    base, total = {}, 0
    for name, ref in (("near", near), ("b0", b0), ("b1", b1), ("b2", b2), ("s0", s0),
                      ("s1", s1), ("s2", s2), ("keys", keys)):
        base[name] = total
        total += ref.shape[0]

    def remote(source, target, send, recv, device):
        return pltpu.make_async_remote_copy(
            src_ref=source, dst_ref=target, send_sem=send_sem.at[send],
            recv_sem=recv_sem.at[recv], device_id=device, device_id_type=MESH,
        )

    sends = {}

    def slot(name, index):
        return sends.setdefault((name, index), len(sends))

    def hop(name, source, v, target, target_name, device):
        return remote(source.at[v], target.at[v], slot(name, v), base[target_name] + v, device)

    def to_near(v):
        return hop("near", own, v, near, "near", beside)

    def own_to_b1(v):
        return hop("in", own, v, b1, "b1", inner)

    def own_to_b0(v):
        return hop("in", own, v, b0, "b0", inner)

    def own_out(v):
        return hop("out", own, v, b0, "b0", outer)

    def b1_in(v):
        return hop("in2", b1, v, b2, "b2", inner)

    def b0_out(v):
        return hop("out1", b0, v, b1, "b1", outer)

    def b2_out(v):
        return hop("out2", b2, v, b2, "b2", outer)

    swaps = (s0, s1, s2)

    def swap(j, k):
        return remote(
            staged.at[j * capacity + k], swaps[j].at[k], slot("swap", j * capacity + k),
            base[f"s{j}"] + k, beside,
        )

    def key_send(i):
        return remote(
            key_out, keys.at[i], slot("key", i), base["keys"] + i, above if i == 0 else below
        )

    def ask_send():
        return remote(ask, asked, slot("ask", 0), total, beside)

    loads = [
        pltpu.make_async_copy(source, target, load_sem.at[i])
        for i, (source, target) in enumerate(
            ((wq_in, w_query), (wk_in, w_key), (wv_in, w_value), (wo_in, w_out))
        )
    ]
    for load in loads:
        load.start()

    barrier = pltpu.get_barrier_semaphore()
    for device in (beside, inner, above, below):
        pl.semaphore_signal(barrier, inc=1, device_id=device, device_id_type=MESH)

    @pl.when(is_mid)
    def _():
        pl.semaphore_signal(barrier, inc=1, device_id=outer, device_id_type=MESH)

    own[0] = layer_norm(tokens[0]).astype(jnp.bfloat16)

    @pl.when(is_mid)
    def _():
        pl.semaphore_wait(barrier, 5)

    @pl.when(is_end)
    def _():
        pl.semaphore_wait(barrier, 4)

    for v in range(views):
        if v:
            own[v] = layer_norm(tokens[v]).astype(jnp.bfloat16)
        to_near(v).start()

        @pl.when(is_end)
        def _():
            own_to_b1(v).start()

        @pl.when(is_mid)
        def _():
            own_to_b0(v).start()
            own_out(v).start()

    key_view = key_slot[0]
    key_out[...] = own[key_view]
    loads[0].wait()
    for v in range(views):
        queries[v] = project(own[v], w_query[...]).astype(jnp.bfloat16) * jnp.bfloat16(size**-0.5)
    for i in range(2):
        key_send(i).start()
    build_tables(layer, side, degree, capacity, views, members, partners, key_view, ask, table)
    ask_send().start()
    loads[1].wait()
    loads[2].wait()
    for i in range(2):
        key_send(i).wait_recv()

    def stage(j, k, source):
        choice = asked[0, j * capacity + k]
        value = source[0]
        for v in range(1, k + views - capacity + 1):
            value = jnp.where(choice == v, source[v], value)
        staged[j * capacity + k] = value
        swap(j, k).start()

    def events(t):
        def far(v):
            @pl.when(is_end)
            def _():
                b0_out(v).wait_recv()

            @pl.when(is_mid)
            def _():
                b1_in(v).wait_recv()
                b2_out(v).start()

        def last(v):
            @pl.when(is_end)
            def _():
                b2_out(v).wait_recv()

        def arrive(j):
            for k in range(capacity):
                swap(j, k).wait_recv()

        extra = views - capacity

        def spread(wait, j, source, v):
            wait(v)
            if v >= extra:
                stage(j, v - extra, source)

        if t == first[0]:
            for v in range(views):
                own_to_b0(v).wait_recv()

                @pl.when(is_mid)
                def _():
                    b0_out(v).start()
                    own_to_b1(v).wait_recv()
                    b1_in(v).start()

                if v >= extra:
                    stage(0, v - extra, b0)
            for v in range(views):
                to_near(v).wait_recv()
        if t == first[2]:
            for v in range(views - 2):
                spread(far, 1, b1, v)
            arrive(0)
        if t == first[2] + 1:
            spread(far, 1, b1, views - 2)
        if t == first[3]:
            spread(far, 1, b1, views - 1)
        if t == first[4]:
            for v in range(views - 2):
                spread(last, 2, b2, v)
            arrive(1)
        if t == first[4] + 1:
            spread(last, 2, b2, views - 2)
        if t == first[5]:
            spread(last, 2, b2, views - 1)
        if t == first[6]:
            arrive(2)

    first = [2 + max(0, entries - capacity * (peers - j)) for j in range(peers)]

    def entry(t, carry):
        for when in sorted({first[0], first[2], first[2] + 1, first[3], first[4], first[4] + 1,
                            first[5], first[6]}):
            @pl.when(t == when)
            def _():
                events(when)

        @pl.when(t < 2)
        def _():
            cur[...] = keys[jnp.minimum(t, 1)]

        block, place, view = table[BLOCK, t], table[PLACE, t], table[VIEW, t]
        for j, ref in enumerate(blocks):
            @pl.when(t >= first[j])
            def _():
                value = ref[jnp.minimum(place, ref.shape[0] - 1)]
                cur[...] = jnp.where(block == j, value, cur[...])

        def store(cols, value):
            results[t, :, cols] = value

        attend(lambda cols: queries[view, :, cols], cur[...], w_key, w_value, pair, store)
        return carry

    ask_send().wait_recv()
    lax.fori_loop(0, entries + 2, entry, 0)
    loads[3].wait()
    for v in range(views):
        is_key = (key_view == v).astype(jnp.int32)
        count = counts[v]
        mixed = is_key.astype(jnp.float32) * (results[0] + results[1])
        for e in range(degree):
            live = (count > e).astype(jnp.int32).astype(jnp.float32)
            mixed += live * results[table[POSITION, v * degree + e]]
        divisor = jnp.full((1, features), count + 2 * is_key, jnp.int32).astype(jnp.float32)
        mixed = mixed * (1.0 / divisor)
        out_ref[v] = (
            tokens[v].astype(jnp.float32) + project(mixed.astype(jnp.bfloat16), w_out[...])
        ).astype(out_ref.dtype)

    for v in range(views):
        to_near(v).wait_send()

        @pl.when(is_end)
        def _():
            own_to_b1(v).wait_send()

        @pl.when(is_mid)
        def _():
            own_to_b0(v).wait_send()
            own_out(v).wait_send()
            b1_in(v).wait_send()
            b0_out(v).wait_send()
            b2_out(v).wait_send()

    for j in range(3):
        for k in range(capacity):
            swap(j, k).wait_send()
    for i in range(2):
        key_send(i).wait_send()
    ask_send().wait_send()


def one_kernel(tokens, w_query, w_key, w_value, w_out, partners, counts, key_slot):
    views, length, features = tokens.shape
    members = lax.axis_size("member")
    degree = partners.shape[1]
    entries = views * degree
    capacity = (entries + members - 2) // (members - 1)
    smem = pl.BlockSpec(memory_space=pltpu.SMEM)
    hbm = pl.BlockSpec(memory_space=pltpu.HBM)
    vmem = pl.BlockSpec(memory_space=pltpu.VMEM)
    stay = [
        pltpu.with_memory_space_constraint(w, pltpu.HBM) for w in (w_query, w_key, w_value, w_out)
    ]
    slab = (length, features)
    weights_shape = pltpu.VMEM((features, features), jnp.bfloat16)
    half = jnp.bfloat16
    blocks = [pltpu.VMEM((views, *slab), half)] * 6 + [pltpu.VMEM((capacity, *slab), half)] * 3
    sends = 6 * views + 3 * capacity + 3 + views
    receives = 4 * views + 3 * capacity + 3
    return pl.pallas_call(
        functools.partial(sublayer_kernel, degree, capacity),
        out_shape=jax.ShapeDtypeStruct(tokens.shape, tokens.dtype),
        in_specs=[smem] * 3 + [vmem] + [hbm] * 4,
        out_specs=vmem,
        scratch_shapes=[
            weights_shape,
            weights_shape,
            weights_shape,
            weights_shape,
            *blocks,
            pltpu.VMEM((2, *slab), half),
            pltpu.VMEM((3 * capacity, *slab), half),
            pltpu.VMEM(slab, half),
            pltpu.SMEM((1, 3 * capacity), jnp.int32),
            pltpu.SMEM((1, 3 * capacity), jnp.int32),
            pltpu.SMEM((6, entries + 2), jnp.int32),
            pltpu.VMEM(slab, half),
            pltpu.VMEM((length, 2 * features), half),
            pltpu.VMEM((entries + 2, *slab), jnp.float32),
            pltpu.SemaphoreType.DMA((4,)),
            pltpu.SemaphoreType.DMA((sends,)),
            pltpu.SemaphoreType.DMA((receives,)),
        ],
        compiler_params=pltpu.CompilerParams(
            collective_id=0, has_side_effects=True, vmem_limit_bytes=44 * 1024 * 1024
        ),
        name="sublayer",
    )(partners, counts, key_slot, tokens, *stay)


NEAR, FAR, WIDE, EARLY = 3, 9, 7, 3
FREE, SLOTS, PLAIN, CROSS = 4, 5, 4, 16
KEYS = CROSS + WIDE


def quick_kernel(degree, *refs):
    partners, counts, key_slot, tokens, wq_in, wk_in, wv_in, wo_in, out_ref, flag_ref = refs[:10]
    w_query, w_key, w_value, w_out = refs[10:14]
    own, queries, arrived, near_out, far_out, wide_out, key_out = refs[14:21]
    ask, asked, union, codes, sources, picks, table, pairs, results = refs[21:30]
    load_sem, send_sem, recv_sem = refs[30:33]
    notes = refs[33:]
    views, length, features = tokens.shape
    members, groups = lax.axis_size("member"), lax.axis_size("group")
    entries = views * degree
    size = features // HEADS
    me, group = lax.axis_index("member"), lax.axis_index("group")
    layer, side = me // ROW, me % ROW
    low = layer < LAYERS // 2
    toward = jnp.where(low, ROW, -ROW)
    is_end = jnp.logical_or(layer == 0, layer == LAYERS - 1)
    is_mid = jnp.logical_not(is_end)
    beside = {"member": layer * ROW + 1 - side}
    inner = {"member": me + toward}
    outer = {"member": jnp.clip(me - toward, 0, members - 1)}
    above = {"group": lax.rem(group + 1, groups)}
    below = {"group": lax.rem(group + groups - 1, groups)}
    key_view = key_slot[0]
    cells = 7 * views
    cut = length // 32 * 16
    halves = (pl.ds(0, cut), pl.ds(cut, length - cut))
    near, b0, b1, b2 = (arrived.at[pl.ds(i * views, views)] for i in range(4))
    first_view, far = arrived.at[pl.ds(FREE, 1)], arrived.at[pl.ds(SLOTS, FAR)]
    wide, keys = arrived.at[pl.ds(CROSS, WIDE)], arrived.at[pl.ds(KEYS, 2)]
    names = {}

    def number(kind, name):
        return names.setdefault((kind, name), sum(1 for k, _ in names if k == kind))

    def remote(name, source, target, landing, device):
        return pltpu.make_async_remote_copy(
            src_ref=source, dst_ref=target, send_sem=send_sem.at[number(0, name)],
            recv_sem=recv_sem.at[number(1, landing)], device_id=device, device_id_type=MESH,
        )

    def near_send(k):
        return remote(("near", k), near_out.at[k], near.at[k], ("near", k), beside)

    def own_to_b1(v):
        return remote(("in", v), own.at[v], b1.at[v], ("b1", v), inner)

    def own_to_b0(v):
        return remote(("in", v), own.at[v], b0.at[v], ("b0", v), inner)

    def b1_in(v):
        return remote(("in2", v), b1.at[v], b2.at[v], ("b2", v), inner)

    def own_out():
        return remote("free", own.at[0], first_view.at[0], "free", outer)

    def far_send(q, p):
        rows = halves[p]
        return remote(("far", q, p), far_out.at[q, rows], far.at[q, rows], ("far", q, p), outer)

    def wide_send(k, p):
        rows = halves[p]
        return remote(("wide", k, p), wide_out.at[k, rows], wide.at[k, rows], ("wide", k, p), beside)

    def key_send(i):
        return remote(("key", i), key_out, keys.at[i], ("key", i), below if i else above)

    def ask_send():
        return remote("ask", ask, asked, "ask", beside)

    def union_send():
        return remote("union", union, union, "union", inner)

    def note(i, device):
        return remote(("note", i), notes[2 * i], notes[2 * i + 1], ("note", i), device)

    loads = [
        pltpu.make_async_copy(source, target, load_sem.at[i])
        for i, (source, target) in enumerate(
            ((wq_in, w_query), (wk_in, w_key), (wv_in, w_value), (wo_in, w_out))
        )
    ]
    for load in loads:
        load.start()
    barrier = pltpu.get_barrier_semaphore()
    for device in (beside, inner, above, below):
        pl.semaphore_signal(barrier, inc=1, device_id=device, device_id_type=MESH)

    @pl.when(is_mid)
    def _():
        pl.semaphore_signal(barrier, inc=1, device_id=outer, device_id_type=MESH)

    def mirror(value):
        return jnp.where(low, value, LAYERS - 1 - value)

    here = mirror(layer)

    def read(e, carry):
        partner = partners[lax.div(e, degree), lax.rem(e, degree)]
        peer = lax.rem(lax.div(partner, views), members)
        there = mirror(lax.div(peer, ROW))
        inside = jnp.where(there == 0, 1, jnp.where(there == 2, 0, 2))
        turn = jnp.where(here == 0, there - 1, inside)
        across = (lax.rem(peer, ROW) != side).astype(jnp.int32)
        block = jnp.where(there == here, 0, 1 + 2 * turn + across)
        live = lax.rem(e, degree) < counts[lax.div(e, degree)]
        codes[0, e] = jnp.where(live, block * views + lax.rem(partner, views), -1)
        return carry

    lax.fori_loop(0, entries, read, 0)

    def mark(cell, carry):
        found = jnp.int32(0)
        for e in range(entries):
            found = jnp.where(codes[0, e] == cell, 1, found)
        ask[0, cell] = found
        return carry

    lax.fori_loop(0, cells, mark, 0)
    own[0] = layer_norm(tokens[0]).astype(jnp.bfloat16)

    @pl.when(is_mid)
    def _():
        pl.semaphore_wait(barrier, 5)

    @pl.when(is_end)
    def _():
        pl.semaphore_wait(barrier, 4)

    ask_send().start()
    for v in range(views):
        if v:
            own[v] = layer_norm(tokens[v]).astype(jnp.bfloat16)

        @pl.when(is_mid)
        def _():
            own_to_b0(v).start()
            if v == 0:
                own_out().start()

    key_out[...] = own[key_view]
    count = 3 * views

    def same(ref, c):
        return ref[0, (1 + 2 * (c // views)) * views + c % views]

    def cross(ref, c):
        return ref[0, (2 + 2 * (c // views)) * views + c % views]

    ask_send().wait_recv()

    @pl.when(is_end)
    def _():
        for c in range(count):
            union[0, c] = jnp.maximum(same(ask, c), cross(asked, c))
        union_send().start()
        for v in range(views):
            own_to_b1(v).start()

    near_flags = [asked[0, v] for v in range(views)]
    near_spots = [sum(near_flags[:v]) for v in range(views)]
    for k in range(NEAR):
        pick = jnp.int32(0)
        for v in range(views):
            pick = jnp.where((near_flags[v] == 1) & (near_spots[v] == k), v, pick)
        near_out[k] = own[pick]
        near_send(k).start()
    loads[0].wait()
    for v in range(views):
        queries[v] = project(own[v], w_query[...]).astype(jnp.bfloat16) * jnp.bfloat16(size**-0.5)
    for i in range(2):
        key_send(i).start()

    @pl.when(is_mid)
    def _():
        union_send().wait_recv()

    def line_up(flags, ready):
        spots, last = [], jnp.int32(-1)
        for flag, at in zip(flags, ready):
            spot = jnp.maximum(last + 1, at)
            spots.append(spot)
            last = jnp.where(flag == 1, spot, last)
        return spots, last

    far_ready = [0] * views + [v + 1 for v in range(views)] + [v + 1 + views for v in range(views)]

    mid_ready = [max(0, v - 2) for v in range(views)] + [max(0, v - 1) for v in range(views)]
    mid_ready += [v + EARLY for v in range(views)]

    def far_slots(flags):
        spots, last = line_up(flags[1:], far_ready[1:])
        return [jnp.int32(-1)] + spots, last

    def wide_slots(flags, behind):
        ready = []
        for c in range(count):
            ready.append(jnp.where(is_end, jnp.maximum(behind[c] - 2, 0), mid_ready[c]))
        return line_up(flags, ready)

    def found(c, spots):
        return jnp.where(is_end, FREE if c == 0 else SLOTS + spots[c], PLAIN + c)

    mine = [union[0, c] for c in range(count)]
    my_far, far_last = far_slots(mine)
    beside_far, _ = far_slots([jnp.maximum(same(asked, c), cross(ask, c)) for c in range(count)])
    out_flags = [cross(asked, c) for c in range(count)]
    my_wide, out_last = wide_slots(out_flags, my_far)
    beside_wide, in_last = wide_slots([cross(ask, c) for c in range(count)], beside_far)
    for q in range(FAR):
        pick = jnp.int32(0)
        for c in range(1, count):
            pick = jnp.where((mine[c] == 1) & (my_far[c] == q), c, pick)
        picks[0, q] = pick
    for k in range(WIDE):
        pick = jnp.where(is_end, FREE, PLAIN)
        for c in range(count):
            pick = jnp.where((out_flags[c] == 1) & (my_wide[c] == k), found(c, my_far), pick)
        picks[0, FAR + k] = pick
    for v in range(views):
        sources[0, v] = sum(ask[0, other] for other in range(v)) if v else 0
    for c in range(count):
        sources[0, (1 + 2 * (c // views)) * views + c % views] = found(c, my_far)
        sources[0, (2 + 2 * (c // views)) * views + c % views] = CROSS + beside_wide[c]
    full = (far_last >= FAR) | (out_last >= WIDE) | (in_last >= WIDE)
    notes[0][0, 0] = full.astype(jnp.int32)

    def view_of(ref, index):
        return ref[index]

    def choose(choice, options):
        value = None
        for key, load in options:
            value = load() if value is None else jnp.where(choice == key, load(), value)
        return value

    def far_stage(q):
        options = [(c, functools.partial(view_of, own, c)) for c in range(min(views, q + views))]
        options += [(views + v, functools.partial(view_of, b0, v)) for v in range(views) if v < q]
        options += [
            (2 * views + v, functools.partial(view_of, b2, v)) for v in range(views) if v + views < q
        ]
        far_out[q] = choose(picks[0, q], options)
        for p in range(2):
            far_send(q, p).start()

    def far_turn(q):
        @pl.when(is_mid)
        def _():
            if 1 <= q <= views:
                own_to_b0(q - 1).wait_recv()
            if q > views:
                b1_in(q - 1 - views).wait_recv()
            far_stage(q)
            if 2 <= q <= views + 1:
                own_to_b1(q - 2).wait_recv()
                b1_in(q - 2).start()

    def wide_end(k, p):
        @pl.when(is_end)
        def _():
            far_send(k + 2, p).wait_recv()
            options = [(FREE, lambda: first_view[0, halves[p]])]
            options += [
                (SLOTS + q, functools.partial(view_of, far, (q, halves[p]))) for q in range(k + 3)
            ]
            wide_out[k, halves[p]] = choose(picks[0, FAR + k], options)
            wide_send(k, p).start()

    def wide_mid(k):
        @pl.when(is_mid)
        def _():
            held = b0, b1, b2
            options = [
                (PLAIN + c, functools.partial(view_of, held[c // views], c % views))
                for c in range(count)
                if mid_ready[c] <= k
            ]
            wide_out[k] = choose(picks[0, FAR + k], options)
            for p in range(2):
                wide_send(k, p).start()

    def far_arrive(q):
        @pl.when(is_end)
        def _():
            for p in range(2):
                far_send(q, p).wait_recv()

    def note_value(i, value):
        notes[2 * i][0, 0] = value

    def seen(i):
        return notes[2 * i + 1][0, 0]

    rounds = groups // 2

    def note_step(i):
        if i == 0:
            note(0, beside).start()
        if i == 1:
            note(0, beside).wait_recv()
            note_value(1, jnp.maximum(notes[0][0, 0], seen(0)))

            @pl.when(is_end)
            def _():
                note(1, inner).start()
        if i == 2:
            @pl.when(is_mid)
            def _():
                note(1, inner).wait_recv()
                note_value(2, jnp.maximum(notes[2][0, 0], seen(1)))
                note(2, inner).start()
        if i == 3:
            @pl.when(is_mid)
            def _():
                note(2, inner).wait_recv()
                note_value(3, jnp.maximum(notes[4][0, 0], seen(2)))
                note(3, outer).start()
                note_value(4, notes[6][0, 0])
        if i == 4:
            @pl.when(is_end)
            def _():
                note(3, outer).wait_recv()
                note_value(4, seen(3))

            note_value(5, notes[8][0, 0])
            note(4, above).start()
            note(5, below).start()
        if i > 4:
            j = 2 * i - 6
            note(j, above).wait_recv()
            note(j + 1, below).wait_recv()
            value = jnp.maximum(notes[2 * j][0, 0], jnp.maximum(seen(j), seen(j + 1)))
            if i < 4 + rounds:
                note_value(j + 2, value)
                note_value(j + 3, value)
                note(j + 2, above).start()
                note(j + 3, below).start()
            else:
                flag_ref[0, 0] = value

    far_turn(0)
    note_step(0)

    def rank(e, carry):
        code = codes[0, e] * entries + e
        position = jnp.int32(2)
        for other in range(entries):
            position = position + (codes[0, other] * entries + other < code).astype(jnp.int32)
        table[0, e] = position
        return carry

    lax.fori_loop(0, entries, rank, 0)

    def sort(r, carry):
        cell, view = jnp.int32(0), key_view
        for e in range(entries):
            match = table[0, e] == r
            cell = jnp.where(match, codes[0, e], cell)
            view = jnp.where(match, e // degree, view)
        source = jnp.where(cell < 0, KEYS, sources[0, jnp.maximum(cell, 0)])
        source = jnp.clip(source, 0, KEYS + 1)
        table[1, r], table[2, r] = jnp.where(r < 2, KEYS + r, source), view
        return carry

    lax.fori_loop(0, entries + 2, sort, 0)
    loads[1].wait()
    loads[2].wait()
    def learn(places, count):
        def one(i, carry):
            place = places[0]
            for turn in range(1, len(places)):
                place = jnp.where(i == turn, places[turn], place)
            rows = arrived[place]
            pairs[place, :, :features] = project(rows, w_key[...]).astype(jnp.bfloat16)
            pairs[place, :, features:] = project(rows, w_value[...]).astype(jnp.bfloat16)
            return carry

        lax.fori_loop(0, count, one, 0)

    def attends(first, last):
        def one(t, carry):
            source, view = table[1, t], table[2, t]

            def store(cols, value):
                results[t, :, cols] = value

            heads(lambda cols: queries[view, :, cols], pairs.at[source], features, store)
            return carry

        if last > first:
            lax.fori_loop(first + 2, last + 2, one, 0)

    def wide_arrive(k):
        for p in range(2):
            wide_send(k, p).wait_recv()
        learn([CROSS + k], 1)

    for v in range(views):
        far_turn(v + 1)
        if v == views - 1:
            wide_end(0, 0)
            wide_end(0, 1)
        elif v:
            far_arrive(v - 1)
        else:
            @pl.when(is_end)
            def _():
                own_out().wait_recv()

        if v >= views - 2:
            wide_mid(v - views + 2)
        places = [FREE + v]
        if v < NEAR:
            near_send(v).wait_recv()
            places = [v, FREE + v]
        more = [PLAIN + views + v - 1] if v else []
        learn(places + more, jnp.where(is_end, len(places), len(places + more)))
        if v == 0:
            for i in range(2):
                key_send(i).wait_recv()
            learn([KEYS, KEYS + 1], 2)
        if v == 1:
            attends(-2, 0)
            results[0] = results[0] + results[1]
    bounds = [max(0, entries - n) for n in (15, 12, 9, 7, 6, 3, 0)]
    attends(0, bounds[0])
    inside = {3: (bounds[0], bounds[0] + 1), 5: (bounds[2] - 1, bounds[2]), 6: (bounds[3], bounds[4])}
    after = {3: (bounds[0] + 1, bounds[1]), 4: (bounds[1], bounds[2] - 1), 5: (bounds[2], bounds[3]),
             6: (bounds[4], bounds[5])}
    for k in range(1, WIDE):
        wide_end(k, 0)
        if k >= EARLY:
            wide_mid(k)
        if views + k < FAR:
            far_turn(views + k)
        if k == 1:
            wide_mid(2)
        wide_arrive(k - 1)
        attends(*inside.get(k, (0, 0)))
        wide_end(k, 1)
        if 1 < k < 5:
            note_step(k - 1)
        landed = jnp.where(is_end, FREE + views - 1 + k, PLAIN + 2 * views + k - 1)
        there = 1 if k <= views else 0
        if k == 1:
            learn([landed, PLAIN + 2 * views - 1], jnp.where(is_end, 1, 2))
        else:
            learn([landed], jnp.where(is_end, 1, there))
        if k == WIDE - 1:
            first, last = after[k]
            attends(first, last - 1)
            note_step(4)
            attends(last - 1, last)
        else:
            attends(*after.get(k, (0, 0)))
    wide_arrive(WIDE - 1)
    for i in range(1, rounds):
        note_step(4 + i)
    attends(bounds[5], bounds[6])
    note_step(4 + rounds)
    loads[3].wait()
    for v in range(views):
        is_key = (key_view == v).astype(jnp.int32)
        total = counts[v]
        mixed = is_key.astype(jnp.float32) * results[0]
        for e in range(degree):
            live = (total > e).astype(jnp.int32).astype(jnp.float32)
            mixed += live * results[table[0, v * degree + e]]
        divisor = jnp.full((1, features), total + 2 * is_key, jnp.int32).astype(jnp.float32)
        mixed = mixed * (1.0 / divisor)
        out_ref[v] = (
            tokens[v].astype(jnp.float32) + project(mixed.astype(jnp.bfloat16), w_out[...])
        ).astype(out_ref.dtype)

    for v in range(views):
        @pl.when(is_end)
        def _():
            own_to_b1(v).wait_send()

        @pl.when(is_mid)
        def _():
            own_to_b0(v).wait_send()
            b1_in(v).wait_send()

    @pl.when(is_mid)
    def _():
        own_out().wait_send()
        for q in range(FAR):
            for p in range(2):
                far_send(q, p).wait_send()
        note(2, inner).wait_send()
        note(3, outer).wait_send()

    @pl.when(is_end)
    def _():
        union_send().wait_send()
        note(1, inner).wait_send()

    for k in range(WIDE):
        for p in range(2):
            wide_send(k, p).wait_send()
    for k in range(NEAR):
        near_send(k).wait_send()
    for i in range(2):
        key_send(i).wait_send()
    ask_send().wait_send()
    note(0, beside).wait_send()
    for i in range(4, 4 + 2 * rounds):
        note(i, above if i % 2 == 0 else below).wait_send()


def quick(tokens, w_query, w_key, w_value, w_out, partners, counts, key_slot):
    views, length, features = tokens.shape
    degree = partners.shape[1]
    entries = views * degree
    rounds = lax.axis_size("group") // 2
    smem = pl.BlockSpec(memory_space=pltpu.SMEM)
    hbm = pl.BlockSpec(memory_space=pltpu.HBM)
    vmem = pl.BlockSpec(memory_space=pltpu.VMEM)
    stay = [
        pltpu.with_memory_space_constraint(w, pltpu.HBM) for w in (w_query, w_key, w_value, w_out)
    ]
    slab = (length, features)
    half = jnp.bfloat16

    def slabs(count):
        return pltpu.VMEM((count, *slab), half)

    def numbers(*shape):
        return pltpu.SMEM(shape, jnp.int32)

    return pl.pallas_call(
        functools.partial(quick_kernel, degree),
        out_shape=(
            jax.ShapeDtypeStruct(tokens.shape, tokens.dtype),
            jax.ShapeDtypeStruct((1, 1), jnp.int32),
        ),
        in_specs=[smem] * 3 + [vmem] + [hbm] * 4,
        out_specs=(vmem, smem),
        scratch_shapes=[
            *[pltpu.VMEM((features, features), half)] * 4,
            *[slabs(views)] * 2,
            slabs(KEYS + 2),
            slabs(NEAR),
            slabs(FAR),
            slabs(WIDE),
            pltpu.VMEM(slab, half),
            numbers(1, 7 * views),
            numbers(1, 7 * views),
            numbers(1, 3 * views),
            numbers(1, entries),
            numbers(1, 7 * views),
            numbers(1, FAR + WIDE),
            numbers(3, entries + 2),
            pltpu.VMEM((KEYS + 2, length, 2 * features), half),
            pltpu.VMEM((entries + 2, *slab), jnp.float32),
            pltpu.SemaphoreType.DMA((4,)),
            pltpu.SemaphoreType.DMA((5 * views + 2 * FAR + 2 * WIDE + 16,)),
            pltpu.SemaphoreType.DMA((5 * views + 2 * FAR + 2 * WIDE + 16,)),
            *[numbers(1, 1)] * (2 * (4 + 2 * rounds)),
        ],
        compiler_params=pltpu.CompilerParams(
            collective_id=1, has_side_effects=True, vmem_limit_bytes=50 * 1024 * 1024
        ),
        name="sublayer_quick",
    )(partners, counts, key_slot, tokens, *stay)


def select_kernel(*arguments):
    result, flag = quick(*arguments)
    return lax.cond(flag[0, 0] > 0, lambda: one_kernel(*arguments), lambda: result)


def local_kernel(table, queries, w_key, w_value, block, inverse, tokens, w_out, out_ref, *scratch):
    held, pair, total, sem = scratch
    copy = pltpu.make_async_copy(block, held, sem)
    copy.start()
    total[...] = jnp.zeros_like(total)
    copy.wait()
    views, length, _ = total.shape

    def entry(e, carry):
        @pl.when(table[0, e] == 1)
        def _():
            place, view = table[1, e], table[2, e]

            def store(cols, value):
                total[view, :, cols] += value

            normed = layer_norm(held[place]).astype(jnp.bfloat16)
            attend(lambda cols: queries[view, :, cols], normed, w_key, w_value, pair, store)

        return carry

    lax.fori_loop(0, table.shape[1], entry, 0)
    for v in range(views):
        mixed = (total[v] * inverse[v]).astype(jnp.bfloat16)
        out_ref[v] = (tokens[v].astype(jnp.float32) + project(mixed, w_out[...])).astype(out_ref.dtype)


def exchange(tokens, w_query, w_key, w_value, w_out, partners, counts, key_slot):
    slot_key = key_slot[0]
    views, length, features = tokens.shape
    members, groups = lax.axis_size("member"), lax.axis_size("group")
    degree = partners.shape[1]
    entry_list = partners.reshape(-1)
    entries = entry_list.shape[0]
    capacity = (entries + members - 2) // (members - 1)
    peers = entry_list // views % members
    places = entry_list % views
    order = jnp.arange(entries, dtype=jnp.int32)
    earlier = (peers[:, None] == peers[None, :]) & (order[None, :] < order[:, None])
    cells = peers * capacity + jnp.sum(earlier.astype(jnp.int32), axis=1)
    requests = jnp.zeros((members * capacity,), jnp.int32).at[cells].set(places)
    asked = lax.all_to_all(
        requests.reshape(members, capacity), "member", split_axis=0, concat_axis=0, tiled=True
    )
    outgoing = tokens[asked.reshape(-1)].reshape(members, capacity, length, features)
    arrived = lax.all_to_all(outgoing, "member", split_axis=0, concat_axis=0, tiled=True)
    own_key = lax.dynamic_slice_in_dim(tokens, slot_key, 1, 0)
    below = lax.ppermute(own_key, "group", [(g, (g + 1) % groups) for g in range(groups)])
    above = lax.ppermute(own_key, "group", [((g + 1) % groups, g) for g in range(groups)])
    block = jnp.concatenate((arrived.reshape(members * capacity, length, features), below, above))
    normed = layer_norm(tokens).astype(jnp.bfloat16)
    queries = project(normed.reshape(views * length, features), w_query).astype(jnp.bfloat16)
    queries = queries.reshape(tokens.shape) * jnp.bfloat16((features // HEADS) ** -0.5)
    is_key = (jnp.arange(views, dtype=jnp.int32) == slot_key).astype(jnp.int32)
    inverse = 1.0 / (counts + 2 * is_key).astype(jnp.float32)
    live = (jnp.arange(degree, dtype=jnp.int32)[None, :] < counts[:, None]).reshape(-1)
    two = jnp.arange(2, dtype=jnp.int32)
    table = jnp.stack(
        (
            jnp.concatenate((live.astype(jnp.int32), jnp.ones_like(two))),
            jnp.concatenate((cells, members * capacity + two)),
            jnp.concatenate((order // degree, jnp.full_like(two, slot_key))),
        )
    )
    vmem = pl.BlockSpec(memory_space=pltpu.VMEM)
    smem = pl.BlockSpec(memory_space=pltpu.SMEM)
    hbm = pl.BlockSpec(memory_space=pl.ANY)
    return pl.pallas_call(
        local_kernel,
        out_shape=jax.ShapeDtypeStruct(tokens.shape, tokens.dtype),
        in_specs=[smem, vmem, vmem, vmem, hbm, smem, vmem, vmem],
        out_specs=vmem,
        scratch_shapes=[
            pltpu.VMEM(block.shape, block.dtype),
            pltpu.VMEM((length, 2 * features), jnp.bfloat16),
            pltpu.VMEM(tokens.shape, jnp.float32),
            pltpu.SemaphoreType.DMA,
        ],
        compiler_params=pltpu.CompilerParams(vmem_limit_bytes=60 * 1024 * 1024),
        name="attend_all",
    )(table, queries, w_key, w_value, block, inverse, tokens, w_out)


def sublayer(tokens, w_query, w_key, w_value, w_out, partners, counts, key_slot):
    views = tokens.shape[0]
    members = lax.axis_size("member")
    entries = partners.shape[0] * partners.shape[1]
    capacity = (entries + members - 2) // (members - 1)
    grid = members == LAYERS * ROW and views == capacity + 1
    run = select_kernel if grid else exchange
    return run(tokens, w_query, w_key, w_value, w_out, partners, counts, key_slot)


def solution(mesh):
    return jax.shard_map(
        sublayer,
        mesh=mesh,
        in_specs=(
            P(("group", "member"), None, None),
            P(),
            P(),
            P(),
            P(),
            P(("group", "member"), None),
            P(("group", "member")),
            P(("group", "member")),
        ),
        out_specs=P(("group", "member"), None, None),
        check_vma=False,
    )
```
